32 devices in a mesh: rep: 2 (over x), shard: 16 (over z, y, core).
Axes of the slice: x: 2, y: 2, z: 4, core: 2. Of those that a mesh axis runs over, the one named last changes fastest.
Arguments:
- inputs: bfloat16 [32, 1024, 768], P(('rep', 'shard')), may hold values from -6 to 6
- doc_ids: int32 [32, 1024], P(('rep', 'shard')), may hold values from 0 to 3, never falling along the last dimension, each value on 1 to 512 neighbouring positions
- attn_gain: bfloat16 [768], P('shard'), may hold values from 0.25 to 1.75
- w_query: bfloat16 [768, 768], P('shard'), may hold values from -0.21875 to 0.21875
- w_key: bfloat16 [768, 768], P('shard'), may hold values from -0.21875 to 0.21875
- w_value: bfloat16 [768, 768], P('shard'), may hold values from -0.21875 to 0.21875
- w_out: bfloat16 [768, 768], P('shard'), may hold values from -1.75 to 1.75
- ffn_gain: bfloat16 [768], P('shard'), may hold values from 0.25 to 1.75
- w_gate: bfloat16 [768, 2048], P('shard'), may hold values from -0.21875 to 0.21875
- w_up: bfloat16 [768, 2048], P('shard'), may hold values from -0.21875 to 0.21875
- w_down: bfloat16 [2048, 768], P('shard'), may hold values from -0.125 to 0.125
- cotangent: bfloat16 [32, 1024, 768], P(('rep', 'shard')), may hold values from -6 to 6
Outputs:
- output: bfloat16 [32, 1024, 768], P(('rep', 'shard'))
- grad_input: float32 [32, 1024, 768], P(('rep', 'shard'))
- grad_attn_gain: float32 [768], P('shard')
- grad_w_query: float32 [768, 768], P('shard')
- grad_w_key: float32 [768, 768], P('shard')
- grad_w_value: float32 [768, 768], P('shard')
- grad_w_out: float32 [768, 768], P('shard')
- grad_ffn_gain: float32 [768], P('shard')
- grad_w_gate: float32 [768, 2048], P('shard')
- grad_w_up: float32 [768, 2048], P('shard')
- grad_w_down: float32 [2048, 768], P('shard')
The draws below stay inside these ranges and needn't reach their ends.
Inputs may be any that keep to these rules, and one draw needn't show every extreme that they name: `doc_ids`: within a sequence document numbers never fall; every document has 1 to 512 tokens, and one has exactly 512.
All inputs are finite; a program needn't handle non-finite values.
Results may differ from the reference program's by a relative error of at most 0.017.
Values may be sent and summed in bfloat16 or wider, within the bound.
No kernel may reach another device: no remote copies, remote signals or barrier semaphores. Data moves between devices by JAX's collectives and lax.ppermute only.
A program may use at most 320 MiB of HBM per device.

```python
import math
import jax
import jax.numpy as jnp
import numpy as np
from jax import lax

D = 768
H = 12
HD = 64
FF = 2048
SEQ = 1024
BLOCK = 256
DOCS = 4
SEQS = 32


def with_spikes(values, stream_key, source, target, shards_of, factor):
    def block_of(dim):
        return (jnp.arange(values.shape[dim]) // (values.shape[dim] // shards_of)).reshape((-1,) + (1,) * (values.ndim - 1 - dim))

    near = jax.random.permutation(stream_key, shards_of)[block_of(target)]
    second = (block_of(target) + shards_of // 2) % shards_of
    return jnp.where((block_of(source) == near) | (block_of(source) == second), factor * values, values)


def block_levels(key, extent, split, smallest, top_value):
    level = 1.0
    for dim, blocks in split:
        heights = jax.random.uniform(jax.random.fold_in(jax.random.fold_in(key, 6), dim), (blocks,), jnp.float32, smallest / len(split), top_value / len(split))
        level = level * jnp.repeat(jnp.exp(heights), extent[dim] // blocks).reshape((-1,) + (1,) * (len(extent) - 1 - dim))
    return level


def profile(amount, total, most, lean):
    weights = [(1 << 20) // math.isqrt(rank ** lean) + 1 for rank in range(2, amount + 1)]
    rest, counts = total - most - (amount - 1), [1] * (amount - 1)
    while rest > 0:
        candidates = [i for i in range(amount - 1) if counts[i] < most]
        mass, left = sum([weights[i] for i in candidates]), rest
        for i in candidates:
            more = min(most - counts[i], max(1, left * weights[i] // mass), rest)
            counts[i] = counts[i] + more
            rest = rest - more
    return np.array([most] + counts)


def uneven_parts(key, count, total, reach, skew):
    if count == 2:
        one = jax.random.randint(key, (), max(1, total - reach), min(reach, total - 1) + 1)
        return jnp.stack([one, total - one])
    lengths = jnp.asarray(profile(count, total, reach, skew), jnp.int32)
    pairs = (count - 1) // 2
    source_of, sink = lengths[1:1 + 2 * pairs:2], lengths[2:2 + 2 * pairs:2]
    margin = jnp.minimum(source_of - 1, reach - sink)
    shifted = jax.random.randint(jax.random.fold_in(key, 1), (pairs,), 0, 1 << 20) % (margin + 1)
    lengths = lengths.at[1:1 + 2 * pairs:2].set(source_of - shifted).at[2:2 + 2 * pairs:2].set(sink + shifted)
    return lengths[jax.random.permutation(jax.random.fold_in(key, 2), count)]


def centred(rng, shape, width, most, shards=(), held_as=jnp.bfloat16):
    loudness = block_levels(rng, shape, shards, -0.22, 0.18) if shards else 1.0
    array = jax.random.normal(rng, shape, jnp.float32) * width * loudness
    return jnp.minimum(jnp.maximum(array, -most), most).astype(held_as)


def gaussian_with(rng, dims, deviation, bound, cuts, heavy, held_as=jnp.bfloat16):
    values = deviation * jax.random.normal(rng, dims, jnp.float32)
    if cuts:
        values = values * block_levels(rng, dims, cuts, -0.22, 0.18)
    return jnp.clip(with_spikes(values, jax.random.fold_in(rng, 3), *heavy), -bound, bound).astype(held_as)


def setup_inputs(seed: int = 0) -> dict:
    arg_keys = jax.random.split(jax.random.key(seed), 13)
    return {
        "inputs": gaussian_with(arg_keys[0], (SEQS, SEQ, D), 1.0, 6.0, ((0, 32),), (0, 2, 32, 2.75)),
        "doc_ids": jax.vmap(lambda own: jnp.searchsorted(jnp.cumsum(uneven_parts(own, DOCS, SEQ, SEQ // 2, 1)), jnp.arange(SEQ), side="right"))(jax.random.split(arg_keys[1], SEQS)).reshape((SEQS, SEQ)).astype(jnp.int32),
        "attn_gain": jnp.clip(1.0 + 0.15 * jax.random.normal(arg_keys[2], (D,), jnp.float32), 0.25, 1.75).astype(jnp.bfloat16),
        "w_query": centred(arg_keys[3], (D, D), D ** -0.5, 0.21875, ((0, 16),)),
        "w_key": centred(arg_keys[4], (D, D), D ** -0.5, 0.21875, ((0, 16),)),
        "w_value": centred(arg_keys[5], (D, D), D ** -0.5, 0.21875, ((0, 16),)),
        "w_out": centred(arg_keys[6], (D, D), (D // 64) ** -0.5, 1.75, ((0, 16),)),
        "ffn_gain": jnp.clip(1.0 + 0.15 * jax.random.normal(arg_keys[7], (D,), jnp.float32), 0.25, 1.75).astype(jnp.bfloat16),
        "w_gate": centred(arg_keys[8], (D, FF), D ** -0.5, 0.21875, ((0, 16),)),
        "w_up": centred(arg_keys[9], (D, FF), D ** -0.5, 0.21875, ((0, 16),)),
        "w_down": centred(arg_keys[10], (FF, D), FF ** -0.5, 0.125, ((0, 16),)),
        "cotangent": gaussian_with(arg_keys[11], (SEQS, SEQ, D), 1.0, 6.0, ((0, 32),), (0, 2, 32, 2.75)),
    }


epsilon = 1e-06
rope_base = 10000.0
masked_score = -1e+30
highest = lax.Precision.HIGHEST

@jax.custom_vjp
def low(v):
    return lax.optimization_barrier(v.astype(jnp.bfloat16)).astype(jnp.float32)

@jax.custom_vjp
def low_back(v):
    return v

def low_keep(v):
    return (low(v), None)

def low_pass(kept, grad):
    return (grad,)

def back_keep(v):
    return (v, None)

def back_low(kept, grad):
    return (low(grad),)
low.defvjp(low_keep, low_pass)
low_back.defvjp(back_keep, back_low)

def rope_tables(length, head_size):
    position = jnp.arange(length, dtype=jnp.float32)
    exponent = jnp.arange(head_size // 2, dtype=jnp.float32) * (2.0 / head_size)
    angles = position[:, None] * jnp.power(rope_base, -exponent)[None, :]
    return (jnp.cos(angles)[:, None, :], jnp.sin(angles)[:, None, :])

def rotate(tensor, cosine_table, sine_table):
    midway = tensor.shape[-1] // 2
    front_half = tensor[..., :midway]
    back_half = tensor[..., midway:]
    return jnp.concatenate([front_half * cosine_table - back_half * sine_table, back_half * cosine_table + front_half * sine_table], axis=-1)

def allowed_pairs(doc_ids, offset, row_step, block_size):
    length = doc_ids.shape[1]
    row_docs = lax.dynamic_slice_in_dim(doc_ids, offset, row_step, 1)
    row_block = (offset + jnp.arange(row_step, dtype=jnp.int32)) // block_size
    col_block = jnp.arange(length, dtype=jnp.int32) // block_size
    same_doc = row_docs[:, :, None] == doc_ids[:, None, :]
    ordered = col_block[None, None, :] <= row_block[None, :, None]
    return (same_doc & ordered)[:, None, :, :]

def rms_scale(tensor):
    return tensor * lax.rsqrt(lax.optimization_barrier(jnp.mean(tensor * tensor, -1, keepdims=True)) + epsilon)

def attend(queries, keys_rot, value_vec, doc_ids):
    batch_size, length = (queries.shape[0], queries.shape[1])
    row_step = min(512, length)
    block_count = length // row_step
    query_blocks = jnp.moveaxis(queries.reshape(batch_size, block_count, row_step, H, HD), 1, 0)
    offsets = jnp.arange(block_count, dtype=jnp.int32) * row_step

    def one_block(block_item):
        query_block, offset = block_item
        allowed = allowed_pairs(doc_ids, offset, row_step, BLOCK)
        scores = jnp.einsum('bqhd,bkhd->bhqk', query_block, keys_rot, precision=highest) * HD ** (-0.5)
        scores = low_back(jnp.where(allowed, scores, masked_score))
        attn_probs = low(jax.nn.softmax(scores, axis=-1))
        return jnp.einsum('bhqk,bkhd->bqhd', attn_probs, value_vec, precision=highest)
    mixed_heads = lax.map(jax.checkpoint(one_block), (query_blocks, offsets))
    return jnp.moveaxis(mixed_heads, 0, 1).reshape(batch_size, length, H * HD)

def block_layer(tokens, doc_ids, attn_gain, w_query, w_key, w_value, w_out, ffn_gain, w_gate, w_up, w_down):
    batch_size, length = (tokens.shape[0], tokens.shape[1])
    cosine_table, sine_table = rope_tables(length, HD)
    attn_in = low(rms_scale(tokens) * attn_gain)

    def project(matrix):
        return low_back(jnp.einsum('btd,de->bte', attn_in, matrix, precision=highest)).reshape(batch_size, length, H, HD)
    queries = low(rotate(project(w_query), cosine_table, sine_table))
    keys_rot = low(rotate(project(w_key), cosine_table, sine_table))
    value_vec = low(project(w_value))
    mixed_heads = low(low_back(attend(queries, keys_rot, value_vec, doc_ids)))
    middle = tokens + low_back(jnp.einsum('btd,de->bte', mixed_heads, w_out, precision=highest))
    ffn_in = low(rms_scale(middle) * ffn_gain)
    gate_pre = low_back(jnp.einsum('btd,df->btf', ffn_in, w_gate, precision=highest))
    up_pre = low_back(jnp.einsum('btd,df->btf', ffn_in, w_up, precision=highest))
    hidden = low(jax.nn.silu(gate_pre) * up_pre)
    return middle + low_back(jnp.einsum('btf,fd->btd', hidden, w_down, precision=highest))

def reference(inputs, doc_ids, attn_gain, w_query, w_key, w_value, w_out, ffn_gain, w_gate, w_up, w_down, cotangent):
    float_weights = tuple((weight.astype(jnp.float32) for weight in (attn_gain, w_query, w_key, w_value, w_out, ffn_gain, w_gate, w_up, w_down)))
    group_size = math.gcd(SEQS, max(1, 4096 // SEQ))
    group_count = SEQS // group_size
    token_groups = inputs.astype(jnp.float32).reshape(group_count, group_size, SEQ, D)
    doc_groups = doc_ids.reshape(group_count, group_size, SEQ)
    cot_groups = cotangent.astype(jnp.float32).reshape(group_count, group_size, SEQ, D)

    def one_group(totals, group_item):
        group_tokens, doc_part, cot_part = group_item

        def forward(layer_in, *weights):
            return block_layer(layer_in, doc_part, *weights)
        result, pullback = jax.vjp(forward, group_tokens, *float_weights)
        gradients = pullback(cot_part)
        totals = tuple((running + added for running, added in zip(totals, gradients[1:])))
        return (totals, (result.astype(jnp.bfloat16), gradients[0]))
    initial = tuple((jnp.zeros(weight.shape, jnp.float32) for weight in float_weights))
    totals, (outputs, grad_inputs) = lax.scan(one_group, initial, (token_groups, doc_groups, cot_groups))
    scaled = tuple((total_grad / SEQS for total_grad in totals))
    return (outputs.reshape(SEQS, SEQ, D), grad_inputs.reshape(SEQS, SEQ, D), scaled[0], scaled[1], scaled[2], scaled[3], scaled[4], scaled[5], scaled[6], scaled[7], scaled[8])
```

```python
import functools

import jax
import jax.numpy as jnp
from jax import lax
from jax.experimental import pallas as pl
from jax.experimental.pallas import tpu as pltpu
from jax.sharding import PartitionSpec as P

H = 12
HD = 64
BLOCK = 256
MAX_DOC = 512

epsilon = 1e-06
rope_base = 10000.0
far = 1e30

bf16 = jnp.bfloat16
f32 = jnp.float32
MIB = 1 << 20
NN = (((1,), (0,)), ((), ()))
NT = (((1,), (1,)), ((), ()))
TN = (((0,), (0,)), ((), ()))


def dot(left, right, dims=NN):
    return lax.dot_general(left, right, dims, preferred_element_type=f32)


def params(mib):
    return pltpu.CompilerParams(vmem_limit_bytes=mib * MIB)


def cost(flops, nbytes, trans=0):
    return pl.CostEstimate(flops=int(flops), bytes_accessed=int(nbytes), transcendentals=int(trans))


ANY = pl.BlockSpec(memory_space=pl.ANY)


def load_weight(pieces, tab_ref, dest, sem):
    copies = []
    index = 0
    for piece in pieces:
        count, rows = piece.shape[0], piece.shape[1]
        for b in range(count):
            row = pl.multiple_of(tab_ref[0, index] * rows, 16)
            copies.append(
                pltpu.make_async_copy(
                    piece.at[b], dest.at[tab_ref[1, index], pl.ds(row, rows)], sem.at[index]
                )
            )
            index += 1
    for copy in copies:
        copy.start()
    return copies


def wait_all(copies):
    for copy in copies:
        copy.wait()


def rope_tables(length):
    position = jnp.arange(length, dtype=f32)
    exponent = jnp.arange(HD // 2, dtype=f32) * (2.0 / HD)
    angles = position[:, None] * jnp.power(rope_base, -exponent)[None, :]
    cosine, sine = jnp.cos(angles), jnp.sin(angles)
    return jnp.concatenate([cosine] * 4, 1), jnp.concatenate([-sine, sine, -sine, sine], 1)


def swap_halves(tensor):
    lane = lax.broadcasted_iota(jnp.int32, tensor.shape, 1)
    return jnp.where(
        (lane & (HD // 2)) == 0, pltpu.roll(tensor, 128 - HD // 2, 1), pltpu.roll(tensor, HD // 2, 1)
    )


def project_kernel(tab_ref, *refs, n_pieces, halves):
    pieces, (x_ref, cos_ref, sin_ref) = refs[:n_pieces], refs[n_pieces : n_pieces + 3]
    n_ref, q_ref, k_ref, v_ref, weight, sem = refs[n_pieces + 3 :]

    @pl.when(pl.program_id(0) == 0)
    def _():
        wait_all(load_weight(pieces, tab_ref, weight, sem))

    x = x_ref[...].astype(f32)
    normed = (x * lax.rsqrt(jnp.mean(x * x, -1, keepdims=True) + epsilon)).astype(bf16)
    n_ref[...] = normed
    width = x_ref.shape[1] // halves
    cosine, sine = cos_ref[...], sin_ref[...]
    for half in range(halves):
        result = dot(normed, weight[half])
        for part, out, scale in ((0, q_ref, HD**-0.5), (1, k_ref, 1.0)):
            for c in range(0, width, 128):
                piece = result[:, part * width + c : part * width + c + 128]
                turned = piece * cosine + swap_halves(piece) * sine
                out[:, half * width + c : half * width + c + 128] = (
                    turned.astype(bf16) * jnp.asarray(scale, bf16)
                )
        v_ref[:, half * width : (half + 1) * width] = result[:, 2 * width :].astype(bf16)


def project(tab, pieces, x, cosine, sine, halves):
    length, width = x.shape
    rows = BLOCK
    n = len(pieces)
    blocks = sum(p.shape[0] for p in pieces)
    block = pl.BlockSpec((rows, width), lambda i, t: (i, 0))
    table = pl.BlockSpec((rows, 128), lambda i, t: (i, 0))
    shape = jax.ShapeDtypeStruct((length, width), bf16)
    return pl.pallas_call(
        functools.partial(project_kernel, n_pieces=n, halves=halves),
        grid_spec=pltpu.PrefetchScalarGridSpec(
            num_scalar_prefetch=1,
            grid=(length // rows,),
            in_specs=[ANY] * n + [block, table, table],
            out_specs=[block] * 4,
            scratch_shapes=[
                pltpu.VMEM((halves, width, 3 * width // halves), bf16),
                pltpu.SemaphoreType.DMA((blocks,)),
            ],
        ),
        out_shape=[shape] * 4,
        compiler_params=params(40),
        cost_estimate=cost(6 * length * width * width, 16 * length * width),
        name="project",
    )(tab, *pieces, x, cosine, sine)


def key_range(block):
    low = max(0, (block * BLOCK - (MAX_DOC - 1)) // BLOCK) if block * BLOCK > MAX_DOC - 1 else 0
    return low * BLOCK, (block + 1) * BLOCK


def marks(docs):
    lane = jnp.arange(128, dtype=jnp.int32)[None, :] % HD
    used = lane < 4
    same = docs == lane
    return (
        jnp.where(used & ~same, -far, 0.0).astype(bf16),
        jnp.where(used & same, 1.0, 0.0).astype(bf16),
    )


def attend_kernel(q_ref, k_ref, v_ref, qm_ref, km_ref, mixed_ref, inv_ref, e_ref):
    length = q_ref.shape[0]
    lane = lax.broadcasted_iota(jnp.int32, (length, 128), 1)
    q, k, v = q_ref[...], k_ref[...], v_ref[...]
    operands = []
    for head in range(2):
        own = (lane < HD) if head == 0 else (lane >= HD)
        ones = jnp.ones((length, 128), bf16)
        operands.append(
            (
                jnp.where(own, q, qm_ref[...]),
                jnp.where(own, k, km_ref[...]),
                jnp.where(own, v, ones).T,
            )
        )
    for block in range(length // BLOCK):
        low, high = key_range(block)
        rows = slice(block * BLOCK, (block + 1) * BLOCK)
        outs, invs = [], []
        for head in range(2):
            qa, ka, vt = operands[head]
            scores = dot(ka[low:high], qa[rows], NT)
            exps = jnp.exp(scores - jnp.max(scores, 0, keepdims=True)).astype(bf16)
            e_ref[head, block, 0 : high - low, :] = exps
            out = dot(vt[:, low:high], exps)
            total = out[HD : HD + 1] if head == 0 else out[0:1]
            inverse = 1.0 / total
            outs.append(out[head * HD : (head + 1) * HD] * inverse)
            invs.append(jnp.broadcast_to(inverse, (HD, BLOCK)))
        mixed_ref[rows, :] = jnp.concatenate(outs, 0).T.astype(bf16)
        inv_ref[rows, :] = jnp.concatenate(invs, 0).T


def attend(q, k, v, q_marks, k_marks):
    length, width = q.shape
    pairs = width // 128
    blocks = length // BLOCK
    most = max(key_range(b)[1] - key_range(b)[0] for b in range(blocks))
    column = pl.BlockSpec((length, 128), lambda i: (0, i))
    fixed = pl.BlockSpec((length, 128), lambda i: (0, 0))
    return pl.pallas_call(
        attend_kernel,
        grid=(pairs,),
        in_specs=[column, column, column, fixed, fixed],
        out_specs=[
            column,
            column,
            pl.BlockSpec((2, blocks, most, BLOCK), lambda i: (i, 0, 0, 0)),
        ],
        out_shape=[
            jax.ShapeDtypeStruct((length, width), bf16),
            jax.ShapeDtypeStruct((length, width), f32),
            jax.ShapeDtypeStruct((2 * pairs, blocks, most, BLOCK), bf16),
        ],
        compiler_params=params(48),
        cost_estimate=cost(10 * length * length * width, 30 * length * width, H * length * length),
        name="attend",
    )(q, k, v, q_marks, k_marks)


def attend_back_kernel(
    q_ref, k_ref, v_ref, mixed_ref, inv_ref, e_ref, grad_ref, cos_ref, sin_ref,
    dq_ref, dk_ref, dv_ref, dk_sum, dv_sum,
):
    length = q_ref.shape[0]
    lane = lax.broadcasted_iota(jnp.int32, (length, 128), 1)
    part = lax.broadcasted_iota(jnp.int32, (BLOCK, 128), 1)
    q, k, v = q_ref[...], k_ref[...], v_ref[...]
    zero = jnp.zeros((length, 128), bf16)
    dk_sum[...] = jnp.zeros_like(dk_sum)
    dv_sum[...] = jnp.zeros_like(dv_sum)
    operands = []
    for head in range(2):
        own = (lane < HD) if head == 0 else (lane >= HD)
        spare = (lane == HD) | (lane == HD + 1) if head == 0 else lane < 2
        minus = jnp.where(spare, -1.0, 0.0).astype(bf16)
        operands.append(
            (jnp.where(own, q, zero), jnp.where(own, k, zero).T, jnp.where(own, v, minus))
        )
    for block in range(length // BLOCK):
        low, high = key_range(block)
        rows = slice(block * BLOCK, (block + 1) * BLOCK)
        scaled = grad_ref[rows, :].astype(f32) * inv_ref[rows, :]
        inner = scaled * mixed_ref[rows, :].astype(f32)
        dq = jnp.zeros((128, BLOCK), f32)
        for head in range(2):
            qo, kt, va = operands[head]
            own = (part < HD) if head == 0 else (part >= HD)
            first = HD if head == 0 else 0
            delta = jnp.sum(jnp.where(own, inner, 0.0), 1, keepdims=True)
            upper = delta.astype(bf16).astype(f32)
            masked = jnp.where(own, scaled, 0.0)
            joined = jnp.where(part == first, upper, masked)
            joined = jnp.where(part == first + 1, delta - upper, joined).astype(bf16)
            masked = masked.astype(bf16)
            exps = e_ref[head, block, 0 : high - low, :]
            slope = dot(va[low:high], joined, NT)
            ds = (exps.astype(f32) * slope).astype(bf16)
            dv_sum[low:high, :] += dot(exps, masked)
            dk_sum[low:high, :] += dot(ds, qo[rows])
            dq += dot(kt[:, low:high], ds)
        turned = dq.T * (HD**-0.5)
        dq_ref[rows, :] = (
            turned * cos_ref[rows, :] - swap_halves(turned) * sin_ref[rows, :]
        ).astype(bf16)
    dk = dk_sum[...]
    dk_ref[...] = (dk * cos_ref[...] - swap_halves(dk) * sin_ref[...]).astype(bf16)
    dv_ref[...] = dv_sum[...].astype(bf16)


def attend_back(q, k, v, mixed, inv, exps, grad, cosine, sine):
    length, width = q.shape
    pairs = width // 128
    column = pl.BlockSpec((length, 128), lambda i: (0, i))
    fixed = pl.BlockSpec((length, 128), lambda i: (0, 0))
    shape = jax.ShapeDtypeStruct((length, width), bf16)
    return pl.pallas_call(
        attend_back_kernel,
        grid=(pairs,),
        in_specs=[column] * 5
        + [pl.BlockSpec((2,) + exps.shape[1:], lambda i: (i, 0, 0, 0)), column, fixed, fixed],
        out_specs=[column] * 3,
        out_shape=[shape] * 3,
        scratch_shapes=[pltpu.VMEM((length, 128), f32)] * 2,
        compiler_params=params(48),
        cost_estimate=cost(20 * length * length * width, 36 * length * width),
        name="attend_back",
    )(q, k, v, mixed, inv, exps, grad, cosine, sine)


def ffn_kernel(tab_ref, *refs, n_pieces, halves):
    pieces, (x_ref, mixed_ref) = refs[:n_pieces], refs[n_pieces : n_pieces + 2]
    middle_ref, normed_ref, hidden_ref, slope_g_ref, slope_u_ref, weight, sem = refs[n_pieces + 2 :]

    @pl.when(pl.program_id(0) == 0)
    def _():
        wait_all(load_weight(pieces, tab_ref, weight, sem))

    width = x_ref.shape[1] // halves
    inner = hidden_ref.shape[1] // halves
    mixed = mixed_ref[...]
    middle = x_ref[...].astype(f32) + jnp.concatenate(
        [dot(mixed, weight[h, :, 0:width]) for h in range(halves)], 1
    )
    middle_ref[...] = middle
    normed = (middle * lax.rsqrt(jnp.mean(middle * middle, -1, keepdims=True) + epsilon)).astype(bf16)
    normed_ref[...] = normed
    step = min(512, inner)
    for h in range(halves):
        for c in range(0, inner, step):
            gate = dot(normed, weight[h, :, width + c : width + c + step])
            up = dot(normed, weight[h, :, width + inner + c : width + inner + c + step])
            sigmoid = jax.nn.sigmoid(gate)
            silu = gate * sigmoid
            cols = slice(h * inner + c, h * inner + c + step)
            hidden_ref[:, cols] = (silu * up).astype(bf16)
            slope_u_ref[:, cols] = silu.astype(bf16)
            slope_g_ref[:, cols] = (up * sigmoid * (1.0 + gate * (1.0 - sigmoid))).astype(bf16)


def ffn(tab, pieces, x, mixed, inner, halves):
    length, width = x.shape
    rows = BLOCK
    n = len(pieces)
    blocks = sum(p.shape[0] for p in pieces)
    narrow = pl.BlockSpec((rows, width), lambda i, t: (i, 0))
    wide = pl.BlockSpec((rows, inner), lambda i, t: (i, 0))
    wide_shape = jax.ShapeDtypeStruct((length, inner), bf16)
    return pl.pallas_call(
        functools.partial(ffn_kernel, n_pieces=n, halves=halves),
        grid_spec=pltpu.PrefetchScalarGridSpec(
            num_scalar_prefetch=1,
            grid=(length // rows,),
            in_specs=[ANY] * n + [narrow, narrow],
            out_specs=[narrow, narrow, wide, wide, wide],
            scratch_shapes=[
                pltpu.VMEM((halves, width, (width + 2 * inner) // halves), bf16),
                pltpu.SemaphoreType.DMA((blocks,)),
            ],
        ),
        out_shape=[
            jax.ShapeDtypeStruct((length, width), f32),
            jax.ShapeDtypeStruct((length, width), bf16),
            wide_shape,
            wide_shape,
            wide_shape,
        ],
        compiler_params=params(48),
        cost_estimate=cost(2 * length * width * (width + 2 * inner), 8 * width * inner + 8 * length * inner),
        name="ffn",
    )(tab, *pieces, x, mixed)


def ffn_back_kernel(tab2_ref, tab3_ref, *refs, n2, n3, halves):
    pieces2, pieces3 = refs[:n2], refs[n2 : n2 + n3]
    middle_ref, hidden_ref, slope_g_ref, slope_u_ref, cot_ref = refs[n2 + n3 : n2 + n3 + 5]
    (
        output_ref, gg_ref, gu_ref, grad_middle_ref, attn_grad_ref, grad_mixed_ref,
        weight2, weight3, sem2, sem3,
    ) = refs[n2 + n3 + 5 :]

    @pl.when(pl.program_id(0) == 0)
    def _():
        copies = load_weight(pieces3, tab3_ref, weight3, sem3)
        copies += load_weight(pieces2, tab2_ref, weight2, sem2)
        wait_all(copies)

    width = cot_ref.shape[1] // halves
    inner = hidden_ref.shape[1] // halves
    middle = middle_ref[...]
    hidden = hidden_ref[...]
    cot = cot_ref[...]
    for h in range(halves):
        cols = slice(h * width, (h + 1) * width)
        output_ref[:, cols] = (middle[:, cols] + dot(hidden, weight3[h])).astype(bf16)
    grad = jnp.zeros(middle.shape, f32)
    step = min(512, inner)
    for h in range(halves):
        for c in range(0, inner, step):
            cols = slice(h * inner + c, h * inner + c + step)
            grad_hidden = jnp.zeros((middle.shape[0], step), f32)
            for j in range(halves):
                grad_hidden += dot(cot[:, j * width : (j + 1) * width], weight3[j, cols, :], NT)
            gg = (grad_hidden * slope_g_ref[:, cols].astype(f32)).astype(bf16)
            gu = (grad_hidden * slope_u_ref[:, cols].astype(f32)).astype(bf16)
            gg_ref[:, cols] = gg
            gu_ref[:, cols] = gu
            grad += dot(gg, weight2[h, :, width + c : width + c + step], NT)
            grad += dot(gu, weight2[h, :, width + inner + c : width + inner + c + step], NT)
    inverse = lax.rsqrt(jnp.mean(middle * middle, -1, keepdims=True) + epsilon)
    normed = middle * inverse
    grad_middle = cot.astype(f32) + inverse * (
        grad - normed * jnp.mean(grad * normed, -1, keepdims=True)
    )
    grad_middle_ref[...] = grad_middle
    low = grad_middle.astype(bf16)
    attn_grad_ref[...] = low
    total = jnp.zeros(middle.shape, f32)
    for h in range(halves):
        total += dot(low[:, h * width : (h + 1) * width], weight2[h, :, 0:width], NT)
    grad_mixed_ref[...] = total.astype(bf16)


def ffn_back(tab2, pieces2, tab3, pieces3, middle, hidden, slope_g, slope_u, cot, halves):
    length, width = middle.shape
    inner = hidden.shape[1]
    rows = BLOCK
    n2, n3 = len(pieces2), len(pieces3)
    narrow = pl.BlockSpec((rows, width), lambda i, t, u: (i, 0))
    wide = pl.BlockSpec((rows, inner), lambda i, t, u: (i, 0))
    narrow_low = jax.ShapeDtypeStruct((length, width), bf16)
    wide_low = jax.ShapeDtypeStruct((length, inner), bf16)
    return pl.pallas_call(
        functools.partial(ffn_back_kernel, n2=n2, n3=n3, halves=halves),
        grid_spec=pltpu.PrefetchScalarGridSpec(
            num_scalar_prefetch=2,
            grid=(length // rows,),
            in_specs=[ANY] * (n2 + n3) + [narrow, wide, wide, wide, narrow],
            out_specs=[narrow, wide, wide, narrow, narrow, narrow],
            scratch_shapes=[
                pltpu.VMEM((halves, width, (width + 2 * inner) // halves), bf16),
                pltpu.VMEM((halves, inner, width // halves), bf16),
                pltpu.SemaphoreType.DMA((sum(p.shape[0] for p in pieces2),)),
                pltpu.SemaphoreType.DMA((sum(p.shape[0] for p in pieces3),)),
            ],
        ),
        out_shape=[
            narrow_low,
            wide_low,
            wide_low,
            jax.ShapeDtypeStruct((length, width), f32),
            narrow_low,
            narrow_low,
        ],
        compiler_params=params(56),
        cost_estimate=cost(
            2 * length * width * (width + 4 * inner), 12 * width * inner + 12 * length * inner
        ),
        name="ffn_back",
    )(tab2, tab3, *pieces2, *pieces3, middle, hidden, slope_g, slope_u, cot)


def input_kernel(tab_ref, *refs, n_pieces, halves):
    pieces = refs[:n_pieces]
    x_ref, grad_middle_ref, dq_ref, dk_ref, dv_ref, out_ref, weight, sem = refs[n_pieces:]

    @pl.when(pl.program_id(0) == 0)
    def _():
        wait_all(load_weight(pieces, tab_ref, weight, sem))

    width = x_ref.shape[1] // halves
    grad = jnp.zeros(x_ref.shape, f32)
    for h in range(halves):
        for part, ref in ((0, dq_ref), (1, dk_ref), (2, dv_ref)):
            grad += dot(
                ref[:, h * width : (h + 1) * width],
                weight[h, :, part * width : (part + 1) * width],
                NT,
            )
    x = x_ref[...].astype(f32)
    inverse = lax.rsqrt(jnp.mean(x * x, -1, keepdims=True) + epsilon)
    normed = x * inverse
    out_ref[...] = grad_middle_ref[...] + inverse * (
        grad - normed * jnp.mean(grad * normed, -1, keepdims=True)
    )


def input_grad(tab, pieces, x, grad_middle, dq, dk, dv, halves):
    length, width = x.shape
    rows = BLOCK
    n = len(pieces)
    blocks = sum(p.shape[0] for p in pieces)
    block = pl.BlockSpec((rows, width), lambda i, t: (i, 0))
    return pl.pallas_call(
        functools.partial(input_kernel, n_pieces=n, halves=halves),
        grid_spec=pltpu.PrefetchScalarGridSpec(
            num_scalar_prefetch=1,
            grid=(length // rows,),
            in_specs=[ANY] * n + [block] * 5,
            out_specs=block,
            scratch_shapes=[
                pltpu.VMEM((halves, width, 3 * width // halves), bf16),
                pltpu.SemaphoreType.DMA((blocks,)),
            ],
        ),
        out_shape=jax.ShapeDtypeStruct((length, width), f32),
        compiler_params=params(40),
        cost_estimate=cost(6 * length * width * width, 20 * length * width),
        name="input_grad",
    )(tab, *pieces, x, grad_middle, dq, dk, dv)


def weight_kernel(tab_ref, *refs, n_right, block_rows, halves):
    left_ref, rights = refs[0], refs[1 : 1 + n_right]
    keep_ref, send_ref, held, sem = refs[1 + n_right :]
    step, steps = pl.program_id(0), pl.num_programs(0)
    slot = lax.rem(step, 2)
    rows = left_ref.shape[1]
    count = rows // block_rows
    kept = keep_ref.shape[0]

    def wait(which):
        for i in range(count * halves):
            pltpu.make_async_copy(held.at[which, 0, pl.ds(0, block_rows)], keep_ref.at[0], sem.at[which, i]).wait()

    @pl.when(step >= 2)
    def _():
        wait(slot)

    left = left_ref[...]
    for h in range(halves):
        offset = 0
        for right in rights:
            width = right.shape[1] // halves
            held[slot, h, :, offset : offset + width] = dot(
                left, right[:, h * width : (h + 1) * width], TN
            ).astype(bf16)
            offset += width
    for b in range(count):
        for h in range(halves):
            place = tab_ref[(step * count + b) * halves + h]
            source = held.at[slot, h, pl.ds(b * block_rows, block_rows)]
            signal = sem.at[slot, b * halves + h]

            @pl.when(place < kept)
            def _():
                pltpu.make_async_copy(source, keep_ref.at[place], signal).start()

            @pl.when(place >= kept)
            def _():
                pltpu.make_async_copy(source, send_ref.at[place - kept], signal).start()

    @pl.when(step == steps - 1)
    def _():
        wait(slot)

        @pl.when(steps > 1)
        def _():
            wait(1 - slot)


def weight_grad(tab, left, rights, block_rows, halves, steps, two, name):
    length, rows = left.shape
    columns = sum(r.shape[1] for r in rights) // halves
    blocks = rows // block_rows * halves
    kept = blocks // 2 if two else blocks
    sent = blocks - kept if two else 1
    step_rows = rows // steps
    return pl.pallas_call(
        functools.partial(weight_kernel, n_right=len(rights), block_rows=block_rows, halves=halves),
        grid_spec=pltpu.PrefetchScalarGridSpec(
            num_scalar_prefetch=1,
            grid=(steps,),
            in_specs=[pl.BlockSpec((length, step_rows), lambda i, t: (0, i))]
            + [pl.BlockSpec(r.shape, lambda i, t: (0, 0)) for r in rights],
            out_specs=[ANY, ANY],
            scratch_shapes=[
                pltpu.VMEM((2, halves, step_rows, columns), bf16),
                pltpu.SemaphoreType.DMA((2, step_rows // block_rows * halves)),
            ],
        ),
        out_shape=[
            jax.ShapeDtypeStruct((kept, block_rows, columns), bf16),
            jax.ShapeDtypeStruct((sent, block_rows, columns), bf16),
        ],
        compiler_params=params(48),
        cost_estimate=cost(
            2 * length * rows * columns * halves,
            2 * (length * rows + length * columns * halves + rows * columns * halves),
        ),
        name=name,
    )(tab, left, *rights)


def place_of(xr, yr, zr, cr):
    low = xr * 4 + yr * 2 + zr
    high = 8 + yr * 4 + xr * 2 + (zr - 2)
    return cr * 16 + jnp.where(zr < 2, low, high)


def swapped(bits, axis="shard"):
    count = lax.axis_size(axis)
    pairs = [(i, i ^ bits) for i in range(count)]
    return lambda array: lax.ppermute(array, axis, pairs)


class Direct:
    halves = 2
    two = True

    def __init__(self):
        self.me = lax.axis_index("shard")
        self.x = lax.axis_index("rep")
        self.core, self.y, self.x_move = swapped(1), swapped(2), swapped(1, "rep")
        self.z = [swapped(4), swapped(8), swapped(12)]
        shard = jnp.arange(16, dtype=jnp.int32)[:, None]
        half = jnp.arange(2, dtype=jnp.int32)[None, :]
        rel = shard ^ self.me
        place = place_of(half ^ self.x, (rel >> 1) & 1, rel >> 2, rel & 1)
        self.place = place.reshape(32)
        order = []
        for cr in range(2):
            for zs in ((0, 1), (2, 3)):
                for outer in range(2):
                    for inner in range(2):
                        for zr in zs:
                            xr, yr = (outer, inner) if zs[0] == 0 else (inner, outer)
                            order.append((zr * 4 + yr * 2 + cr, xr))
        rel_shard = jnp.array([o[0] for o in order], jnp.int32)
        rel_half = jnp.array([o[1] for o in order], jnp.int32)
        self.tab = jnp.stack([rel_shard ^ self.me, rel_half ^ self.x])

    def own_half(self, array):
        width = array.shape[1] // 2
        return lax.dynamic_slice(array, (0, self.x * width), (array.shape[0], width))

    def pack(self, arrays):
        return jnp.concatenate([self.own_half(a) for a in arrays], 1)

    def gather(self, block):
        own = block[None]
        z1, z2, z3 = (move(own) for move in self.z)
        a1 = jnp.concatenate([own, z1], 0)
        b1 = jnp.concatenate([z2, z3], 0)
        a2 = jnp.concatenate([a1, self.y(a1)], 0)
        b2 = jnp.concatenate([b1, self.x_move(b1)], 0)
        a2x, b2y = self.x_move(a2), self.y(b2)
        own_core = [a2, a2x, b2, b2y]
        return own_core + [self.core(p) for p in own_core]

    def scatter(self, grads):
        keep, send = grads
        got = self.core(send)

        def add(*terms):
            total = terms[0].astype(f32)
            for term in terms[1:]:
                total = total + term.astype(f32)
            return total

        ax = self.x_move(add(keep[4:8], got[4:8]).astype(bf16))
        by = self.y(add(keep[12:16], got[12:16]).astype(bf16))
        ay = self.y(add(keep[2:4], got[2:4], ax[2:4]).astype(bf16))
        bx = self.x_move(add(keep[10:12], got[10:12], by[2:4]).astype(bf16))
        z1 = self.z[0](add(keep[1], got[1], ax[1], ay[1]).astype(bf16))
        z2 = self.z[1](add(keep[8], got[8], by[0], bx[0]).astype(bf16))
        z3 = self.z[2](add(keep[9], got[9], by[1], bx[1]).astype(bf16))
        own = add(keep[0], got[0], ax[0], ay[0], z1, z2, z3).astype(bf16)
        other = self.x_move(own)
        return [jnp.where(self.x == 0, own, other), jnp.where(self.x == 0, other, own)]


class Plain:
    halves = 1
    two = False

    def __init__(self):
        self.place = jnp.zeros((1,), jnp.int32)
        self.tab = jnp.zeros((2, 1), jnp.int32)

    def pack(self, arrays):
        return jnp.concatenate(arrays, 1)

    def gather(self, block):
        return [lax.all_gather(block, "shard", axis=0, tiled=True)[None]]

    def scatter(self, grads):
        part = lax.psum_scatter(grads[0][0].astype(f32), "shard", scatter_dimension=0, tiled=True)
        return [lax.psum(part.astype(bf16), "rep")]


def columns_of(halves, *widths):
    arrays = []
    offset = 0
    for width in widths:
        step = width // len(halves)
        arrays.append(
            jnp.concatenate([h[:, offset : offset + step] for h in halves], 1).astype(f32)
        )
        offset += step
    return arrays


def one_sequence(moves, x, docs, tabs, w1, w2, w3, cot, inner):
    cosine, sine = rope_tables(x.shape[0])
    q_marks, k_marks = marks(docs.reshape(-1, 1))
    halves = moves.halves
    normed1, q, k, v = project(tabs, w1, x, cosine, sine, halves)
    mixed, inv, exps = attend(q, k, v, q_marks, k_marks)
    middle, normed2, hidden, slope_g, slope_u = ffn(tabs, w2, x, mixed, inner, halves)
    output, gg, gu, grad_middle, attn_grad, grad_mixed = ffn_back(
        tabs, w2, tabs, w3, middle, hidden, slope_g, slope_u, cot, halves
    )
    dq, dk, dv = attend_back(q, k, v, mixed, inv, exps, grad_mixed, cosine, sine)
    grad_input = input_grad(tabs, w1, x, grad_middle, dq, dk, dv, halves)
    width = x.shape[1]
    place = moves.place

    def cut(rows):
        return rows // 16 if moves.two else rows

    def weights(left, rights, steps, name):
        rows = left.shape[1]
        steps = steps if moves.two else 1
        return weight_grad(place, left, rights, cut(rows), halves, steps, moves.two, name)

    g3 = weights(hidden, [cot], 8, "grad_down")
    g2 = weights(normed2, [gg, gu], 2, "grad_gate_up")
    go = weights(mixed, [attn_grad], 2, "grad_out")
    g1 = weights(normed1, [dq, dk, dv], 2, "grad_qkv")
    return output, grad_input, g1, go, g2, g3


def per_device(
    inputs,
    doc_ids,
    attn_gain,
    w_query,
    w_key,
    w_value,
    w_out,
    ffn_gain,
    w_gate,
    w_up,
    w_down,
    cotangent,
):
    batch_size, length, width = inputs.shape
    inner = w_gate.shape[1]
    replicas, members = lax.axis_size("rep"), lax.axis_size("shard")
    moves = Direct() if (replicas, members, batch_size) == (2, 16, 1) else Plain()
    gain1 = attn_gain.astype(f32)[:, None]
    gain2 = ffn_gain.astype(f32)[:, None]

    def fold(weight, gain):
        return (weight.astype(f32) * gain).astype(bf16)

    w1 = moves.gather(moves.pack([fold(w, gain1) for w in (w_query, w_key, w_value)]))
    w2 = moves.gather(moves.pack([w_out, fold(w_gate, gain2), fold(w_up, gain2)]))
    w3 = moves.gather(moves.pack([w_down]))
    outputs, grad_inputs, totals = [], [], None
    for b in range(batch_size):
        output, grad_input, *grads = one_sequence(
            moves, inputs[b], doc_ids[b], moves.tab, w1, w2, w3, cotangent[b], inner
        )
        outputs.append(output)
        grad_inputs.append(grad_input)
        totals = grads if totals is None else jax.tree.map(jnp.add, totals, grads)
    g1, go, g2, g3 = totals
    scale = 1.0 / (batch_size * replicas * members)
    (down,) = columns_of(moves.scatter(g3), width)
    gate, up = columns_of(moves.scatter(g2), inner, inner)
    (out,) = columns_of(moves.scatter(go), width)
    query, key, value = columns_of(moves.scatter(g1), width, width, width)

    def gain_grad(pairs):
        total = sum(jnp.sum(w.astype(f32) * g, 1) for w, g in pairs)
        return total * scale

    return (
        jnp.stack(outputs),
        jnp.stack(grad_inputs),
        gain_grad([(w_query, query), (w_key, key), (w_value, value)]),
        query * gain1 * scale,
        key * gain1 * scale,
        value * gain1 * scale,
        out * scale,
        gain_grad([(w_gate, gate), (w_up, up)]),
        gate * gain2 * scale,
        up * gain2 * scale,
        down * scale,
    )


def solution(mesh):
    row = P("shard", None)
    tokens = P(("rep", "shard"), None, None)
    return jax.shard_map(
        per_device,
        mesh=mesh,
        in_specs=(
            tokens, P(("rep", "shard"), None), P("shard"), row, row, row, row, P("shard"), row, row, row, tokens,
        ),
        out_specs=(tokens, tokens, P("shard"), row, row, row, row, P("shard"), row, row, row),
        check_vma=False,
    )
```

```python
import functools

import jax
import jax.numpy as jnp
from jax import lax
from jax.experimental import pallas as pl
from jax.experimental.pallas import tpu as pltpu
from jax.sharding import PartitionSpec as P

H = 12
HD = 64
BLOCK = 256
MAX_DOC = 512

epsilon = 1e-06
rope_base = 10000.0
far = 1e30

bf16 = jnp.bfloat16
f32 = jnp.float32
MIB = 1 << 20
NN = (((1,), (0,)), ((), ()))
NT = (((1,), (1,)), ((), ()))
TN = (((0,), (0,)), ((), ()))


def dot(left, right, dims=NN):
    return lax.dot_general(left, right, dims, preferred_element_type=f32)


def params():
    return pltpu.CompilerParams(vmem_limit_bytes=60 * MIB)


HINT = 1.0


def cost(flops, nbytes, trans=0):
    return pl.CostEstimate(
        flops=int(HINT * flops), bytes_accessed=int(HINT * nbytes), transcendentals=int(HINT * trans)
    )


ANY = pl.BlockSpec(memory_space=pl.ANY)


def weight_copies(pieces, tab_ref, dest, sem, start, width):
    copies = []
    index = 0
    for piece in pieces:
        count, rows = piece.shape[0], piece.shape[1]
        for b in range(count):
            row = pl.multiple_of(tab_ref[0, index] * rows, 16)
            col = pl.multiple_of(tab_ref[1, index] * width, 128)
            copies.append(
                pltpu.make_async_copy(
                    piece.at[b, :, pl.ds(start, width)],
                    dest.at[pl.ds(row, rows), pl.ds(col, width)],
                    sem.at[index],
                )
            )
            index += 1
    return copies


def start_all(copies):
    for copy in copies:
        copy.start()


def wait_all(copies):
    for copy in copies:
        copy.wait()


def load_weight(pieces, tab_ref, dest, sem):
    copies = weight_copies(pieces, tab_ref, dest, sem, 0, pieces[0].shape[2])
    start_all(copies)
    wait_all(copies)


GROUPS = 3


def in_order(refs, half=0, halves=1):
    return jnp.concatenate(
        [
            ref[:, j * 128 : (j + 1) * 128]
            for j in range(2)
            if j * halves // 2 == half
            for ref in refs
        ],
        1,
    )


def pack_kernel(half_ref, *refs, folded):
    *sources, gain_ref, out_ref = refs
    offset = 0
    for source, scaled in zip(sources, folded):
        width = source.shape[1]
        value = source[...]
        if scaled:
            value = (value.astype(f32) * gain_ref[...]).astype(bf16)
        out_ref[:, offset : offset + width] = value
        offset += width


def pack(half, arrays, gain, halves):
    folded = [scaled for _, scaled in arrays]
    arrays = [array for array, _ in arrays]
    rows = arrays[0].shape[0]
    columns = sum(array.shape[1] for array in arrays) // halves
    return pl.pallas_call(
        functools.partial(pack_kernel, folded=folded),
        grid_spec=pltpu.PrefetchScalarGridSpec(
            num_scalar_prefetch=1,
            grid=(1,),
            in_specs=[
                pl.BlockSpec((rows, array.shape[1] // halves), lambda i, h: (0, h[0])) for array in arrays
            ]
            + [pl.BlockSpec((rows, 1), lambda i, h: (0, 0))],
            out_specs=pl.BlockSpec((rows, columns), lambda i, h: (0, 0)),
        ),
        out_shape=jax.ShapeDtypeStruct((rows, columns), bf16),
        compiler_params=params(),
        cost_estimate=cost(rows * columns, 4 * rows * columns),
        name="pack",
    )(half.reshape(1), *arrays, gain)


def rope_tables(length):
    position = jnp.arange(length, dtype=f32)
    exponent = jnp.arange(HD // 2, dtype=f32) * (2.0 / HD)
    angles = position[:, None] * jnp.power(rope_base, -exponent)[None, :]
    cosine, sine = jnp.cos(angles), jnp.sin(angles)
    return jnp.concatenate([cosine] * 4, 1), jnp.concatenate([-sine, sine, -sine, sine], 1)


def swap_halves(tensor):
    lane = lax.broadcasted_iota(jnp.int32, tensor.shape, 1)
    return jnp.where(
        (lane & (HD // 2)) == 0, pltpu.roll(tensor, 128 - HD // 2, 1), pltpu.roll(tensor, HD // 2, 1)
    )


def project_kernel(tab_ref, *refs, n_pieces, halves):
    pieces, (x_ref, cos_ref, sin_ref) = refs[:n_pieces], refs[n_pieces : n_pieces + 3]
    n_ref, q_ref, k_ref, v_ref, weight, sem = refs[n_pieces + 3 :]

    @pl.when(pl.program_id(0) == 0)
    def _():
        load_weight(pieces, tab_ref, weight, sem)

    x = x_ref[...].astype(f32)
    normed = (x * lax.rsqrt(jnp.mean(x * x, -1, keepdims=True) + epsilon)).astype(bf16)
    n_ref[...] = normed
    width = x_ref.shape[1] // halves
    cosine, sine = cos_ref[...], sin_ref[...]
    for half in range(halves):
        result = dot(normed, weight[:, 3 * half * width : 3 * (half + 1) * width])
        for part, out, scale in ((0, q_ref, HD**-0.5), (1, k_ref, 1.0)):
            for c in range(0, width, 128):
                piece = result[:, part * width + c : part * width + c + 128]
                turned = piece * cosine + swap_halves(piece) * sine
                out[:, half * width + c : half * width + c + 128] = (
                    turned.astype(bf16) * jnp.asarray(scale, bf16)
                )
        v_ref[:, half * width : (half + 1) * width] = result[:, 2 * width :].astype(bf16)


def project(tab, pieces, x, cosine, sine, halves):
    length, width = x.shape
    rows = BLOCK
    n = len(pieces)
    blocks = sum(p.shape[0] for p in pieces)
    block = pl.BlockSpec((rows, width), lambda i, t: (i, 0))
    table = pl.BlockSpec((rows, 128), lambda i, t: (i, 0))
    shape = jax.ShapeDtypeStruct((length, width), bf16)
    return pl.pallas_call(
        functools.partial(project_kernel, n_pieces=n, halves=halves),
        grid_spec=pltpu.PrefetchScalarGridSpec(
            num_scalar_prefetch=1,
            grid=(length // rows,),
            in_specs=[ANY] * n + [block, table, table],
            out_specs=[block] * 4,
            scratch_shapes=[
                pltpu.VMEM((width, 3 * width), bf16),
                pltpu.SemaphoreType.DMA((blocks,)),
            ],
        ),
        out_shape=[shape] * 4,
        compiler_params=params(),
        cost_estimate=cost(6 * length * width * width, 16 * length * width),
        name="project",
    )(tab, *pieces, x, cosine, sine)


def key_range(block):
    low = max(0, (block * BLOCK - (MAX_DOC - 1)) // BLOCK) if block * BLOCK > MAX_DOC - 1 else 0
    return low * BLOCK, (block + 1) * BLOCK


def marks(docs):
    lane = jnp.arange(128, dtype=jnp.int32)[None, :] % HD
    used = lane < 4
    same = docs == lane
    return (
        jnp.where(used & ~same, -far, 0.0).astype(bf16),
        jnp.where(used & same, 1.0, 0.0).astype(bf16),
    )


def pipeline(items, first, second, third):
    ahead = 2
    made = [first(item) for item in items[:ahead]]
    pending = None
    for i, item in enumerate(items):
        if i + ahead < len(items):
            made.append(first(items[i + ahead]))
        middle = second(item, made[i])
        made[i] = None
        if pending is not None:
            third(*pending)
        pending = (item, middle)
    third(*pending)


def attend_kernel(q_ref, k_ref, v_ref, qm_ref, km_ref, mixed_ref, inv_ref, e_ref):
    length = q_ref.shape[0]
    lane = lax.broadcasted_iota(jnp.int32, (length, 128), 1)
    front = lax.broadcasted_iota(jnp.int32, (BLOCK, 128), 1) < HD
    q, k, v = q_ref[...], k_ref[...], v_ref[...]
    ones = jnp.ones((length, 128), bf16)
    operands = []
    for head in range(2):
        own = (lane < HD) if head == 0 else (lane >= HD)
        operands.append(
            (jnp.where(own, q, qm_ref[...]), jnp.where(own, k, km_ref[...]), jnp.where(own, v, ones))
        )
    outs = {}

    def scores(item):
        block, head = item
        low, high = key_range(block)
        qa, ka, _ = operands[head]
        return dot(ka[low:high], qa[block * BLOCK : (block + 1) * BLOCK], NT)

    def softmax(item, values):
        block, head = item
        low, high = key_range(block)
        exps = jnp.exp(values - jnp.max(values, 0, keepdims=True)).astype(bf16)
        for kb in range(low // BLOCK, high // BLOCK):
            e_ref[head, kb, :, (block - kb) * BLOCK : (block - kb + 1) * BLOCK] = exps[
                kb * BLOCK - low : (kb + 1) * BLOCK - low
            ]
        return exps

    def mix(item, exps):
        block, head = item
        low, high = key_range(block)
        outs[head] = dot(exps, operands[head][2][low:high], TN)
        if head == 1:
            rows = slice(block * BLOCK, (block + 1) * BLOCK)
            value = jnp.where(front, outs[0], outs[1])
            total = jnp.where(front, outs[1], outs[0])
            inverse = pltpu.roll(1.0 / total, HD, 1)
            mixed_ref[rows, :] = (value * inverse).astype(bf16)
            inv_ref[rows, :] = inverse

    items = [(block, head) for block in range(length // BLOCK) for head in range(2)]
    pipeline(items, scores, softmax, mix)


def span(length):
    return min(length, MAX_DOC + BLOCK)


def attend(q, k, v, q_marks, k_marks, first, jump):
    length = q.shape[0]
    blocks = length // BLOCK
    column = pl.BlockSpec((length, 128), lambda i: (0, first + jump * i))
    fixed = pl.BlockSpec((length, 128), lambda i: (0, 0))
    part = pl.BlockSpec((length, 128), lambda i: (0, i))
    return pl.pallas_call(
        attend_kernel,
        grid=(2,),
        in_specs=[column, column, column, fixed, fixed],
        out_specs=[part, part, pl.BlockSpec((2, blocks, BLOCK, span(length)), lambda i: (i, 0, 0, 0))],
        out_shape=[
            jax.ShapeDtypeStruct((length, 256), bf16),
            jax.ShapeDtypeStruct((length, 256), f32),
            jax.ShapeDtypeStruct((4, blocks, BLOCK, span(length)), bf16),
        ],
        compiler_params=params(),
        cost_estimate=cost(10 * length * length * 256, 30 * length * 256, 4 * length * length),
        name="attend",
    )(q, k, v, q_marks, k_marks)


def attend_back_kernel(
    q_ref, k_ref, v_ref, mixed_ref, inv_ref, e_ref, grad_ref, cos_ref, sin_ref,
    dq_ref, dk_ref, dv_ref, ds_ref,
):
    length = q_ref.shape[0]
    count = length // BLOCK
    lane = lax.broadcasted_iota(jnp.int32, (length, 128), 1)
    q, k, v = q_ref[...], k_ref[...], v_ref[...]
    zero = jnp.zeros((length, 128), bf16)
    scaled = grad_ref[...].astype(f32) * inv_ref[...]
    inner = scaled * mixed_ref[...].astype(f32)
    operands = []
    for head in range(2):
        own = (lane < HD) if head == 0 else (lane >= HD)
        first = HD if head == 0 else 0
        spare = (lane == first) | (lane == first + 1)
        minus = jnp.where(spare, -1.0, 0.0).astype(bf16)
        delta = jnp.sum(jnp.where(own, inner, 0.0), 1, keepdims=True)
        upper = delta.astype(bf16).astype(f32)
        masked = jnp.where(own, scaled, 0.0)
        joined = jnp.where(lane == first, upper, masked)
        joined = jnp.where(lane == first + 1, delta - upper, joined).astype(bf16)
        operands.append(
            (
                jnp.where(own, q, zero),
                jnp.where(own, k, zero),
                jnp.where(own, v, minus),
                masked.astype(bf16),
                joined,
            )
        )
    sums = {}

    def turn_back(value, rows):
        return (value * cos_ref[rows, :] - swap_halves(value) * sin_ref[rows, :]).astype(bf16)

    def slopes(item):
        block, head = item
        low, high = key_range(block)
        return dot(
            operands[head][2][low:high], operands[head][4][block * BLOCK : (block + 1) * BLOCK], NT
        )

    def products(item, slope):
        block, head = item
        low, high = key_range(block)
        parts = []
        for kb in range(low // BLOCK, high // BLOCK):
            cols = slice((block - kb) * BLOCK, (block - kb + 1) * BLOCK)
            part = e_ref[head, kb, :, cols].astype(f32) * slope[kb * BLOCK - low : (kb + 1) * BLOCK - low]
            part = part.astype(bf16)
            ds_ref[head, kb, :, cols] = part
            parts.append(part)
        return jnp.concatenate(parts, 0)

    def finish(item, ds):
        block, head = item
        low, high = key_range(block)
        rows = slice(block * BLOCK, (block + 1) * BLOCK)
        part = dot(ds, operands[head][1][low:high], TN)
        if head == 0:
            sums["q"] = part
        else:
            dq_ref[rows, :] = turn_back((sums["q"] + part) * (HD**-0.5), rows)
        for kb in range(count):
            if max(b for b in range(count) if key_range(b)[0] <= kb * BLOCK) != block:
                continue
            width = (block - kb + 1) * BLOCK
            seen = slice(kb * BLOCK, kb * BLOCK + width)
            keys = slice(kb * BLOCK, (kb + 1) * BLOCK)
            dv = dot(e_ref[head, kb, :, 0:width], operands[head][3][seen])
            dk = dot(ds_ref[head, kb, :, 0:width], operands[head][0][seen])
            if head == 0:
                sums[kb] = (dv, dk)
            else:
                dv_ref[keys, :] = (sums[kb][0] + dv).astype(bf16)
                dk_ref[keys, :] = turn_back(sums[kb][1] + dk, keys)

    items = [(block, head) for block in range(count) for head in range(2)]
    pipeline(items, slopes, products, finish)


def attend_back(q, k, v, mixed, inv, exps, grad, cosine, sine, first, jump):
    length = q.shape[0]
    column = pl.BlockSpec((length, 128), lambda i: (0, first + jump * i))
    part = pl.BlockSpec((length, 128), lambda i: (0, i))
    fixed = pl.BlockSpec((length, 128), lambda i: (0, 0))
    shape = jax.ShapeDtypeStruct((length, 256), bf16)
    return pl.pallas_call(
        attend_back_kernel,
        grid=(2,),
        in_specs=[column] * 3
        + [part, part, pl.BlockSpec((2,) + exps.shape[1:], lambda i: (i, 0, 0, 0)), column, fixed, fixed],
        out_specs=[part] * 3,
        out_shape=[shape] * 3,
        scratch_shapes=[pltpu.VMEM((2,) + exps.shape[1:], bf16)],
        compiler_params=params(),
        cost_estimate=cost(20 * length * length * 256, 36 * length * 256),
        name="attend_back",
    )(q, k, v, mixed, inv, exps, grad, cosine, sine)


def ffn_kernel(tab_ref, *refs, n_pieces, halves):
    pieces, x_ref, mixed_refs = refs[:n_pieces], refs[n_pieces], refs[n_pieces + 1 : n_pieces + 4]
    middle_ref, normed_ref, hidden_ref, slope_g_ref, slope_u_ref, w_out, w_in, sem = refs[n_pieces + 4 :]
    width = x_ref.shape[1] // halves
    inner = hidden_ref.shape[1] // halves
    early = weight_copies(pieces, tab_ref, w_out, sem.at[0], 0, width)
    late = weight_copies(pieces, tab_ref, w_in, sem.at[1], width, 2 * inner)

    @pl.when(pl.program_id(0) == 0)
    def _():
        start_all(early)
        start_all(late)
        wait_all(early)

    middle = x_ref[...].astype(f32) + dot(in_order(mixed_refs), w_out[...])
    middle_ref[...] = middle
    normed = (middle * lax.rsqrt(jnp.mean(middle * middle, -1, keepdims=True) + epsilon)).astype(bf16)
    normed_ref[...] = normed

    @pl.when(pl.program_id(0) == 0)
    def _():
        wait_all(late)

    step = min(512, inner)
    for h in range(halves):
        for c in range(0, inner, step):
            first = 2 * h * inner + c
            gate = dot(normed, w_in[:, first : first + step])
            up = dot(normed, w_in[:, first + inner : first + inner + step])
            sigmoid = jax.nn.sigmoid(gate)
            silu = gate * sigmoid
            cols = slice(h * inner + c, h * inner + c + step)
            hidden_ref[:, cols] = (silu * up).astype(bf16)
            slope_u_ref[:, cols] = silu.astype(bf16)
            slope_g_ref[:, cols] = (up * sigmoid * (1.0 + gate * (1.0 - sigmoid))).astype(bf16)


def ffn(tab, pieces, x, mixed, inner, halves):
    length, width = x.shape
    rows = BLOCK
    n = len(pieces)
    blocks = sum(p.shape[0] for p in pieces)
    narrow = pl.BlockSpec((rows, width), lambda i, t: (i, 0))
    third = pl.BlockSpec((rows, width // 3), lambda i, t: (i, 0))
    wide = pl.BlockSpec((rows, inner), lambda i, t: (i, 0))
    wide_shape = jax.ShapeDtypeStruct((length, inner), bf16)
    return pl.pallas_call(
        functools.partial(ffn_kernel, n_pieces=n, halves=halves),
        grid_spec=pltpu.PrefetchScalarGridSpec(
            num_scalar_prefetch=1,
            grid=(length // rows,),
            in_specs=[ANY] * n + [narrow] + [third] * 3,
            out_specs=[narrow, narrow, wide, wide, wide],
            scratch_shapes=[
                pltpu.VMEM((width, width), bf16),
                pltpu.VMEM((width, 2 * inner), bf16),
                pltpu.SemaphoreType.DMA((2, blocks)),
            ],
        ),
        out_shape=[
            jax.ShapeDtypeStruct((length, width), f32),
            jax.ShapeDtypeStruct((length, width), bf16),
            wide_shape,
            wide_shape,
            wide_shape,
        ],
        compiler_params=params(),
        cost_estimate=cost(2 * length * width * (width + 2 * inner), 8 * width * inner + 8 * length * inner),
        name="ffn",
    )(tab, *pieces, x, *mixed)


def hidden_back_kernel(tab_ref, *refs, n_pieces, halves):
    pieces = refs[:n_pieces]
    middle_ref, hidden_ref, slope_g_ref, slope_u_ref, cot_ref = refs[n_pieces : n_pieces + 5]
    output_ref, gg_ref, gu_ref, weight, sem = refs[n_pieces + 5 :]

    @pl.when(pl.program_id(0) == 0)
    def _():
        load_weight(pieces, tab_ref, weight, sem)

    inner = hidden_ref.shape[1]
    step = min(512, inner)
    cot = cot_ref[...]
    for c in range(0, inner, step):
        cols = slice(c, c + step)
        grad_hidden = dot(cot, weight[cols, :], NT)
        gg_ref[:, cols] = (grad_hidden * slope_g_ref[:, cols].astype(f32)).astype(bf16)
        gu_ref[:, cols] = (grad_hidden * slope_u_ref[:, cols].astype(f32)).astype(bf16)
    output_ref[...] = (middle_ref[...] + dot(hidden_ref[...], weight[...])).astype(bf16)


def hidden_back(tab, pieces, middle, hidden, slope_g, slope_u, cot, halves):
    length, width = middle.shape
    inner = hidden.shape[1]
    rows = BLOCK
    n = len(pieces)
    narrow = pl.BlockSpec((rows, width), lambda i, t: (i, 0))
    wide = pl.BlockSpec((rows, inner), lambda i, t: (i, 0))
    wide_low = jax.ShapeDtypeStruct((length, inner), bf16)
    return pl.pallas_call(
        functools.partial(hidden_back_kernel, n_pieces=n, halves=halves),
        grid_spec=pltpu.PrefetchScalarGridSpec(
            num_scalar_prefetch=1,
            grid=(length // rows,),
            in_specs=[ANY] * n + [narrow, wide, wide, wide, narrow],
            out_specs=[narrow, wide, wide],
            scratch_shapes=[
                pltpu.VMEM((inner, width), bf16),
                pltpu.SemaphoreType.DMA((sum(p.shape[0] for p in pieces),)),
            ],
        ),
        out_shape=[jax.ShapeDtypeStruct((length, width), bf16), wide_low, wide_low],
        compiler_params=params(),
        cost_estimate=cost(4 * length * width * inner, 2 * width * inner + 12 * length * inner),
        name="hidden_back",
    )(tab, *pieces, middle, hidden, slope_g, slope_u, cot)


def middle_back_kernel(tab_ref, *refs, n_pieces, halves):
    pieces = refs[:n_pieces]
    middle_ref, gg_ref, gu_ref, cot_ref = refs[n_pieces : n_pieces + 4]
    grad_middle_ref, attn_grad_ref, grad_mixed_ref, w_out, w_in, sem = refs[n_pieces + 4 :]
    width = cot_ref.shape[1] // halves
    inner = gg_ref.shape[1] // halves
    early = weight_copies(pieces, tab_ref, w_in, sem.at[0], width, 2 * inner)
    late = weight_copies(pieces, tab_ref, w_out, sem.at[1], 0, width)

    @pl.when(pl.program_id(0) == 0)
    def _():
        start_all(early)
        start_all(late)
        wait_all(early)
        wait_all(late)

    middle = middle_ref[...]
    both = [
        ref[:, h * inner : (h + 1) * inner] for h in range(halves) for ref in (gg_ref, gu_ref)
    ]
    grad = dot(jnp.concatenate(both, 1), w_in[...], NT)
    inverse = lax.rsqrt(jnp.mean(middle * middle, -1, keepdims=True) + epsilon)
    normed = middle * inverse
    grad_middle = cot_ref[...].astype(f32) + inverse * (
        grad - normed * jnp.mean(grad * normed, -1, keepdims=True)
    )
    grad_middle_ref[...] = grad_middle
    low = grad_middle.astype(bf16)
    attn_grad_ref[...] = low
    grad_mixed_ref[...] = dot(low, w_out[...], NT).astype(bf16)


def middle_back(tab, pieces, middle, gg, gu, cot, halves):
    length, width = middle.shape
    inner = gg.shape[1]
    rows = BLOCK
    n = len(pieces)
    narrow = pl.BlockSpec((rows, width), lambda i, t: (i, 0))
    wide = pl.BlockSpec((rows, inner), lambda i, t: (i, 0))
    low = jax.ShapeDtypeStruct((length, width), bf16)
    return pl.pallas_call(
        functools.partial(middle_back_kernel, n_pieces=n, halves=halves),
        grid_spec=pltpu.PrefetchScalarGridSpec(
            num_scalar_prefetch=1,
            grid=(length // rows,),
            in_specs=[ANY] * n + [narrow, wide, wide, narrow],
            out_specs=[narrow] * 3,
            scratch_shapes=[
                pltpu.VMEM((width, width), bf16),
                pltpu.VMEM((width, 2 * inner), bf16),
                pltpu.SemaphoreType.DMA((2, sum(p.shape[0] for p in pieces))),
            ],
        ),
        out_shape=[jax.ShapeDtypeStruct((length, width), f32), low, low],
        compiler_params=params(),
        cost_estimate=cost(
            2 * length * width * (width + 2 * inner), 4 * width * inner + 4 * length * inner
        ),
        name="middle_back",
    )(tab, *pieces, middle, gg, gu, cot)


def input_kernel(tab_ref, *refs, n_pieces, halves):
    pieces = refs[:n_pieces]
    x_ref, grad_middle_ref = refs[n_pieces : n_pieces + 2]
    parts = refs[n_pieces + 2 : n_pieces + 2 + 3 * GROUPS]
    out_ref, weight, sem = refs[n_pieces + 2 + 3 * GROUPS :]

    @pl.when(pl.program_id(0) == 0)
    def _():
        load_weight(pieces, tab_ref, weight, sem)

    left = [
        in_order(parts[part * GROUPS : (part + 1) * GROUPS], h, halves)
        for h in range(halves)
        for part in range(3)
    ]
    grad = dot(jnp.concatenate(left, 1), weight[...], NT)
    x = x_ref[...].astype(f32)
    inverse = lax.rsqrt(jnp.mean(x * x, -1, keepdims=True) + epsilon)
    normed = x * inverse
    out_ref[...] = grad_middle_ref[...] + inverse * (
        grad - normed * jnp.mean(grad * normed, -1, keepdims=True)
    )


def input_grad(tab, pieces, x, grad_middle, parts, halves):
    length, width = x.shape
    rows = BLOCK
    n = len(pieces)
    blocks = sum(p.shape[0] for p in pieces)
    block = pl.BlockSpec((rows, width), lambda i, t: (i, 0))
    third = pl.BlockSpec((rows, width // GROUPS), lambda i, t: (i, 0))
    return pl.pallas_call(
        functools.partial(input_kernel, n_pieces=n, halves=halves),
        grid_spec=pltpu.PrefetchScalarGridSpec(
            num_scalar_prefetch=1,
            grid=(length // rows,),
            in_specs=[ANY] * n + [block] * 2 + [third] * (3 * GROUPS),
            out_specs=block,
            scratch_shapes=[
                pltpu.VMEM((width, 3 * width), bf16),
                pltpu.SemaphoreType.DMA((blocks,)),
            ],
        ),
        out_shape=jax.ShapeDtypeStruct((length, width), f32),
        compiler_params=params(),
        cost_estimate=cost(6 * length * width * width, 20 * length * width),
        name="input_grad",
    )(tab, *pieces, x, grad_middle, *parts)


def weight_kernel(tab_ref, *refs, counts, block_rows, chunks):
    n_left, n_right = sum(n for n, _ in counts), sum(n for _, n in counts)
    lefts, rights = list(refs[:n_left]), list(refs[n_left : n_left + n_right])
    keep_ref, send_ref, held, sem = refs[n_left + n_right :]
    step, steps = pl.program_id(0), pl.num_programs(0)
    slot = lax.rem(step, 2)
    half, chunk = step // chunks, lax.rem(step, chunks)
    halves = tab_ref.shape[0] * block_rows // held.shape[1]
    kept = keep_ref.shape[0]
    widths = [r.shape[1] for r in rights]
    if chunks == 1:
        widths = [sum(widths)]

    def pieces():
        for b in range(held.shape[1] // block_rows):
            offset = 0
            for i, width in enumerate(widths):
                yield b, i, offset, width
                offset += width

    def wait(which):
        for b, i, offset, width in pieces():
            pltpu.make_async_copy(
                held.at[which, pl.ds(0, block_rows), pl.ds(offset, width)],
                keep_ref.at[0, :, pl.ds(offset, width)],
                sem.at[which, b * len(widths) + i],
            ).wait()

    @pl.when(step >= 2)
    def _():
        wait(slot)

    offset = 0
    queue = list(rights)
    for n_left, n_right in counts:
        left = lefts.pop(0)[...] if n_left == 1 else in_order([lefts.pop(0) for _ in range(n_left)])
        right = jnp.concatenate([queue.pop(0)[...] for _ in range(n_right)], 1)
        held[slot, :, offset : offset + right.shape[1]] = dot(left, right, TN).astype(bf16)
        offset += right.shape[1]
    for b, i, offset, width in pieces():
        place = tab_ref[b * halves + half]
        source = held.at[slot, pl.ds(b * block_rows, block_rows), pl.ds(offset, width)]
        cols = pl.ds(pl.multiple_of(offset * chunks + chunk * width, 128), width)
        signal = sem.at[slot, b * len(widths) + i]

        @pl.when(place < kept)
        def _():
            pltpu.make_async_copy(source, keep_ref.at[place, :, cols], signal).start()

        @pl.when(place >= kept)
        def _():
            pltpu.make_async_copy(source, send_ref.at[place - kept, :, cols], signal).start()

    @pl.when(step == steps - 1)
    def _():
        wait(slot)

        @pl.when(steps > 1)
        def _():
            wait(1 - slot)


def weight_grad(moves, products, chunks, name):
    lefts = [left for group, _ in products for left in group]
    rights = [right for _, group in products for right in group]
    counts = [(len(left), len(right)) for left, right in products]
    length, rows = lefts[0].shape
    halves, blocks = moves.halves, moves.place.shape[0]
    block_rows = rows * halves // blocks
    columns = sum(r.shape[1] for r in rights) // halves
    kept = moves.kept
    sent = max(1, blocks - kept)
    steps = halves * chunks
    n_pieces = rows // block_rows * (1 if chunks == 1 else len(rights))
    return pl.pallas_call(
        functools.partial(weight_kernel, counts=counts, block_rows=block_rows, chunks=chunks),
        grid_spec=pltpu.PrefetchScalarGridSpec(
            num_scalar_prefetch=1,
            grid=(steps,),
            in_specs=[pl.BlockSpec(left.shape, lambda i, t: (0, 0)) for left in lefts]
            + [pl.BlockSpec((length, r.shape[1] // steps), lambda i, t: (0, i)) for r in rights],
            out_specs=[ANY, ANY],
            scratch_shapes=[
                pltpu.VMEM((2, rows, columns // chunks), bf16),
                pltpu.SemaphoreType.DMA((2, n_pieces)),
            ],
        ),
        out_shape=[
            jax.ShapeDtypeStruct((kept, block_rows, columns), bf16),
            jax.ShapeDtypeStruct((sent, block_rows, columns), bf16),
        ],
        compiler_params=params(),
        cost_estimate=cost(
            2 * length * rows * columns * halves,
            2 * (length * rows + length * columns * halves + rows * columns * halves),
        ),
        name=name,
    )(moves.place, *lefts, *rights)


def after(value, *others):
    return lax.optimization_barrier((value, others))[0]


def place_of(xr, yr, zr, cr):
    low = xr * 4 + yr * 2 + zr
    high = 8 + yr * 4 + xr * 2 + (zr - 2)
    return cr * 16 + jnp.where(zr < 2, low, high)


def swapped(bits, axis="shard"):
    count = lax.axis_size(axis)
    pairs = [(i, i ^ bits) for i in range(count)]
    return lambda array: lax.ppermute(array, axis, pairs)


class Direct:
    halves = 2
    kept = 16

    def __init__(self):
        self.me = lax.axis_index("shard")
        self.x = lax.axis_index("rep")
        self.core, self.y, self.x_move = swapped(1), swapped(2), swapped(1, "rep")
        self.z = [swapped(4), swapped(8), swapped(12)]
        shard = jnp.arange(16, dtype=jnp.int32)[:, None]
        half = jnp.arange(2, dtype=jnp.int32)[None, :]
        rel = shard ^ self.me
        place = place_of(half ^ self.x, (rel >> 1) & 1, rel >> 2, rel & 1)
        self.place = place.reshape(32)
        order = []
        for cr in range(2):
            for zs in ((0, 1), (2, 3)):
                for outer in range(2):
                    for inner in range(2):
                        for zr in zs:
                            xr, yr = (outer, inner) if zs[0] == 0 else (inner, outer)
                            order.append((zr * 4 + yr * 2 + cr, xr))
        rel_shard = jnp.array([o[0] for o in order], jnp.int32)
        rel_half = jnp.array([o[1] for o in order], jnp.int32)
        self.tab = jnp.stack([rel_shard ^ self.me, rel_half ^ self.x])

    def pack(self, arrays, gain):
        return pack(self.x, arrays, gain, 2)

    def along_z(self, own):
        z1, z2, z3 = (move(own) for move in self.z)
        return jnp.concatenate([own, z1], 0), jnp.concatenate([z2, z3], 0), (z1, z2, z3)

    def one_axis(self, a, b):
        ay, bx = self.y(a), self.x_move(b)
        return (a, ay), (b, bx)

    def rest(self, a, b):
        ax, by = self.x_move(a), self.y(b)
        return [a, ax, b, by]

    def with_core(self, own, *deps):
        own = [after(p, *deps) for p in own] if deps else own
        return own + [self.core(p) for p in own]

    def gather(self, blocks):
        first, second, third = (block[None] for block in blocks)
        a1, b1, z_done1 = self.along_z(first)
        a2, b2, z_done2 = self.along_z(after(second, *z_done1))
        a1, b1 = self.one_axis(a1, b1)
        a1, b1 = jnp.concatenate(a1, 0), jnp.concatenate(b1, 0)
        own1 = self.rest(a1, b1)
        w1 = self.with_core(own1)
        self.a2, self.b2 = after(a2, *own1), after(b2, *own1)
        self.third = after(third, *z_done2, *own1)
        return w1

    def stage0(self):
        self.pair2 = self.one_axis(self.a2, self.b2)
        self.z3 = self.z[0](self.third)
        return self.a2, self.b2, self.third

    def stage1(self, *deps):
        (a, ay), (b, bx) = self.pair2
        deps = (*deps, self.z3, ay, bx)
        a = jnp.concatenate([after(a, *deps), ay], 0)
        b = jnp.concatenate([after(b, *deps), bx], 0)
        a3 = jnp.concatenate([after(self.third, *deps), self.z3], 0)
        self.a3, self.b3 = a3, self.z[1](a3)
        self.own2 = self.rest(a, b)
        self.core2 = [self.core(a), None, self.core(b), None]
        return a, b, a3

    def stage2(self, *deps):
        deps = (*deps, self.b3, self.core2[0], self.core2[2])
        self.a3, self.b3 = after(self.a3, *deps), after(self.b3, *deps)
        self.pair3 = self.one_axis(self.a3, self.b3)
        return self.a3, self.b3

    def stage3(self, *deps):
        (a, ay), (b, bx) = self.pair3
        deps = (*deps, *self.own2, ay, bx)
        a = jnp.concatenate([after(a, *deps), ay], 0)
        b = jnp.concatenate([after(b, *deps), bx], 0)
        self.own3 = self.rest(a, b)
        for i in (1, 3):
            self.core2[i] = self.core(after(self.own2[i], *deps, a, b))
        self.own2 += self.core2
        return a, b

    def scatter(self, grads, direct=False):
        return Direct.Sum(self, grads, direct)

    class Sum:
        def __init__(self, moves, grads, direct):
            self.moves = moves
            self.keep, self.send = grads
            over_z = [self.over_z] if direct else [self.over_z2, self.over_z1]
            self.steps = [self.over_core, self.over_two, self.over_other, *over_z, self.over_x]
            self.start = self.steps[0]
            self.got = ()

        def step(self, *deps):
            if deps:
                self.keep = after(self.keep, *deps)
                if self.steps[0] == self.start:
                    self.send = after(self.send, *deps)
            return self.steps.pop(0)()

        def finish(self):
            while self.steps:
                self.step()
            return self.result

        @staticmethod
        def add(*terms):
            total = terms[0].astype(f32)
            for term in terms[1:]:
                total = total + term.astype(f32)
            return total.astype(bf16)

        def over_core(self):
            self.core = self.moves.core(self.send)
            self.got = (self.core,)
            return (self.send,)

        def over_two(self):
            keep, core = self.keep, self.core
            to_x, to_y = self.add(keep[4:8], core[4:8]), self.add(keep[12:16], core[12:16])
            self.ax, self.by = self.got = self.moves.x_move(to_x), self.moves.y(to_y)
            return to_x, to_y

        def over_other(self):
            keep, core, ax, by = self.keep, self.core, self.ax, self.by
            to_y = self.add(keep[2:4], core[2:4], ax[2:4])
            to_x = self.add(keep[10:12], core[10:12], by[2:4])
            self.ay, self.bx = self.got = self.moves.y(to_y), self.moves.x_move(to_x)
            return to_y, to_x

        def over_z(self):
            keep, core, ax, by, ay, bx = self.keep, self.core, self.ax, self.by, self.ay, self.bx
            sends = (
                self.add(keep[1], core[1], ax[1], ay[1]),
                self.add(keep[8], core[8], by[0], bx[0]),
                self.add(keep[9], core[9], by[1], bx[1]),
            )
            self.got = self.zs = tuple(move(send) for move, send in zip(self.moves.z, sends))
            return sends

        def over_z2(self):
            keep, core = self.keep, self.core
            send = self.add(keep[8:10], core[8:10], self.by[0:2], self.bx[0:2])
            self.z2 = self.moves.z[1](send)
            self.got = (self.z2,)
            return (send,)

        def over_z1(self):
            send = self.add(self.keep[1], self.core[1], self.ax[1], self.ay[1], self.z2[1])
            z1 = self.moves.z[0](send)
            self.zs = (self.z2[0], z1)
            self.got = (z1,)
            return (send,)

        def over_x(self):
            own = self.add(self.keep[0], self.core[0], self.ax[0], self.ay[0], *self.zs)
            other = self.moves.x_move(own)
            first = self.moves.x == 0
            self.result = [jnp.where(first, own, other), jnp.where(first, other, own)]
            self.got = (other,)
            return (own,)


class Plain:
    halves = 1
    kept = 1

    def __init__(self):
        self.place = jnp.zeros((1,), jnp.int32)
        self.tab = jnp.zeros((2, 1), jnp.int32)

    def pack(self, arrays, gain):
        return pack(jnp.int32(0), arrays, gain, 1)

    def gather(self, blocks):
        first, *others = (
            [lax.all_gather(block, "shard", axis=0, tiled=True)[None]] for block in blocks
        )
        self.own2, self.own3 = others
        return first

    def with_core(self, own, *deps):
        return own

    def stage0(self):
        return ()

    def stage1(self, *deps):
        return ()

    stage2 = stage3 = stage1

    def scatter(self, grads, direct=False):
        return Plain.Sum(grads)

    class Sum:
        got = ()

        def __init__(self, grads):
            self.grads = grads

        def step(self, *deps):
            return ()

        def finish(self):
            total = self.grads[0][0].astype(f32)
            part = lax.psum_scatter(total, "shard", scatter_dimension=0, tiled=True)
            return [lax.psum(part.astype(bf16), "rep")]


def columns(halves, start, width):
    step = width // len(halves)
    first = start // len(halves)
    return jnp.concatenate([h[:, first : first + step] for h in halves], 1).astype(f32)


def one_sequence(moves, x, docs, w1, cot, inner):
    cosine, sine = rope_tables(x.shape[0])
    q_marks, k_marks = marks(docs.reshape(-1, 1))
    halves, tab = moves.halves, moves.tab
    sends = moves.stage0()
    normed1, q, k, v = project(tab, w1, after(x, *sends), cosine, sine, halves)
    sends = moves.stage1(normed1)
    seen = []
    for g in range(GROUPS):
        seen.append(attend(q, k, v, after(q_marks, *sends), k_marks, g, GROUPS))
        sends = (seen[-1][0],)
        if g == 1:
            sends = moves.stage2(*sends)
    mixed = [s[0] for s in seen]
    sends = moves.stage3(mixed[2])
    w2 = moves.own2
    middle, normed2, hidden, slope_g, slope_u = ffn(
        tab, w2, after(x, *sends), mixed, inner, halves
    )
    w3 = moves.with_core(moves.own3, hidden)
    g3 = weight_grad(moves, [([after(hidden, *moves.own3)], [cot])], 1, "grad_down")
    sum3 = moves.scatter(g3)
    sum3.step(*g3, *w3)
    output, gg, gu = hidden_back(
        tab, w3, middle, after(hidden, *g3), slope_g, slope_u, cot, halves
    )
    sends = sum3.step(gg, *sum3.got)
    g2 = weight_grad(moves, [([after(normed2, *sends)], [gg, gu])], 2, "grad_gate_up")
    sum2 = moves.scatter(g2)
    due = (*g2, *sum3.got)
    sends = sum3.step(*due)
    sends = (*sends, *sum2.step(*due))
    grad_middle, attn_grad, grad_mixed = middle_back(
        tab, w2, after(middle, *g2, *sends), gg, gu, cot, halves
    )
    due = (attn_grad, *sum3.got, *sum2.got)
    sends = sum3.step(*due)
    sends = (*sends, *sum2.step(*due))

    def back(g, sends):
        return attend_back(q, k, v, *seen[g], after(grad_mixed, *sends), cosine, sine, g, GROUPS)

    turned0 = back(0, sends)
    sends = sum3.step(*turned0[:1], *sum3.got)
    turned1 = back(1, (*turned0[:1], *sends))
    due = (*turned1[:1], *sum2.got, *sum3.got)
    sends = sum2.step(*due)
    sends = (*sends, *sum3.step(*due))
    g1 = weight_grad(
        moves,
        [([after(normed1, *sends)], [*turned0, *turned1]), (mixed, [attn_grad])],
        1,
        "grad_qk_out",
    )
    sum1 = moves.scatter(g1)
    due = (*g1, *sum2.got, *sum3.got)
    sum1.step(*due)
    sends = sum2.step(*due)
    sends = (*sends, *sum1.step(*sends, *sum1.got))
    turned2 = back(2, (*g1, *sends))
    due = (*turned2[:1], *sum1.got, *sum2.got)
    sends = sum1.step(*due)
    sends = (*sends, *sum2.step(*due))
    g0 = weight_grad(moves, [([after(normed1, *sends)], turned2)], 1, "grad_qkv_rest")
    sum0 = moves.scatter(g0, True)
    due = (*g0, *sum1.got, *sum2.got)
    sum0.step(*due)
    sends = (*sum1.step(*due), *sum2.step(*due))
    sends = (*sends, *sum0.step(*sends, *sum0.got))
    parts = [t[part] for part in range(3) for t in (turned0, turned1, turned2)]
    grad_input = input_grad(tab, w1, after(x, *g0, *sends), grad_middle, parts, halves)
    sums = (sum0, sum1, sum2, sum3)
    due = (grad_input, *sum2.got, *sum1.got, *sum0.got)
    for one in (sum0, sum1):
        one.step(*due)
    return output, grad_input, [s.finish() for s in sums]


def per_device(
    inputs,
    doc_ids,
    attn_gain,
    w_query,
    w_key,
    w_value,
    w_out,
    ffn_gain,
    w_gate,
    w_up,
    w_down,
    cotangent,
):
    batch_size, length, width = inputs.shape
    inner = w_gate.shape[1]
    replicas, members = lax.axis_size("rep"), lax.axis_size("shard")
    moves = Direct() if (replicas, members, batch_size) == (2, 16, 1) else Plain()
    gain1 = attn_gain.astype(f32)[:, None]
    gain2 = ffn_gain.astype(f32)[:, None]

    w1 = moves.gather(
        [
            moves.pack([(w, True) for w in (w_query, w_key, w_value)], gain1),
            moves.pack([(w_out, False), (w_gate, True), (w_up, True)], gain2),
            moves.pack([(w_down, False)], jnp.ones((w_down.shape[0], 1), f32)),
        ]
    )
    outputs, grad_inputs, sums = [], [], None
    for b in range(batch_size):
        output, grad_input, own = one_sequence(
            moves, inputs[b], doc_ids[b], w1, cotangent[b], inner
        )
        outputs.append(output)
        grad_inputs.append(grad_input)
        sums = own if sums is None else jax.tree.map(jnp.add, sums, own)
    s0, s1, s2, s3 = sums
    scale = 1.0 / (batch_size * replicas * members)
    down = columns(s3, 0, width)
    gate, up = columns(s2, 0, inner), columns(s2, inner, inner)
    third = width // GROUPS
    out = columns(s1, 6 * third, width)

    def head_columns(part):
        sources = [columns(s, start * third, third) for s, start in ((s1, part), (s1, part + 3), (s0, part))]
        return jnp.concatenate([c[:, j * 128 : (j + 1) * 128] for j in range(2) for c in sources], 1)

    query, key, value = (head_columns(part) for part in range(3))

    def gain_grad(pairs):
        total = sum(jnp.sum(w.astype(f32) * g, 1) for w, g in pairs)
        return total * scale

    return (
        jnp.stack(outputs),
        jnp.stack(grad_inputs),
        gain_grad([(w_query, query), (w_key, key), (w_value, value)]),
        query * gain1 * scale,
        key * gain1 * scale,
        value * gain1 * scale,
        out * scale,
        gain_grad([(w_gate, gate), (w_up, up)]),
        gate * gain2 * scale,
        up * gain2 * scale,
        down * scale,
    )


def solution(mesh):
    row = P("shard", None)
    tokens = P(("rep", "shard"), None, None)
    return jax.shard_map(
        per_device,
        mesh=mesh,
        in_specs=(
            tokens, P(("rep", "shard"), None), P("shard"), row, row, row, row, P("shard"), row, row, row, tokens,
        ),
        out_specs=(tokens, tokens, P("shard"), row, row, row, row, P("shard"), row, row, row),
        check_vma=False,
    )
```

```python
import functools

import jax
import jax.numpy as jnp
import numpy as np
from jax import lax
from jax.experimental import pallas as pl
from jax.experimental.pallas import tpu as pltpu
from jax.sharding import PartitionSpec as P

H = 12
HD = 64
BLOCK = 256
MAX_DOC = 512

epsilon = 1e-06
rope_base = 10000.0
far = 1e30

bf16 = jnp.bfloat16
f32 = jnp.float32
MIB = 1 << 20
NN = (((1,), (0,)), ((), ()))
NT = (((1,), (1,)), ((), ()))
TN = (((0,), (0,)), ((), ()))


def dot(left, right, dims=NN):
    return lax.dot_general(left, right, dims, preferred_element_type=f32)


def params():
    return pltpu.CompilerParams(vmem_limit_bytes=60 * MIB)


HINT = 1.0


def cost(flops, nbytes, trans=0):
    return pl.CostEstimate(
        flops=int(HINT * flops), bytes_accessed=int(HINT * nbytes), transcendentals=int(HINT * trans)
    )


ANY = pl.BlockSpec(memory_space=pl.ANY)


class WeightCopies:
    def __init__(self, pieces, tab_ref, dest, sem, start, width):
        self.pieces, self.tab, self.dest, self.sem = pieces, tab_ref, dest, sem
        self.start_col, self.width = start, width

    def each(self, act):
        for number, piece in enumerate(self.pieces):
            count, rows = piece.shape[0], piece.shape[1]

            def step(b, carry):
                index = number * count + b
                row = pl.multiple_of(self.tab[0, index] * rows, 16)
                col = pl.multiple_of(self.tab[1, index] * self.width, 128)
                act(
                    pltpu.make_async_copy(
                        piece.at[b, :, pl.ds(self.start_col, self.width)],
                        self.dest.at[pl.ds(row, rows), pl.ds(col, self.width)],
                        self.sem.at[index],
                    )
                )
                return carry

            lax.fori_loop(0, count, step, 0)

    def start(self):
        self.each(lambda copy: copy.start())

    def wait(self):
        self.each(lambda copy: copy.wait())


def load_weight(pieces, tab_ref, dest, sem):
    copies = WeightCopies(pieces, tab_ref, dest, sem, 0, pieces[0].shape[2])
    copies.start()
    copies.wait()


SPLIT = (2, 1)


def in_order(refs, half=0, halves=1):
    return jnp.concatenate(
        [
            ref[:, j * (ref.shape[1] // 2) : (j + 1) * (ref.shape[1] // 2)]
            for j in range(2)
            if j * halves // 2 == half
            for ref in refs
        ],
        1,
    )


def pair_of(call):
    first, count = sum(SPLIT[:call]), SPLIT[call]
    return lambda i: (0, first + i % count + sum(SPLIT) * (i // count))


def pack_kernel(half_ref, *refs, folded):
    *sources, gain_ref, out_ref = refs
    offset = 0
    for source, scaled in zip(sources, folded):
        width = source.shape[1]
        value = source[...]
        if scaled:
            value = (value.astype(f32) * gain_ref[...]).astype(bf16)
        out_ref[:, offset : offset + width] = value
        offset += width


def pack(half, arrays, gain, halves):
    folded = [scaled for _, scaled in arrays]
    arrays = [array for array, _ in arrays]
    rows = arrays[0].shape[0]
    columns = sum(array.shape[1] for array in arrays) // halves
    return pl.pallas_call(
        functools.partial(pack_kernel, folded=folded),
        grid_spec=pltpu.PrefetchScalarGridSpec(
            num_scalar_prefetch=1,
            grid=(1,),
            in_specs=[
                pl.BlockSpec((rows, array.shape[1] // halves), lambda i, h: (0, h[0])) for array in arrays
            ]
            + [pl.BlockSpec((rows, 1), lambda i, h: (0, 0))],
            out_specs=pl.BlockSpec((rows, columns), lambda i, h: (0, 0)),
        ),
        out_shape=jax.ShapeDtypeStruct((rows, columns), bf16),
        compiler_params=params(),
        cost_estimate=cost(rows * columns, 4 * rows * columns),
        name="pack",
    )(half.reshape(1), *arrays, gain)


def rope_tables(length):
    frequency = rope_base ** -(np.arange(HD // 2) * (2.0 / HD))
    coarse = np.arange(length // 32)[:, None] * 32.0 * frequency[None, :]
    fine = np.arange(32)[:, None] * frequency[None, :]
    coarse, fine = np.tile(coarse, (1, 4))[:, None, :], np.tile(fine, (1, 4))[None, :, :]
    sign = np.tile(np.repeat([-1.0, 1.0], HD // 2), 2)
    cos_a, sin_a = jnp.asarray(np.cos(coarse), f32), jnp.asarray(np.sin(coarse), f32)
    cos_b, sin_b = jnp.asarray(np.cos(fine), f32), jnp.asarray(np.sin(fine), f32)
    cosine = cos_a * cos_b - sin_a * sin_b
    sine = (sin_a * cos_b + cos_a * sin_b) * jnp.asarray(sign, f32)
    return cosine.reshape(length, 128), sine.reshape(length, 128)


def swap_halves(tensor):
    lane = lax.broadcasted_iota(jnp.int32, tensor.shape, 1)
    return jnp.where(
        (lane & (HD // 2)) == 0, pltpu.roll(tensor, 128 - HD // 2, 1), pltpu.roll(tensor, HD // 2, 1)
    )


def project_kernel(tab_ref, *refs, n_pieces, halves):
    pieces, (x_ref, cos_ref, sin_ref) = refs[:n_pieces], refs[n_pieces : n_pieces + 3]
    n_ref, q_ref, k_ref, v_ref, weight, sem = refs[n_pieces + 3 :]

    @pl.when(pl.program_id(0) == 0)
    def _():
        load_weight(pieces, tab_ref, weight, sem)

    x = x_ref[...].astype(f32)
    normed = (x * lax.rsqrt(jnp.mean(x * x, -1, keepdims=True) + epsilon)).astype(bf16)
    n_ref[...] = normed
    width = x_ref.shape[1] // halves
    cosine, sine = cos_ref[...], sin_ref[...]
    everything = dot(normed, weight[...])
    for half in range(halves):
        result = everything[:, 3 * half * width : 3 * (half + 1) * width]
        for part, out, scale in ((0, q_ref, HD**-0.5), (1, k_ref, 1.0)):
            for c in range(0, width, 128):
                piece = result[:, part * width + c : part * width + c + 128]
                turned = piece * cosine + swap_halves(piece) * sine
                out[:, half * width + c : half * width + c + 128] = (
                    turned.astype(bf16) * jnp.asarray(scale, bf16)
                )
        v_ref[:, half * width : (half + 1) * width] = result[:, 2 * width :].astype(bf16)


def project(tab, pieces, x, cosine, sine, halves):
    length, width = x.shape
    rows = BLOCK
    n = len(pieces)
    blocks = sum(p.shape[0] for p in pieces)
    block = pl.BlockSpec((rows, width), lambda i, t: (i, 0))
    table = pl.BlockSpec((rows, 128), lambda i, t: (i, 0))
    shape = jax.ShapeDtypeStruct((length, width), bf16)
    return pl.pallas_call(
        functools.partial(project_kernel, n_pieces=n, halves=halves),
        grid_spec=pltpu.PrefetchScalarGridSpec(
            num_scalar_prefetch=1,
            grid=(length // rows,),
            in_specs=[ANY] * n + [block, table, table],
            out_specs=[block] * 4,
            scratch_shapes=[
                pltpu.VMEM((width, 3 * width), bf16),
                pltpu.SemaphoreType.DMA((blocks,)),
            ],
        ),
        out_shape=[shape] * 4,
        compiler_params=params(),
        cost_estimate=cost(6 * length * width * width, 16 * length * width),
        name="project",
    )(tab, *pieces, x, cosine, sine)


def key_range(block):
    low = max(0, (block * BLOCK - (MAX_DOC - 1)) // BLOCK) if block * BLOCK > MAX_DOC - 1 else 0
    return low * BLOCK, (block + 1) * BLOCK


def marks(docs):
    lane = jnp.arange(128, dtype=jnp.int32)[None, :] % HD
    used = lane < 4
    same = docs == lane
    return (
        jnp.where(used & ~same, -far, 0.0).astype(bf16),
        jnp.where(used & same, 1.0, 0.0).astype(bf16),
    )


def pipeline(items, first, second, third, ahead=2):
    made = [first(item) for item in items[:ahead]]
    pending = None
    for i, item in enumerate(items):
        if i + ahead < len(items):
            made.append(first(items[i + ahead]))
        middle = second(item, made[i])
        made[i] = None
        if pending is not None:
            third(*pending)
        pending = (item, middle)
    third(*pending)


def attend_kernel(q_ref, k_ref, v_ref, qm_ref, km_ref, mixed_ref, inv_ref, e_ref):
    length = q_ref.shape[0]
    lane = lax.broadcasted_iota(jnp.int32, (length, 128), 1)
    front = lax.broadcasted_iota(jnp.int32, (BLOCK, 128), 1) < HD
    q, k, v = q_ref[...], k_ref[...], v_ref[...]
    ones = jnp.ones((length, 128), bf16)
    operands = []
    for head in range(2):
        own = (lane < HD) if head == 0 else (lane >= HD)
        operands.append(
            (jnp.where(own, q, qm_ref[...]), jnp.where(own, k, km_ref[...]), jnp.where(own, v, ones))
        )
    outs = {}

    def scores(item):
        block, head = item
        low, high = key_range(block)
        qa, ka, _ = operands[head]
        return dot(ka[low:high], qa[block * BLOCK : (block + 1) * BLOCK], NT)

    def softmax(item, values):
        block, head = item
        low, high = key_range(block)
        exps = jnp.exp(values - jnp.max(values, 0, keepdims=True)).astype(bf16)
        for kb in range(low // BLOCK, high // BLOCK):
            e_ref[head, kb, :, (block - kb) * BLOCK : (block - kb + 1) * BLOCK] = exps[
                kb * BLOCK - low : (kb + 1) * BLOCK - low
            ]
        return exps

    def mix(item, exps):
        block, head = item
        low, high = key_range(block)
        outs[head] = dot(exps, operands[head][2][low:high], TN)
        if head == 1:
            rows = slice(block * BLOCK, (block + 1) * BLOCK)
            value = jnp.where(front, outs[0], outs[1])
            total = jnp.where(front, outs[1], outs[0])
            inverse = pltpu.roll(1.0 / total, HD, 1)
            mixed_ref[rows, :] = (value * inverse).astype(bf16)
            inv_ref[rows, :] = inverse

    items = [(block, head) for block in range(length // BLOCK) for head in range(2)]
    pipeline(items, scores, softmax, mix)


def span(length):
    return min(length, MAX_DOC + BLOCK)


def attend(q, k, v, q_marks, k_marks):
    length, width = q.shape
    blocks = length // BLOCK
    pairs = width // 128
    column = pl.BlockSpec((length, 128), lambda i: (0, i))
    fixed = pl.BlockSpec((length, 128), lambda i: (0, 0))
    return pl.pallas_call(
        attend_kernel,
        grid=(pairs,),
        in_specs=[column, column, column, fixed, fixed],
        out_specs=[column, column, pl.BlockSpec((2, blocks, BLOCK, span(length)), lambda i: (i, 0, 0, 0))],
        out_shape=[
            jax.ShapeDtypeStruct((length, 128 * pairs), bf16),
            jax.ShapeDtypeStruct((length, 128 * pairs), f32),
            jax.ShapeDtypeStruct((2 * pairs, blocks, BLOCK, span(length)), bf16),
        ],
        compiler_params=params(),
        cost_estimate=cost(1280 * pairs * length * length, 3840 * pairs * length, 2 * pairs * length * length),
        name="attend",
    )(q, k, v, q_marks, k_marks)


def attend_back_kernel(
    q_ref, k_ref, v_ref, mixed_ref, inv_ref, e_ref, grad_ref, cos_ref, sin_ref,
    dq_ref, dk_ref, dv_ref, ds_ref,
):
    length = q_ref.shape[0]
    count = length // BLOCK
    lane = lax.broadcasted_iota(jnp.int32, (length, 128), 1)
    q, k, v = q_ref[...], k_ref[...], v_ref[...]
    zero = jnp.zeros((length, 128), bf16)
    scaled = grad_ref[...].astype(f32) * inv_ref[...]
    inner = scaled * mixed_ref[...].astype(f32)
    operands = []
    for head in range(2):
        own = (lane < HD) if head == 0 else (lane >= HD)
        first = HD if head == 0 else 0
        spare = (lane == first) | (lane == first + 1)
        minus = jnp.where(spare, -1.0, 0.0).astype(bf16)
        delta = jnp.sum(jnp.where(own, inner, 0.0), 1, keepdims=True)
        upper = delta.astype(bf16).astype(f32)
        masked = jnp.where(own, scaled, 0.0)
        joined = jnp.where(lane == first, upper, masked)
        joined = jnp.where(lane == first + 1, delta - upper, joined).astype(bf16)
        operands.append(
            (
                jnp.where(own, q, zero),
                jnp.where(own, k, zero),
                jnp.where(own, v, minus),
                masked.astype(bf16),
                joined,
            )
        )
    sums = {}

    def turn_back(value, rows):
        return (value * cos_ref[rows, :] - swap_halves(value) * sin_ref[rows, :]).astype(bf16)

    def slopes(item):
        block, head = item
        low, high = key_range(block)
        return dot(
            operands[head][2][low:high], operands[head][4][block * BLOCK : (block + 1) * BLOCK], NT
        )

    def products(item, slope):
        block, head = item
        low, high = key_range(block)
        parts = []
        for kb in range(low // BLOCK, high // BLOCK):
            cols = slice((block - kb) * BLOCK, (block - kb + 1) * BLOCK)
            part = e_ref[head, kb, :, cols].astype(f32) * slope[kb * BLOCK - low : (kb + 1) * BLOCK - low]
            part = part.astype(bf16)
            ds_ref[head, kb, :, cols] = part
            parts.append(part)
        return jnp.concatenate(parts, 0)

    def finish(item, ds):
        block, head = item
        low, high = key_range(block)
        rows = slice(block * BLOCK, (block + 1) * BLOCK)
        part = dot(ds, operands[head][1][low:high], TN)
        if head == 0:
            sums["q"] = part
        else:
            dq_ref[rows, :] = turn_back((sums["q"] + part) * (HD**-0.5), rows)
        for kb in range(count):
            if max(b for b in range(count) if key_range(b)[0] <= kb * BLOCK) != block:
                continue
            width = (block - kb + 1) * BLOCK
            seen = slice(kb * BLOCK, kb * BLOCK + width)
            keys = slice(kb * BLOCK, (kb + 1) * BLOCK)
            dv = dot(e_ref[head, kb, :, 0:width], operands[head][3][seen])
            dk = dot(ds_ref[head, kb, :, 0:width], operands[head][0][seen])
            if head == 0:
                sums[kb] = (dv, dk)
            else:
                dv_ref[keys, :] = (sums[kb][0] + dv).astype(bf16)
                dk_ref[keys, :] = turn_back(sums[kb][1] + dk, keys)

    items = [(block, head) for block in range(count) for head in range(2)]
    pipeline(items, slopes, products, finish)


def attend_back(q, k, v, mixed, inv, exps, grad, cosine, sine, call):
    length = q.shape[0]
    pairs = 2 * SPLIT[call]
    column = pl.BlockSpec((length, 128), pair_of(call))
    part = pl.BlockSpec((length, 128), lambda i: (0, i))
    fixed = pl.BlockSpec((length, 128), lambda i: (0, 0))
    shape = jax.ShapeDtypeStruct((length, 128 * pairs), bf16)
    return pl.pallas_call(
        attend_back_kernel,
        grid=(pairs,),
        in_specs=[column] * 5
        + [
            pl.BlockSpec((2,) + exps.shape[1:], lambda i: (pair_of(call)(i)[1], 0, 0, 0)),
            column,
            fixed,
            fixed,
        ],
        out_specs=[part] * 3,
        out_shape=[shape] * 3,
        scratch_shapes=[pltpu.VMEM((2,) + exps.shape[1:], bf16)],
        compiler_params=params(),
        cost_estimate=cost(2560 * pairs * length * length, 4608 * pairs * length),
        name="attend_back",
    )(q, k, v, mixed, inv, exps, grad, cosine, sine)


def ffn_kernel(tab_ref, *refs, n_pieces, halves):
    pieces, (x_ref, mixed_ref), refs = refs[:n_pieces], refs[n_pieces : n_pieces + 2], refs[n_pieces + 2 :]
    middle_ref, normed_ref, hidden_ref, slope_g_ref, slope_u_ref, w_out, w_in, sem = refs
    width = x_ref.shape[1] // halves
    inner = hidden_ref.shape[1] // halves
    early = WeightCopies(pieces, tab_ref, w_out, sem.at[0], 0, width)
    late = WeightCopies(pieces, tab_ref, w_in, sem.at[1], width, 2 * inner)

    @pl.when(pl.program_id(0) == 0)
    def _():
        early.start()
        late.start()
        early.wait()

    middle = x_ref[...].astype(f32) + dot(mixed_ref[...], w_out[...])
    middle_ref[...] = middle
    normed = (middle * lax.rsqrt(jnp.mean(middle * middle, -1, keepdims=True) + epsilon)).astype(bf16)
    normed_ref[...] = normed

    @pl.when(pl.program_id(0) == 0)
    def _():
        late.wait()

    step = min(256, inner)

    def dots(first):
        return (
            dot(normed, w_in[:, first : first + step]),
            dot(normed, w_in[:, first + inner : first + inner + step]),
        )

    def activate(first, values):
        gate, up = values
        half_tanh = 0.5 * jnp.tanh(0.5 * gate)
        sigmoid = half_tanh + 0.5
        silu = gate * sigmoid
        cols = slice(first - first // (2 * inner) * inner, first - first // (2 * inner) * inner + step)
        hidden_ref[:, cols] = (silu * up).astype(bf16)
        slope_u_ref[:, cols] = silu.astype(bf16)
        slope_g_ref[:, cols] = (up * (sigmoid + silu * (0.5 - half_tanh))).astype(bf16)

    items = [2 * h * inner + c for h in range(halves) for c in range(0, inner, step)]
    pipeline(items, dots, activate, lambda *_: None)


def ffn(tab, pieces, x, mixed, inner, halves):
    length, width = x.shape
    rows = BLOCK
    n = len(pieces)
    blocks = sum(p.shape[0] for p in pieces)
    narrow = pl.BlockSpec((rows, width), lambda i, t: (i, 0))
    wide = pl.BlockSpec((rows, inner), lambda i, t: (i, 0))
    wide_shape = jax.ShapeDtypeStruct((length, inner), bf16)
    return pl.pallas_call(
        functools.partial(ffn_kernel, n_pieces=n, halves=halves),
        grid_spec=pltpu.PrefetchScalarGridSpec(
            num_scalar_prefetch=1,
            grid=(length // rows,),
            in_specs=[ANY] * n + [narrow, narrow],
            out_specs=[narrow, narrow, wide, wide, wide],
            scratch_shapes=[
                pltpu.VMEM((width, width), bf16),
                pltpu.VMEM((width, 2 * inner), bf16),
                pltpu.SemaphoreType.DMA((2, blocks)),
            ],
        ),
        out_shape=[
            jax.ShapeDtypeStruct((length, width), f32),
            jax.ShapeDtypeStruct((length, width), bf16),
            wide_shape,
            wide_shape,
            wide_shape,
        ],
        compiler_params=params(),
        cost_estimate=cost(2 * length * width * (width + 2 * inner), 8 * width * inner + 8 * length * inner),
        name="ffn",
    )(tab, *pieces, x, mixed)


def hidden_back_kernel(tab_ref, *refs, n_pieces, halves):
    pieces = refs[:n_pieces]
    middle_ref, hidden_ref, slope_g_ref, slope_u_ref, cot_ref = refs[n_pieces : n_pieces + 5]
    output_ref, gg_ref, gu_ref, weight, sem = refs[n_pieces + 5 :]

    @pl.when(pl.program_id(0) == 0)
    def _():
        load_weight(pieces, tab_ref, weight, sem)

    inner = hidden_ref.shape[1]
    step = min(512, inner)
    cot = cot_ref[...]
    for c in range(0, inner, step):
        cols = slice(c, c + step)
        grad_hidden = dot(cot, weight[cols, :], NT)
        gg_ref[:, cols] = (grad_hidden * slope_g_ref[:, cols].astype(f32)).astype(bf16)
        gu_ref[:, cols] = (grad_hidden * slope_u_ref[:, cols].astype(f32)).astype(bf16)
    output_ref[...] = (middle_ref[...] + dot(hidden_ref[...], weight[...])).astype(bf16)


def hidden_back(tab, pieces, middle, hidden, slope_g, slope_u, cot, halves):
    length, width = middle.shape
    inner = hidden.shape[1]
    rows = BLOCK
    n = len(pieces)
    narrow = pl.BlockSpec((rows, width), lambda i, t: (i, 0))
    wide = pl.BlockSpec((rows, inner), lambda i, t: (i, 0))
    wide_low = jax.ShapeDtypeStruct((length, inner), bf16)
    return pl.pallas_call(
        functools.partial(hidden_back_kernel, n_pieces=n, halves=halves),
        grid_spec=pltpu.PrefetchScalarGridSpec(
            num_scalar_prefetch=1,
            grid=(length // rows,),
            in_specs=[ANY] * n + [narrow, wide, wide, wide, narrow],
            out_specs=[narrow, wide, wide],
            scratch_shapes=[
                pltpu.VMEM((inner, width), bf16),
                pltpu.SemaphoreType.DMA((sum(p.shape[0] for p in pieces),)),
            ],
        ),
        out_shape=[jax.ShapeDtypeStruct((length, width), bf16), wide_low, wide_low],
        compiler_params=params(),
        cost_estimate=cost(4 * length * width * inner, 2 * width * inner + 12 * length * inner),
        name="hidden_back",
    )(tab, *pieces, middle, hidden, slope_g, slope_u, cot)


def middle_back_kernel(tab_ref, *refs, n_pieces, halves):
    pieces = refs[:n_pieces]
    middle_ref, gg_ref, gu_ref, cot_ref = refs[n_pieces : n_pieces + 4]
    grad_middle_ref, attn_grad_ref, grad_mixed_ref, w_out, w_in, sem = refs[n_pieces + 4 :]
    width = cot_ref.shape[1] // halves
    inner = gg_ref.shape[1] // halves
    early = WeightCopies(pieces, tab_ref, w_in, sem.at[0], width, 2 * inner)
    late = WeightCopies(pieces, tab_ref, w_out, sem.at[1], 0, width)

    @pl.when(pl.program_id(0) == 0)
    def _():
        early.start()
        late.start()
        early.wait()
        late.wait()

    def gradient(rows):
        both = [
            ref[rows, h * inner : (h + 1) * inner] for h in range(halves) for ref in (gg_ref, gu_ref)
        ]
        return dot(jnp.concatenate(both, 1), w_in[...], NT)

    def norm_back(rows, grad):
        middle = middle_ref[rows, :]
        inverse = lax.rsqrt(jnp.mean(middle * middle, -1, keepdims=True) + epsilon)
        normed = middle * inverse
        grad_middle = cot_ref[rows, :].astype(f32) + inverse * (
            grad - normed * jnp.mean(grad * normed, -1, keepdims=True)
        )
        grad_middle_ref[rows, :] = grad_middle
        low = grad_middle.astype(bf16)
        attn_grad_ref[rows, :] = low
        return low

    def mixed_grad(rows, low):
        grad_mixed_ref[rows, :] = dot(low, w_out[...], NT).astype(bf16)

    total = middle_ref.shape[0]
    items = [slice(r, r + SUB) for r in range(0, total, SUB)]
    pipeline(items, gradient, norm_back, mixed_grad, 1)


SUB = 256
MB_ROWS = 256


def middle_back(tab, pieces, middle, gg, gu, cot, halves):
    length, width = middle.shape
    inner = gg.shape[1]
    rows = MB_ROWS
    n = len(pieces)
    narrow = pl.BlockSpec((rows, width), lambda i, t: (i, 0))
    wide = pl.BlockSpec((rows, inner), lambda i, t: (i, 0))
    low = jax.ShapeDtypeStruct((length, width), bf16)
    return pl.pallas_call(
        functools.partial(middle_back_kernel, n_pieces=n, halves=halves),
        grid_spec=pltpu.PrefetchScalarGridSpec(
            num_scalar_prefetch=1,
            grid=(length // rows,),
            in_specs=[ANY] * n + [narrow, wide, wide, narrow],
            out_specs=[narrow] * 3,
            scratch_shapes=[
                pltpu.VMEM((width, width), bf16),
                pltpu.VMEM((width, 2 * inner), bf16),
                pltpu.SemaphoreType.DMA((2, sum(p.shape[0] for p in pieces))),
            ],
        ),
        out_shape=[jax.ShapeDtypeStruct((length, width), f32), low, low],
        compiler_params=params(),
        cost_estimate=cost(
            2 * length * width * (width + 2 * inner), 4 * width * inner + 4 * length * inner
        ),
        name="middle_back",
    )(tab, *pieces, middle, gg, gu, cot)


def input_kernel(tab_ref, *refs, n_pieces, halves):
    pieces = refs[:n_pieces]
    x_ref, grad_middle_ref = refs[n_pieces : n_pieces + 2]
    calls = len(SPLIT)
    parts = refs[n_pieces + 2 : n_pieces + 2 + 3 * calls]
    out_ref, weight, sem = refs[n_pieces + 2 + 3 * calls :]

    @pl.when(pl.program_id(0) == 0)
    def _():
        load_weight(pieces, tab_ref, weight, sem)

    left = [
        in_order(parts[part * calls : (part + 1) * calls], h, halves)
        for h in range(halves)
        for part in range(3)
    ]
    grad = dot(jnp.concatenate(left, 1), weight[...], NT)
    x = x_ref[...].astype(f32)
    inverse = lax.rsqrt(jnp.mean(x * x, -1, keepdims=True) + epsilon)
    normed = x * inverse
    out_ref[...] = grad_middle_ref[...] + inverse * (
        grad - normed * jnp.mean(grad * normed, -1, keepdims=True)
    )


def input_grad(tab, pieces, x, grad_middle, parts, halves):
    length, width = x.shape
    rows = BLOCK
    n = len(pieces)
    blocks = sum(p.shape[0] for p in pieces)
    block = pl.BlockSpec((rows, width), lambda i, t: (i, 0))
    shares = [pl.BlockSpec((rows, p.shape[1]), lambda i, t: (i, 0)) for p in parts]
    return pl.pallas_call(
        functools.partial(input_kernel, n_pieces=n, halves=halves),
        grid_spec=pltpu.PrefetchScalarGridSpec(
            num_scalar_prefetch=1,
            grid=(length // rows,),
            in_specs=[ANY] * n + [block] * 2 + shares,
            out_specs=block,
            scratch_shapes=[
                pltpu.VMEM((width, 3 * width), bf16),
                pltpu.SemaphoreType.DMA((blocks,)),
            ],
        ),
        out_shape=jax.ShapeDtypeStruct((length, width), f32),
        compiler_params=params(),
        cost_estimate=cost(6 * length * width * width, 20 * length * width),
        name="input_grad",
    )(tab, *pieces, x, grad_middle, *parts)


def weight_kernel(tab_ref, *refs, counts, block_rows, chunks, halves):
    n_left, n_right = sum(n for n, _ in counts), sum(n for _, n in counts)
    lefts, rights = list(refs[:n_left]), list(refs[n_left : n_left + n_right])
    keep_ref, send_ref, held, sem = refs[n_left + n_right :]
    step, steps = pl.program_id(0), pl.num_programs(0)
    slot = lax.rem(step, 2)
    here = halves if chunks == 0 else 1
    parts = max(1, chunks)
    rows = held.shape[2]
    kept = keep_ref.shape[0]
    widths = [r.shape[1] // here for r in rights]
    sizes = [sum(widths)] if parts == 1 else widths

    def pieces():
        for b in range(rows // block_rows):
            for h in range(here):
                offset = 0
                for i, width in enumerate(sizes):
                    yield b, h, (b * here + h) * len(sizes) + i, offset, width
                    offset += width

    def wait(which):
        for _, h, number, offset, width in pieces():
            pltpu.make_async_copy(
                held.at[which, h, pl.ds(0, block_rows), pl.ds(offset, width)],
                keep_ref.at[0, :, pl.ds(offset, width)],
                sem.at[which, number],
            ).wait()

    @pl.when(step >= 2)
    def _():
        wait(slot)

    offset = 0
    for _, n_right in counts:
        left = lefts.pop(0)[...]
        group = [rights.pop(0)[...] for _ in range(n_right)]
        result = dot(left, jnp.concatenate(group, 1), TN).astype(bf16)
        column = 0
        for right in group:
            width = right.shape[1] // here
            for h in range(here):
                held[slot, h, :, offset : offset + width] = result[:, column : column + width]
                column += width
            offset += width
    if chunks == 0:
        first, half, chunk = step * (rows // block_rows), 0, 0
    else:
        first, half, chunk = 0, step // chunks, lax.rem(step, chunks)
    def send_out(parity):
        for b, h, number, offset, width in pieces():
            place = tab_ref[(first + b) * halves + half + h]
            if b % 2 == parity:
                target = keep_ref.at[place]
            else:
                target = send_ref.at[place - kept]
            pltpu.make_async_copy(
                held.at[slot, h, pl.ds(b * block_rows, block_rows), pl.ds(offset, width)],
                target.at[:, pl.ds(pl.multiple_of(offset * parts + chunk * width, 128), width)],
                sem.at[slot, number],
            ).start()

    for parity in range(2):
        pl.when((tab_ref[0] < kept) == (parity == 0))(functools.partial(send_out, parity))

    @pl.when(step == steps - 1)
    def _():
        wait(slot)

        @pl.when(steps > 1)
        def _():
            wait(1 - slot)


def weight_grad(moves, products, name, chunks=0, row_steps=1):
    lefts = [left for group, _ in products for left in group]
    rights = [right for _, group in products for right in group]
    counts = [(len(left), len(right)) for left, right in products]
    length = lefts[0].shape[0]
    rows = sum(left.shape[1] for left in products[0][0])
    halves, blocks = moves.halves, moves.place.shape[0]
    block_rows = rows * halves // blocks
    columns = sum(r.shape[1] for r in rights) // halves
    kept = moves.kept
    sent = max(1, blocks - kept)
    if halves == 1 and chunks == 0:
        row_steps = 1
    steps = halves * chunks if chunks else row_steps
    here = 1 if chunks else halves
    step_rows = rows if chunks else rows // row_steps
    n_pieces = step_rows // block_rows * here * (len(rights) if chunks > 1 else 1)
    if chunks:
        left_specs = [pl.BlockSpec(left.shape, lambda i, t: (0, 0)) for left in lefts]
        right_specs = [pl.BlockSpec((length, r.shape[1] // steps), lambda i, t: (0, i)) for r in rights]
    else:
        left_specs = [
            pl.BlockSpec((length, left.shape[1] // row_steps), lambda i, t: (0, i)) for left in lefts
        ]
        right_specs = [pl.BlockSpec(r.shape, lambda i, t: (0, 0)) for r in rights]
    return pl.pallas_call(
        functools.partial(
            weight_kernel, counts=counts, block_rows=block_rows, chunks=chunks, halves=halves
        ),
        grid_spec=pltpu.PrefetchScalarGridSpec(
            num_scalar_prefetch=1,
            grid=(steps,),
            in_specs=left_specs + right_specs,
            out_specs=[ANY, ANY],
            scratch_shapes=[
                pltpu.VMEM((2, here, step_rows, columns // max(1, chunks)), bf16),
                pltpu.SemaphoreType.DMA((2, n_pieces)),
            ],
        ),
        out_shape=[
            jax.ShapeDtypeStruct((kept, block_rows, columns), bf16),
            jax.ShapeDtypeStruct((sent, block_rows, columns), bf16),
        ],
        compiler_params=params(),
        cost_estimate=cost(
            2 * length * rows * columns * halves,
            2 * (length * rows + length * columns * halves + rows * columns * halves),
        ),
        name=name,
    )(moves.place, *lefts, *rights)


def after(value, *others):
    return lax.optimization_barrier((value, others))[0]


def place_of(xr, yr, zr, cr):
    low = xr * 4 + yr * 2 + zr
    high = 8 + yr * 4 + xr * 2 + (zr - 2)
    return cr * 16 + jnp.where(zr < 2, low, high)


def swapped(bits, axis="shard"):
    count = lax.axis_size(axis)
    pairs = [(i, i ^ bits) for i in range(count)]
    return lambda array: lax.ppermute(array, axis, pairs)


class Direct:
    halves = 2
    kept = 16

    def __init__(self):
        self.me = lax.axis_index("shard")
        self.x = lax.axis_index("rep")
        self.core, self.y, self.x_move = swapped(1), swapped(2), swapped(1, "rep")
        self.z = [swapped(4), swapped(8), swapped(12)]
        shard = jnp.arange(16, dtype=jnp.int32)[:, None]
        half = jnp.arange(2, dtype=jnp.int32)[None, :]
        rel = shard ^ self.me
        place = place_of(half ^ self.x, (rel >> 1) & 1, rel >> 2, rel & 1)
        self.place = place.reshape(32)
        order = []
        for cr in range(2):
            for zs in ((0, 1), (2, 3)):
                for outer in range(2):
                    for inner in range(2):
                        for zr in zs:
                            xr, yr = (outer, inner) if zs[0] == 0 else (inner, outer)
                            order.append((zr * 4 + yr * 2 + cr, xr))
        rel_shard = jnp.array([o[0] for o in order], jnp.int32)
        rel_half = jnp.array([o[1] for o in order], jnp.int32)
        self.tab = jnp.stack([rel_shard ^ self.me, rel_half ^ self.x])

    def pack(self, arrays, gain):
        return pack(self.x, arrays, gain, 2)

    def along_z(self, own):
        z1, z2, z3 = (move(own) for move in self.z)
        return jnp.concatenate([own, z1], 0), jnp.concatenate([z2, z3], 0), (z1, z2, z3)

    def one_axis(self, a, b):
        ay, bx = self.y(a), self.x_move(b)
        return (a, ay), (b, bx)

    def rest(self, a, b):
        ax, by = self.x_move(a), self.y(b)
        return [a, ax, b, by]

    def with_core(self, own, *deps):
        own = [after(p, *deps) for p in own] if deps else own
        return own + [self.core(p) for p in own]

    def gather(self, blocks):
        first, second, third = (block[None] for block in blocks)
        a1, b1, z_done1 = self.along_z(first)
        a2, b2, z_done2 = self.along_z(after(second, *z_done1))
        a1, b1 = self.one_axis(a1, b1)
        a1, b1 = jnp.concatenate(a1, 0), jnp.concatenate(b1, 0)
        own1 = self.rest(a1, b1)
        w1 = self.with_core(own1)
        self.a2, self.b2 = after(a2, *own1), after(b2, *own1)
        self.third = after(third, *z_done2, *own1)
        return w1

    def stage0(self):
        self.pair2 = self.one_axis(self.a2, self.b2)
        self.z3 = self.z[0](self.third)
        return self.a2, self.b2, self.third

    def stage1(self, *deps):
        (a, ay), (b, bx) = self.pair2
        deps = (*deps, self.z3, ay, bx)
        a = jnp.concatenate([after(a, *deps), ay], 0)
        b = jnp.concatenate([after(b, *deps), bx], 0)
        a3 = jnp.concatenate([after(self.third, *deps), self.z3], 0)
        self.a3, self.b3 = a3, self.z[1](a3)
        self.own2 = self.rest(a, b)
        self.core2 = [self.core(a), None, self.core(b), None]
        return a, b, a3

    def stage2(self, *deps):
        deps = (*deps, self.b3, self.core2[0], self.core2[2])
        self.a3, self.b3 = after(self.a3, *deps), after(self.b3, *deps)
        self.pair3 = self.one_axis(self.a3, self.b3)
        return self.a3, self.b3

    def stage3(self, *deps):
        (a, ay), (b, bx) = self.pair3
        deps = (*deps, *self.own2, ay, bx)
        a = jnp.concatenate([after(a, *deps), ay], 0)
        b = jnp.concatenate([after(b, *deps), bx], 0)
        self.own3 = self.rest(a, b)
        for i in (1, 3):
            self.core2[i] = self.core(after(self.own2[i], *deps, a, b))
        self.own2 += self.core2
        return a, b

    def scatter(self, grads, direct=False):
        return Direct.Sum(self, grads, direct)

    class Sum:
        def __init__(self, moves, grads, direct):
            self.moves = moves
            self.keep, self.send = grads
            over_z = [self.over_z] if direct else [self.over_z2, self.over_z1]
            self.steps = [self.over_core, self.over_two, self.over_other, *over_z, self.over_x]
            self.start = self.steps[0]
            self.got = ()

        def step(self, *deps):
            if deps:
                self.keep = after(self.keep, *deps)
                if self.steps[0] == self.start:
                    self.send = after(self.send, *deps)
            return self.steps.pop(0)()

        def finish(self):
            while self.steps:
                self.step()
            return self.result

        @staticmethod
        def add(*terms):
            total = terms[0].astype(f32)
            for term in terms[1:]:
                total = total + term.astype(f32)
            return total.astype(bf16)

        def over_core(self):
            self.core = self.moves.core(self.send)
            self.got = (self.core,)
            return (self.send,)

        def over_two(self):
            keep, core = self.keep, self.core
            to_x, to_y = self.add(keep[4:8], core[4:8]), self.add(keep[12:16], core[12:16])
            self.ax, self.by = self.got = self.moves.x_move(to_x), self.moves.y(to_y)
            return to_x, to_y

        def over_other(self):
            keep, core, ax, by = self.keep, self.core, self.ax, self.by
            to_y = self.add(keep[2:4], core[2:4], ax[2:4])
            to_x = self.add(keep[10:12], core[10:12], by[2:4])
            self.ay, self.bx = self.got = self.moves.y(to_y), self.moves.x_move(to_x)
            return to_y, to_x

        def over_z(self):
            keep, core, ax, by, ay, bx = self.keep, self.core, self.ax, self.by, self.ay, self.bx
            sends = (
                self.add(keep[1], core[1], ax[1], ay[1]),
                self.add(keep[8], core[8], by[0], bx[0]),
                self.add(keep[9], core[9], by[1], bx[1]),
            )
            self.got = self.zs = tuple(move(send) for move, send in zip(self.moves.z, sends))
            return sends

        def over_z2(self):
            keep, core = self.keep, self.core
            send = self.add(keep[8:10], core[8:10], self.by[0:2], self.bx[0:2])
            self.z2 = self.moves.z[1](send)
            self.got = (self.z2,)
            return (send,)

        def over_z1(self):
            send = self.add(self.keep[1], self.core[1], self.ax[1], self.ay[1], self.z2[1])
            z1 = self.moves.z[0](send)
            self.zs = (self.z2[0], z1)
            self.got = (z1,)
            return (send,)

        def over_x(self):
            own = self.add(self.keep[0], self.core[0], self.ax[0], self.ay[0], *self.zs)
            other = self.moves.x_move(own)
            first = self.moves.x == 0
            self.result = [jnp.where(first, own, other), jnp.where(first, other, own)]
            self.got = (other,)
            return (own,)


class Plain:
    halves = 1
    kept = 1

    def __init__(self):
        self.place = jnp.zeros((1,), jnp.int32)
        self.tab = jnp.zeros((2, 1), jnp.int32)

    def pack(self, arrays, gain):
        return pack(jnp.int32(0), arrays, gain, 1)

    def gather(self, blocks):
        first, *others = (
            [lax.all_gather(block, "shard", axis=0, tiled=True)[None]] for block in blocks
        )
        self.own2, self.own3 = others
        return first

    def with_core(self, own, *deps):
        return own

    def stage0(self):
        return ()

    def stage1(self, *deps):
        return ()

    stage2 = stage3 = stage1

    def scatter(self, grads, direct=False):
        return Plain.Sum(grads)

    class Sum:
        got = ()

        def __init__(self, grads):
            self.grads = grads

        def step(self, *deps):
            return ()

        def finish(self):
            total = self.grads[0][0].astype(f32)
            part = lax.psum_scatter(total, "shard", scatter_dimension=0, tiled=True)
            return [lax.psum(part.astype(bf16), "rep")]


def columns(halves, start, width):
    step = width // len(halves)
    first = start // len(halves)
    return jnp.concatenate([h[:, first : first + step] for h in halves], 1).astype(f32)


def one_sequence(moves, x, docs, w1, cot, inner):
    cosine, sine = rope_tables(x.shape[0])
    q_marks, k_marks = marks(docs.reshape(-1, 1))
    halves, tab = moves.halves, moves.tab
    sends = moves.stage0()
    normed1, q, k, v = project(tab, w1, after(x, *sends), cosine, sine, halves)
    sends = moves.stage1(normed1)
    mixed, inv, exps = attend(q, k, v, after(q_marks, *sends), k_marks)
    sends = moves.stage2(mixed)
    sends = moves.stage3(mixed, *sends)
    w2 = moves.own2
    middle, normed2, hidden, slope_g, slope_u = ffn(
        tab, w2, after(x, *sends), mixed, inner, halves
    )
    w3 = moves.with_core(moves.own3, hidden)
    g3 = weight_grad(moves, [([after(hidden, *moves.own3)], [cot])], "grad_down", row_steps=4)
    sum3 = moves.scatter(g3)
    sum3.step(*g3, *w3)
    output, gg, gu = hidden_back(
        tab, w3, middle, after(hidden, *g3), slope_g, slope_u, cot, halves
    )
    sends = sum3.step(gg, *sum3.got)
    g2 = weight_grad(moves, [([after(normed2, *sends)], [gg, gu])], "grad_gate_up", chunks=2)
    sum2 = moves.scatter(g2)
    due = (*g2, *sum3.got)
    sends = sum3.step(*due)
    sends = (*sends, *sum2.step(*due))
    grad_middle, attn_grad, grad_mixed = middle_back(
        tab, w2, after(middle, *g2, *sends), gg, gu, cot, halves
    )
    due = (attn_grad, *sum3.got, *sum2.got)
    sends = sum3.step(*due)
    sends = (*sends, *sum2.step(*due))

    def back(call, sends):
        return attend_back(q, k, v, mixed, inv, exps, after(grad_mixed, *sends), cosine, sine, call)

    turned0 = back(0, sends)
    due = (*turned0[:1], *sum2.got, *sum3.got)
    sends = sum2.step(*due)
    sends = (*sends, *sum3.step(*due))
    g1 = weight_grad(
        moves,
        [([after(normed1, *sends)], turned0), ([mixed], [attn_grad])],
        "grad_qk_out",
        row_steps=2,
    )
    sum1 = moves.scatter(g1)
    due = (*g1, *sum2.got, *sum3.got)
    sum1.step(*due)
    sends = (*sum2.step(*due), *sum3.step(*due))
    sends = (*sends, *sum1.step(*sends, *sum1.got))
    turned1 = back(1, (*g1, *sends))
    due = (*turned1[:1], *sum1.got, *sum2.got)
    sends = sum1.step(*due)
    sends = (*sends, *sum2.step(*due))
    g0 = weight_grad(moves, [([after(normed1, *sends)], turned1)], "grad_qkv_rest", row_steps=2)
    sum0 = moves.scatter(g0, True)
    due = (*g0, *sum1.got, *sum2.got)
    sum0.step(*due)
    sends = (*sum1.step(*due), *sum2.step(*due))
    sends = (*sends, *sum0.step(*sends, *sum0.got))
    parts = [t[part] for part in range(3) for t in (turned0, turned1)]
    grad_input = input_grad(tab, w1, after(x, *g0, *sends), grad_middle, parts, halves)
    sums = (sum0, sum1, sum2, sum3)
    due = (grad_input, *sum2.got, *sum1.got, *sum0.got)
    for one in (sum0, sum1):
        one.step(*due)
    return output, grad_input, [s.finish() for s in sums]


def per_device(
    inputs,
    doc_ids,
    attn_gain,
    w_query,
    w_key,
    w_value,
    w_out,
    ffn_gain,
    w_gate,
    w_up,
    w_down,
    cotangent,
):
    batch_size, length, width = inputs.shape
    inner = w_gate.shape[1]
    replicas, members = lax.axis_size("rep"), lax.axis_size("shard")
    moves = Direct() if (replicas, members, batch_size) == (2, 16, 1) else Plain()
    gain1 = attn_gain.astype(f32)[:, None]
    gain2 = ffn_gain.astype(f32)[:, None]

    w1 = moves.gather(
        [
            moves.pack([(w, True) for w in (w_query, w_key, w_value)], gain1),
            moves.pack([(w_out, False), (w_gate, True), (w_up, True)], gain2),
            moves.pack([(w_down, False)], jnp.ones((w_down.shape[0], 1), f32)),
        ]
    )
    outputs, grad_inputs, sums = [], [], None
    for b in range(batch_size):
        output, grad_input, own = one_sequence(
            moves, inputs[b], doc_ids[b], w1, cotangent[b], inner
        )
        outputs.append(output)
        grad_inputs.append(grad_input)
        sums = own if sums is None else jax.tree.map(jnp.add, sums, own)
    s0, s1, s2, s3 = sums
    scale = 1.0 / (batch_size * replicas * members)
    down = columns(s3, 0, width)
    gate, up = columns(s2, 0, inner), columns(s2, inner, inner)
    shares = [width * count // sum(SPLIT) for count in SPLIT]
    out = columns(s1, 3 * shares[0], width)

    def head_columns(part):
        sources = [columns(s, part * share, share) for s, share in zip((s1, s0), shares)]
        return jnp.concatenate(
            [c[:, j * c.shape[1] // 2 : (j + 1) * c.shape[1] // 2] for j in range(2) for c in sources], 1
        )

    query, key, value = (head_columns(part) for part in range(3))

    def gain_grad(pairs):
        total = sum(jnp.sum(w.astype(f32) * g, 1) for w, g in pairs)
        return total * scale

    return (
        jnp.stack(outputs),
        jnp.stack(grad_inputs),
        gain_grad([(w_query, query), (w_key, key), (w_value, value)]),
        query * gain1 * scale,
        key * gain1 * scale,
        value * gain1 * scale,
        out * scale,
        gain_grad([(w_gate, gate), (w_up, up)]),
        gate * gain2 * scale,
        up * gain2 * scale,
        down * scale,
    )


def solution(mesh):
    row = P("shard", None)
    tokens = P(("rep", "shard"), None, None)
    return jax.shard_map(
        per_device,
        mesh=mesh,
        in_specs=(
            tokens, P(("rep", "shard"), None), P("shard"), row, row, row, row, P("shard"), row, row, row, tokens,
        ),
        out_specs=(tokens, tokens, P("shard"), row, row, row, row, P("shard"), row, row, row),
        check_vma=False,
    )
```

```python
import functools

import jax
import jax.numpy as jnp
import numpy as np
from jax import lax
from jax.experimental import pallas as pl
from jax.experimental.pallas import tpu as pltpu
from jax.sharding import PartitionSpec as P

H = 12
HD = 64
BLOCK = 256
MAX_DOC = 512

epsilon = 1e-06
rope_base = 10000.0
far = 1e30

bf16 = jnp.bfloat16
f32 = jnp.float32
MIB = 1 << 20
NN = (((1,), (0,)), ((), ()))
NT = (((1,), (1,)), ((), ()))
TN = (((0,), (0,)), ((), ()))


def dot(left, right, dims=NN):
    return lax.dot_general(left, right, dims, preferred_element_type=f32)


def params():
    return pltpu.CompilerParams(vmem_limit_bytes=60 * MIB)


HINT = 1.0


def cost(flops, nbytes, trans=0):
    return pl.CostEstimate(
        flops=int(HINT * flops), bytes_accessed=int(HINT * nbytes), transcendentals=int(HINT * trans)
    )


ANY = pl.BlockSpec(memory_space=pl.ANY)


class WeightCopies:
    def __init__(self, pieces, tab_ref, dest, sem, start, width):
        self.pieces, self.tab, self.dest, self.sem = pieces, tab_ref, dest, sem
        self.start_col, self.width = start, width

    def each(self, act):
        for number, piece in enumerate(self.pieces):
            count, rows = piece.shape[0], piece.shape[1]

            def step(b, carry):
                index = number * count + b
                row = pl.multiple_of(self.tab[0, index] * rows, 16)
                col = pl.multiple_of(self.tab[1, index] * self.width, 128)
                act(
                    pltpu.make_async_copy(
                        piece.at[b, :, pl.ds(self.start_col, self.width)],
                        self.dest.at[pl.ds(row, rows), pl.ds(col, self.width)],
                        self.sem.at[index],
                    )
                )
                return carry

            lax.fori_loop(0, count, step, 0)

    def start(self):
        self.each(lambda copy: copy.start())

    def wait(self):
        self.each(lambda copy: copy.wait())


def load_weight(pieces, tab_ref, dest, sem):
    copies = WeightCopies(pieces, tab_ref, dest, sem, 0, pieces[0].shape[2])
    copies.start()
    copies.wait()


SPLIT = (2, 1)


def in_order(refs, half=0, halves=1):
    return jnp.concatenate(
        [
            ref[:, j * (ref.shape[1] // 2) : (j + 1) * (ref.shape[1] // 2)]
            for j in range(2)
            if j * halves // 2 == half
            for ref in refs
        ],
        1,
    )


def pair_of(call):
    first, count = sum(SPLIT[:call]), SPLIT[call]
    return lambda i: (0, first + i % count + sum(SPLIT) * (i // count))


def pack_kernel(half_ref, *refs, folded):
    *sources, gain_ref, out_ref = refs
    offset = 0
    for source, scaled in zip(sources, folded):
        width = source.shape[1]
        value = source[...]
        if scaled:
            value = (value.astype(f32) * gain_ref[...]).astype(bf16)
        out_ref[:, offset : offset + width] = value
        offset += width


def pack(half, arrays, gain, halves):
    folded = [scaled for _, scaled in arrays]
    arrays = [array for array, _ in arrays]
    rows = arrays[0].shape[0]
    columns = sum(array.shape[1] for array in arrays) // halves
    return pl.pallas_call(
        functools.partial(pack_kernel, folded=folded),
        grid_spec=pltpu.PrefetchScalarGridSpec(
            num_scalar_prefetch=1,
            grid=(1,),
            in_specs=[
                pl.BlockSpec((rows, array.shape[1] // halves), lambda i, h: (0, h[0])) for array in arrays
            ]
            + [pl.BlockSpec((rows, 1), lambda i, h: (0, 0))],
            out_specs=pl.BlockSpec((rows, columns), lambda i, h: (0, 0)),
        ),
        out_shape=jax.ShapeDtypeStruct((rows, columns), bf16),
        compiler_params=params(),
        cost_estimate=cost(rows * columns, 4 * rows * columns),
        name="pack",
    )(half.reshape(1), *arrays, gain)


def rope_tables(length):
    frequency = rope_base ** -(np.arange(HD // 2) * (2.0 / HD))
    coarse = np.arange(length // 32)[:, None] * 32.0 * frequency[None, :]
    fine = np.arange(32)[:, None] * frequency[None, :]
    coarse, fine = np.tile(coarse, (1, 4))[:, None, :], np.tile(fine, (1, 4))[None, :, :]
    sign = np.tile(np.repeat([-1.0, 1.0], HD // 2), 2)
    cos_a, sin_a = jnp.asarray(np.cos(coarse), f32), jnp.asarray(np.sin(coarse), f32)
    cos_b, sin_b = jnp.asarray(np.cos(fine), f32), jnp.asarray(np.sin(fine), f32)
    cosine = cos_a * cos_b - sin_a * sin_b
    sine = (sin_a * cos_b + cos_a * sin_b) * jnp.asarray(sign, f32)
    return cosine.reshape(length, 128), sine.reshape(length, 128)


def swap_halves(tensor):
    lane = lax.broadcasted_iota(jnp.int32, tensor.shape, 1)
    return jnp.where(
        (lane & (HD // 2)) == 0, pltpu.roll(tensor, 128 - HD // 2, 1), pltpu.roll(tensor, HD // 2, 1)
    )


def project_kernel(tab_ref, *refs, n_pieces, halves):
    pieces, (x_ref, cos_ref, sin_ref) = refs[:n_pieces], refs[n_pieces : n_pieces + 3]
    n_ref, q_ref, k_ref, v_ref, weight, sem = refs[n_pieces + 3 :]

    @pl.when(pl.program_id(0) == 0)
    def _():
        load_weight(pieces, tab_ref, weight, sem)

    x = x_ref[...].astype(f32)
    normed = (x * lax.rsqrt(jnp.mean(x * x, -1, keepdims=True) + epsilon)).astype(bf16)
    n_ref[...] = normed
    width = x_ref.shape[1] // halves
    cosine, sine = cos_ref[...], sin_ref[...]
    everything = dot(normed, weight[...])
    for half in range(halves):
        result = everything[:, 3 * half * width : 3 * (half + 1) * width]
        for part, out, scale in ((0, q_ref, HD**-0.5), (1, k_ref, 1.0)):
            for c in range(0, width, 128):
                piece = result[:, part * width + c : part * width + c + 128]
                turned = piece * cosine + swap_halves(piece) * sine
                out[:, half * width + c : half * width + c + 128] = (
                    turned.astype(bf16) * jnp.asarray(scale, bf16)
                )
        v_ref[:, half * width : (half + 1) * width] = result[:, 2 * width :].astype(bf16)


def project(tab, pieces, x, cosine, sine, halves):
    length, width = x.shape
    rows = BLOCK
    n = len(pieces)
    blocks = sum(p.shape[0] for p in pieces)
    block = pl.BlockSpec((rows, width), lambda i, t: (i, 0))
    table = pl.BlockSpec((rows, 128), lambda i, t: (i, 0))
    shape = jax.ShapeDtypeStruct((length, width), bf16)
    return pl.pallas_call(
        functools.partial(project_kernel, n_pieces=n, halves=halves),
        grid_spec=pltpu.PrefetchScalarGridSpec(
            num_scalar_prefetch=1,
            grid=(length // rows,),
            in_specs=[ANY] * n + [block, table, table],
            out_specs=[block] * 4,
            scratch_shapes=[
                pltpu.VMEM((width, 3 * width), bf16),
                pltpu.SemaphoreType.DMA((blocks,)),
            ],
        ),
        out_shape=[shape] * 4,
        compiler_params=params(),
        cost_estimate=cost(6 * length * width * width, 16 * length * width),
        name="project",
    )(tab, *pieces, x, cosine, sine)


def key_range(block):
    low = max(0, (block * BLOCK - (MAX_DOC - 1)) // BLOCK) if block * BLOCK > MAX_DOC - 1 else 0
    return low * BLOCK, (block + 1) * BLOCK


def marks(docs):
    lane = jnp.arange(128, dtype=jnp.int32)[None, :] % HD
    used = lane < 4
    same = docs == lane
    return (
        jnp.where(used & ~same, -far, 0.0).astype(bf16),
        jnp.where(used & same, 1.0, 0.0).astype(bf16),
    )


def pipeline(items, first, second, third, ahead=2):
    made = [first(item) for item in items[:ahead]]
    pending = None
    for i, item in enumerate(items):
        if i + ahead < len(items):
            made.append(first(items[i + ahead]))
        middle = second(item, made[i])
        made[i] = None
        if pending is not None:
            third(*pending)
        pending = (item, middle)
    third(*pending)


def attend_kernel(q_ref, k_ref, v_ref, qm_ref, km_ref, mixed_ref, inv_ref, e_ref):
    length = q_ref.shape[0]
    lane = lax.broadcasted_iota(jnp.int32, (length, 128), 1)
    front = lax.broadcasted_iota(jnp.int32, (BLOCK, 128), 1) < HD
    q, k, v = q_ref[...], k_ref[...], v_ref[...]
    ones = jnp.ones((length, 128), bf16)
    operands = []
    for head in range(2):
        own = (lane < HD) if head == 0 else (lane >= HD)
        operands.append(
            (jnp.where(own, q, qm_ref[...]), jnp.where(own, k, km_ref[...]), jnp.where(own, v, ones))
        )
    outs = {}

    def scores(item):
        block, head = item
        low, high = key_range(block)
        qa, ka, _ = operands[head]
        return dot(ka[low:high], qa[block * BLOCK : (block + 1) * BLOCK], NT)

    def softmax(item, values):
        block, head = item
        low, high = key_range(block)
        exps = jnp.exp(values - jnp.max(values, 0, keepdims=True)).astype(bf16)
        for kb in range(low // BLOCK, high // BLOCK):
            e_ref[head, kb, :, (block - kb) * BLOCK : (block - kb + 1) * BLOCK] = exps[
                kb * BLOCK - low : (kb + 1) * BLOCK - low
            ]
        return exps

    def mix(item, exps):
        block, head = item
        low, high = key_range(block)
        outs[head] = dot(exps, operands[head][2][low:high], TN)
        if head == 1:
            rows = slice(block * BLOCK, (block + 1) * BLOCK)
            value = jnp.where(front, outs[0], outs[1])
            total = jnp.where(front, outs[1], outs[0])
            inverse = pltpu.roll(1.0 / total, HD, 1)
            mixed_ref[rows, :] = (value * inverse).astype(bf16)
            inv_ref[rows, :] = inverse

    items = [(block, head) for block in range(length // BLOCK) for head in range(2)]
    pipeline(items, scores, softmax, mix)


def span(length):
    return min(length, MAX_DOC + BLOCK)


def attend(q, k, v, q_marks, k_marks):
    length, width = q.shape
    blocks = length // BLOCK
    pairs = width // 128
    column = pl.BlockSpec((length, 128), lambda i: (0, i))
    fixed = pl.BlockSpec((length, 128), lambda i: (0, 0))
    return pl.pallas_call(
        attend_kernel,
        grid=(pairs,),
        in_specs=[column, column, column, fixed, fixed],
        out_specs=[column, column, pl.BlockSpec((2, blocks, BLOCK, span(length)), lambda i: (i, 0, 0, 0))],
        out_shape=[
            jax.ShapeDtypeStruct((length, 128 * pairs), bf16),
            jax.ShapeDtypeStruct((length, 128 * pairs), f32),
            jax.ShapeDtypeStruct((2 * pairs, blocks, BLOCK, span(length)), bf16),
        ],
        compiler_params=params(),
        cost_estimate=cost(1280 * pairs * length * length, 3840 * pairs * length, 2 * pairs * length * length),
        name="attend",
    )(q, k, v, q_marks, k_marks)


def attend_back_kernel(
    q_ref, k_ref, v_ref, mixed_ref, inv_ref, e_ref, grad_ref, cos_ref, sin_ref,
    dq_ref, dk_ref, dv_ref, ds_ref,
):
    length = q_ref.shape[0]
    count = length // BLOCK
    lane = lax.broadcasted_iota(jnp.int32, (length, 128), 1)
    q, k, v = q_ref[...], k_ref[...], v_ref[...]
    zero = jnp.zeros((length, 128), bf16)
    scaled = grad_ref[...].astype(f32) * inv_ref[...]
    inner = scaled * mixed_ref[...].astype(f32)
    operands = []
    for head in range(2):
        own = (lane < HD) if head == 0 else (lane >= HD)
        first = HD if head == 0 else 0
        spare = (lane == first) | (lane == first + 1)
        minus = jnp.where(spare, -1.0, 0.0).astype(bf16)
        delta = jnp.sum(jnp.where(own, inner, 0.0), 1, keepdims=True)
        upper = delta.astype(bf16).astype(f32)
        masked = jnp.where(own, scaled, 0.0)
        joined = jnp.where(lane == first, upper, masked)
        joined = jnp.where(lane == first + 1, delta - upper, joined).astype(bf16)
        operands.append(
            (
                jnp.where(own, q, zero),
                jnp.where(own, k, zero),
                jnp.where(own, v, minus),
                masked.astype(bf16),
                joined,
            )
        )
    sums = {}

    def turn_back(value, rows):
        return (value * cos_ref[rows, :] - swap_halves(value) * sin_ref[rows, :]).astype(bf16)

    def slopes(item):
        block, head = item
        low, high = key_range(block)
        return dot(
            operands[head][2][low:high], operands[head][4][block * BLOCK : (block + 1) * BLOCK], NT
        )

    def products(item, slope):
        block, head = item
        low, high = key_range(block)
        parts = []
        for kb in range(low // BLOCK, high // BLOCK):
            cols = slice((block - kb) * BLOCK, (block - kb + 1) * BLOCK)
            part = e_ref[head, kb, :, cols].astype(f32) * slope[kb * BLOCK - low : (kb + 1) * BLOCK - low]
            part = part.astype(bf16)
            ds_ref[head, kb, :, cols] = part
            parts.append(part)
        return jnp.concatenate(parts, 0)

    def finish(item, ds):
        block, head = item
        low, high = key_range(block)
        rows = slice(block * BLOCK, (block + 1) * BLOCK)
        part = dot(ds, operands[head][1][low:high], TN)
        if head == 0:
            sums["q"] = part
        else:
            dq_ref[rows, :] = turn_back((sums["q"] + part) * (HD**-0.5), rows)
        for kb in range(count):
            if max(b for b in range(count) if key_range(b)[0] <= kb * BLOCK) != block:
                continue
            width = (block - kb + 1) * BLOCK
            seen = slice(kb * BLOCK, kb * BLOCK + width)
            keys = slice(kb * BLOCK, (kb + 1) * BLOCK)
            dv = dot(e_ref[head, kb, :, 0:width], operands[head][3][seen])
            dk = dot(ds_ref[head, kb, :, 0:width], operands[head][0][seen])
            if head == 0:
                sums[kb] = (dv, dk)
            else:
                dv_ref[keys, :] = (sums[kb][0] + dv).astype(bf16)
                dk_ref[keys, :] = turn_back(sums[kb][1] + dk, keys)

    items = [(block, head) for block in range(count) for head in range(2)]
    pipeline(items, slopes, products, finish)


def attend_back(q, k, v, mixed, inv, exps, grad, cosine, sine, call):
    length = q.shape[0]
    pairs = 2 * SPLIT[call]
    column = pl.BlockSpec((length, 128), pair_of(call))
    part = pl.BlockSpec((length, 128), lambda i: (0, i))
    fixed = pl.BlockSpec((length, 128), lambda i: (0, 0))
    shape = jax.ShapeDtypeStruct((length, 128 * pairs), bf16)
    return pl.pallas_call(
        attend_back_kernel,
        grid=(pairs,),
        in_specs=[column] * 5
        + [
            pl.BlockSpec((2,) + exps.shape[1:], lambda i: (pair_of(call)(i)[1], 0, 0, 0)),
            column,
            fixed,
            fixed,
        ],
        out_specs=[part] * 3,
        out_shape=[shape] * 3,
        scratch_shapes=[pltpu.VMEM((2,) + exps.shape[1:], bf16)],
        compiler_params=params(),
        cost_estimate=cost(2560 * pairs * length * length, 4608 * pairs * length),
        name="attend_back",
    )(q, k, v, mixed, inv, exps, grad, cosine, sine)


def ffn_kernel(tab_ref, *refs, n_pieces, halves):
    pieces, (x_ref, mixed_ref), refs = refs[:n_pieces], refs[n_pieces : n_pieces + 2], refs[n_pieces + 2 :]
    middle_ref, normed_ref, hidden_ref, slope_g_ref, slope_u_ref, w_out, w_in, sem = refs
    width = x_ref.shape[1] // halves
    inner = hidden_ref.shape[1] // halves
    early = WeightCopies(pieces, tab_ref, w_out, sem.at[0], 0, width)
    late = WeightCopies(pieces, tab_ref, w_in, sem.at[1], width, 2 * inner)

    @pl.when(pl.program_id(0) == 0)
    def _():
        early.start()
        late.start()
        early.wait()

    middle = x_ref[...].astype(f32) + dot(mixed_ref[...], w_out[...])
    middle_ref[...] = middle
    normed = (middle * lax.rsqrt(jnp.mean(middle * middle, -1, keepdims=True) + epsilon)).astype(bf16)
    normed_ref[...] = normed

    @pl.when(pl.program_id(0) == 0)
    def _():
        late.wait()

    step = min(256, inner)

    def dots(first):
        return (
            dot(normed, w_in[:, first : first + step]),
            dot(normed, w_in[:, first + inner : first + inner + step]),
        )

    def activate(first, values):
        gate, up = values
        half_tanh = 0.5 * jnp.tanh(0.5 * gate)
        sigmoid = half_tanh + 0.5
        silu = gate * sigmoid
        cols = slice(first - first // (2 * inner) * inner, first - first // (2 * inner) * inner + step)
        hidden_ref[:, cols] = (silu * up).astype(bf16)
        slope_u_ref[:, cols] = silu.astype(bf16)
        slope_g_ref[:, cols] = (up * (sigmoid + silu * (0.5 - half_tanh))).astype(bf16)

    items = [2 * h * inner + c for h in range(halves) for c in range(0, inner, step)]
    pipeline(items, dots, activate, lambda *_: None)


def ffn(tab, pieces, x, mixed, inner, halves):
    length, width = x.shape
    rows = BLOCK
    n = len(pieces)
    blocks = sum(p.shape[0] for p in pieces)
    narrow = pl.BlockSpec((rows, width), lambda i, t: (i, 0))
    wide = pl.BlockSpec((rows, inner), lambda i, t: (i, 0))
    wide_shape = jax.ShapeDtypeStruct((length, inner), bf16)
    return pl.pallas_call(
        functools.partial(ffn_kernel, n_pieces=n, halves=halves),
        grid_spec=pltpu.PrefetchScalarGridSpec(
            num_scalar_prefetch=1,
            grid=(length // rows,),
            in_specs=[ANY] * n + [narrow, narrow],
            out_specs=[narrow, narrow, wide, wide, wide],
            scratch_shapes=[
                pltpu.VMEM((width, width), bf16),
                pltpu.VMEM((width, 2 * inner), bf16),
                pltpu.SemaphoreType.DMA((2, blocks)),
            ],
        ),
        out_shape=[
            jax.ShapeDtypeStruct((length, width), f32),
            jax.ShapeDtypeStruct((length, width), bf16),
            wide_shape,
            wide_shape,
            wide_shape,
        ],
        compiler_params=params(),
        cost_estimate=cost(2 * length * width * (width + 2 * inner), 8 * width * inner + 8 * length * inner),
        name="ffn",
    )(tab, *pieces, x, mixed)


def hidden_back_kernel(tab_ref, *refs, n_pieces, halves):
    pieces = refs[:n_pieces]
    middle_ref, hidden_ref, slope_g_ref, slope_u_ref, cot_ref = refs[n_pieces : n_pieces + 5]
    output_ref, gg_ref, gu_ref, weight, sem = refs[n_pieces + 5 :]

    @pl.when(pl.program_id(0) == 0)
    def _():
        load_weight(pieces, tab_ref, weight, sem)

    inner = hidden_ref.shape[1]
    step = min(512, inner)
    cot = cot_ref[...]
    for c in range(0, inner, step):
        cols = slice(c, c + step)
        grad_hidden = dot(cot, weight[cols, :], NT)
        gg_ref[:, cols] = (grad_hidden * slope_g_ref[:, cols].astype(f32)).astype(bf16)
        gu_ref[:, cols] = (grad_hidden * slope_u_ref[:, cols].astype(f32)).astype(bf16)
    output_ref[...] = (middle_ref[...] + dot(hidden_ref[...], weight[...])).astype(bf16)


def hidden_back(tab, pieces, middle, hidden, slope_g, slope_u, cot, halves):
    length, width = middle.shape
    inner = hidden.shape[1]
    rows = BLOCK
    n = len(pieces)
    narrow = pl.BlockSpec((rows, width), lambda i, t: (i, 0))
    wide = pl.BlockSpec((rows, inner), lambda i, t: (i, 0))
    wide_low = jax.ShapeDtypeStruct((length, inner), bf16)
    return pl.pallas_call(
        functools.partial(hidden_back_kernel, n_pieces=n, halves=halves),
        grid_spec=pltpu.PrefetchScalarGridSpec(
            num_scalar_prefetch=1,
            grid=(length // rows,),
            in_specs=[ANY] * n + [narrow, wide, wide, wide, narrow],
            out_specs=[narrow, wide, wide],
            scratch_shapes=[
                pltpu.VMEM((inner, width), bf16),
                pltpu.SemaphoreType.DMA((sum(p.shape[0] for p in pieces),)),
            ],
        ),
        out_shape=[jax.ShapeDtypeStruct((length, width), bf16), wide_low, wide_low],
        compiler_params=params(),
        cost_estimate=cost(4 * length * width * inner, 2 * width * inner + 12 * length * inner),
        name="hidden_back",
    )(tab, *pieces, middle, hidden, slope_g, slope_u, cot)


def middle_back_kernel(tab_ref, *refs, n_pieces, halves):
    pieces = refs[:n_pieces]
    middle_ref, gg_ref, gu_ref, cot_ref = refs[n_pieces : n_pieces + 4]
    grad_middle_ref, attn_grad_ref, grad_mixed_ref, w_out, w_in, sem = refs[n_pieces + 4 :]
    width = cot_ref.shape[1] // halves
    inner = gg_ref.shape[1] // halves
    early = WeightCopies(pieces, tab_ref, w_in, sem.at[0], width, 2 * inner)
    late = WeightCopies(pieces, tab_ref, w_out, sem.at[1], 0, width)

    @pl.when(pl.program_id(0) == 0)
    def _():
        early.start()
        late.start()
        early.wait()
        late.wait()

    def gradient(rows):
        both = [
            ref[rows, h * inner : (h + 1) * inner] for h in range(halves) for ref in (gg_ref, gu_ref)
        ]
        return dot(jnp.concatenate(both, 1), w_in[...], NT)

    def norm_back(rows, grad):
        middle = middle_ref[rows, :]
        inverse = lax.rsqrt(jnp.mean(middle * middle, -1, keepdims=True) + epsilon)
        normed = middle * inverse
        grad_middle = cot_ref[rows, :].astype(f32) + inverse * (
            grad - normed * jnp.mean(grad * normed, -1, keepdims=True)
        )
        grad_middle_ref[rows, :] = grad_middle
        low = grad_middle.astype(bf16)
        attn_grad_ref[rows, :] = low
        return low

    def mixed_grad(rows, low):
        grad_mixed_ref[rows, :] = dot(low, w_out[...], NT).astype(bf16)

    total = middle_ref.shape[0]
    items = [slice(r, r + SUB) for r in range(0, total, SUB)]
    pipeline(items, gradient, norm_back, mixed_grad, 1)


SUB = 256
MB_ROWS = 256


def middle_back(tab, pieces, middle, gg, gu, cot, halves):
    length, width = middle.shape
    inner = gg.shape[1]
    rows = MB_ROWS
    n = len(pieces)
    narrow = pl.BlockSpec((rows, width), lambda i, t: (i, 0))
    wide = pl.BlockSpec((rows, inner), lambda i, t: (i, 0))
    low = jax.ShapeDtypeStruct((length, width), bf16)
    return pl.pallas_call(
        functools.partial(middle_back_kernel, n_pieces=n, halves=halves),
        grid_spec=pltpu.PrefetchScalarGridSpec(
            num_scalar_prefetch=1,
            grid=(length // rows,),
            in_specs=[ANY] * n + [narrow, wide, wide, narrow],
            out_specs=[narrow] * 3,
            scratch_shapes=[
                pltpu.VMEM((width, width), bf16),
                pltpu.VMEM((width, 2 * inner), bf16),
                pltpu.SemaphoreType.DMA((2, sum(p.shape[0] for p in pieces))),
            ],
        ),
        out_shape=[jax.ShapeDtypeStruct((length, width), f32), low, low],
        compiler_params=params(),
        cost_estimate=cost(
            2 * length * width * (width + 2 * inner), 4 * width * inner + 4 * length * inner
        ),
        name="middle_back",
    )(tab, *pieces, middle, gg, gu, cot)


def input_kernel(tab_ref, *refs, n_pieces, halves):
    pieces = refs[:n_pieces]
    x_ref, grad_middle_ref = refs[n_pieces : n_pieces + 2]
    calls = len(SPLIT)
    parts = refs[n_pieces + 2 : n_pieces + 2 + 3 * calls]
    out_ref, weight, sem = refs[n_pieces + 2 + 3 * calls :]

    @pl.when(pl.program_id(0) == 0)
    def _():
        load_weight(pieces, tab_ref, weight, sem)

    left = [
        in_order(parts[part * calls : (part + 1) * calls], h, halves)
        for h in range(halves)
        for part in range(3)
    ]
    grad = dot(jnp.concatenate(left, 1), weight[...], NT)
    x = x_ref[...].astype(f32)
    inverse = lax.rsqrt(jnp.mean(x * x, -1, keepdims=True) + epsilon)
    normed = x * inverse
    out_ref[...] = grad_middle_ref[...] + inverse * (
        grad - normed * jnp.mean(grad * normed, -1, keepdims=True)
    )


def input_grad(tab, pieces, x, grad_middle, parts, halves):
    length, width = x.shape
    rows = BLOCK
    n = len(pieces)
    blocks = sum(p.shape[0] for p in pieces)
    block = pl.BlockSpec((rows, width), lambda i, t: (i, 0))
    shares = [pl.BlockSpec((rows, p.shape[1]), lambda i, t: (i, 0)) for p in parts]
    return pl.pallas_call(
        functools.partial(input_kernel, n_pieces=n, halves=halves),
        grid_spec=pltpu.PrefetchScalarGridSpec(
            num_scalar_prefetch=1,
            grid=(length // rows,),
            in_specs=[ANY] * n + [block] * 2 + shares,
            out_specs=block,
            scratch_shapes=[
                pltpu.VMEM((width, 3 * width), bf16),
                pltpu.SemaphoreType.DMA((blocks,)),
            ],
        ),
        out_shape=jax.ShapeDtypeStruct((length, width), f32),
        compiler_params=params(),
        cost_estimate=cost(6 * length * width * width, 20 * length * width),
        name="input_grad",
    )(tab, *pieces, x, grad_middle, *parts)


def weight_kernel(tab_ref, *refs, counts, block_rows, chunks, halves):
    n_left, n_right = sum(n for n, _ in counts), sum(n for _, n in counts)
    lefts, rights = list(refs[:n_left]), list(refs[n_left : n_left + n_right])
    keep_ref, send_ref, held, sem = refs[n_left + n_right :]
    step, steps = pl.program_id(0), pl.num_programs(0)
    slot = lax.rem(step, 2)
    here = halves if chunks == 0 else 1
    parts = max(1, chunks)
    rows = held.shape[2]
    kept = keep_ref.shape[0]
    widths = [r.shape[1] // here for r in rights]
    sizes = [sum(widths)] if parts == 1 else widths

    def pieces():
        for b in range(rows // block_rows):
            for h in range(here):
                offset = 0
                for i, width in enumerate(sizes):
                    yield b, h, (b * here + h) * len(sizes) + i, offset, width
                    offset += width

    def wait(which):
        for _, h, number, offset, width in pieces():
            pltpu.make_async_copy(
                held.at[which, h, pl.ds(0, block_rows), pl.ds(offset, width)],
                keep_ref.at[0, :, pl.ds(offset, width)],
                sem.at[which, number],
            ).wait()

    @pl.when(step >= 2)
    def _():
        wait(slot)

    offset = 0
    for _, n_right in counts:
        left = lefts.pop(0)[...]
        group = [rights.pop(0)[...] for _ in range(n_right)]
        result = dot(left, jnp.concatenate(group, 1), TN).astype(bf16)
        column = 0
        for right in group:
            width = right.shape[1] // here
            for h in range(here):
                held[slot, h, :, offset : offset + width] = result[:, column : column + width]
                column += width
            offset += width
    if chunks == 0:
        first, half, chunk = step * (rows // block_rows), 0, 0
    else:
        first, half, chunk = 0, step // chunks, lax.rem(step, chunks)
    def send_out(parity):
        for b, h, number, offset, width in pieces():
            place = tab_ref[(first + b) * halves + half + h]
            if b % 2 == parity:
                target = keep_ref.at[place]
            else:
                target = send_ref.at[place - kept]
            pltpu.make_async_copy(
                held.at[slot, h, pl.ds(b * block_rows, block_rows), pl.ds(offset, width)],
                target.at[:, pl.ds(pl.multiple_of(offset * parts + chunk * width, 128), width)],
                sem.at[slot, number],
            ).start()

    for parity in range(2):
        pl.when((tab_ref[0] < kept) == (parity == 0))(functools.partial(send_out, parity))

    @pl.when(step == steps - 1)
    def _():
        wait(slot)

        @pl.when(steps > 1)
        def _():
            wait(1 - slot)


def weight_grad(moves, products, name, chunks=0, row_steps=1):
    lefts = [left for group, _ in products for left in group]
    rights = [right for _, group in products for right in group]
    counts = [(len(left), len(right)) for left, right in products]
    length = lefts[0].shape[0]
    rows = sum(left.shape[1] for left in products[0][0])
    halves, blocks = moves.halves, moves.place.shape[0]
    block_rows = rows * halves // blocks
    columns = sum(r.shape[1] for r in rights) // halves
    kept = moves.kept
    sent = max(1, blocks - kept)
    if blocks == 1 and chunks == 0:
        row_steps = 1
    steps = halves * chunks if chunks else row_steps
    here = 1 if chunks else halves
    step_rows = rows if chunks else rows // row_steps
    n_pieces = step_rows // block_rows * here * (len(rights) if chunks > 1 else 1)
    if chunks:
        left_specs = [pl.BlockSpec(left.shape, lambda i, t: (0, 0)) for left in lefts]
        right_specs = [pl.BlockSpec((length, r.shape[1] // steps), lambda i, t: (0, i)) for r in rights]
    else:
        left_specs = [
            pl.BlockSpec((length, left.shape[1] // row_steps), lambda i, t: (0, i)) for left in lefts
        ]
        right_specs = [pl.BlockSpec(r.shape, lambda i, t: (0, 0)) for r in rights]
    return pl.pallas_call(
        functools.partial(
            weight_kernel, counts=counts, block_rows=block_rows, chunks=chunks, halves=halves
        ),
        grid_spec=pltpu.PrefetchScalarGridSpec(
            num_scalar_prefetch=1,
            grid=(steps,),
            in_specs=left_specs + right_specs,
            out_specs=[ANY, ANY],
            scratch_shapes=[
                pltpu.VMEM((2, here, step_rows, columns // max(1, chunks)), bf16),
                pltpu.SemaphoreType.DMA((2, n_pieces)),
            ],
        ),
        out_shape=[
            jax.ShapeDtypeStruct((kept, block_rows, columns), bf16),
            jax.ShapeDtypeStruct((sent, block_rows, columns), bf16),
        ],
        compiler_params=params(),
        cost_estimate=cost(
            2 * length * rows * columns * halves,
            2 * (length * rows + length * columns * halves + rows * columns * halves),
        ),
        name=name,
    )(moves.place, *lefts, *rights)


def after(value, *others):
    return lax.optimization_barrier((value, others))[0]


def place_of(xr, yr, zr, cr):
    low = xr * 4 + yr * 2 + zr
    high = 8 + yr * 4 + xr * 2 + (zr - 2)
    return cr * 16 + jnp.where(zr < 2, low, high)


def swapped(bits, axis="shard"):
    count = lax.axis_size(axis)
    pairs = [(i, i ^ bits) for i in range(count)]
    return lambda array: lax.ppermute(array, axis, pairs)


class Direct:
    halves = 2
    kept = 16

    def __init__(self):
        self.me = lax.axis_index("shard")
        self.x = lax.axis_index("rep")
        self.core, self.y, self.x_move = swapped(1), swapped(2), swapped(1, "rep")
        self.z = [swapped(4), swapped(8), swapped(12)]
        shard = jnp.arange(16, dtype=jnp.int32)[:, None]
        half = jnp.arange(2, dtype=jnp.int32)[None, :]
        rel = shard ^ self.me
        place = place_of(half ^ self.x, (rel >> 1) & 1, rel >> 2, rel & 1)
        self.place = place.reshape(32)
        order = []
        for cr in range(2):
            for zs in ((0, 1), (2, 3)):
                for outer in range(2):
                    for inner in range(2):
                        for zr in zs:
                            xr, yr = (outer, inner) if zs[0] == 0 else (inner, outer)
                            order.append((zr * 4 + yr * 2 + cr, xr))
        rel_shard = jnp.array([o[0] for o in order], jnp.int32)
        rel_half = jnp.array([o[1] for o in order], jnp.int32)
        self.tab = jnp.stack([rel_shard ^ self.me, rel_half ^ self.x])
        order = [(zr * 4 + yr * 2 + cr, xr) for cr in range(2) for xr in range(2) for yr in range(2) for zr in range(4)]
        rel_shard = jnp.array([o[0] for o in order], jnp.int32)
        rel_half = jnp.array([o[1] for o in order], jnp.int32)
        self.tab3 = jnp.stack([rel_shard ^ self.me, rel_half ^ self.x])
        rel = rel[:, 0]
        self.wide = Wide(self, (rel & 1) * 8 + ((rel >> 1) & 1) * 4 + (rel >> 2))

    def xy(self, array):
        pairs = [(i, i ^ 18) for i in range(32)]
        return lax.ppermute(array, ("rep", "shard"), pairs)

    def pack(self, arrays, gain):
        return pack(self.x, arrays, gain, 2)

    def along_z(self, own):
        z1, z2, z3 = (move(own) for move in self.z)
        return jnp.concatenate([own, z1], 0), jnp.concatenate([z2, z3], 0), (z1, z2, z3)

    def one_axis(self, a, b):
        ay, bx = self.y(a), self.x_move(b)
        return (a, ay), (b, bx)

    def rest(self, a, b):
        ax, by = self.x_move(a), self.y(b)
        return [a, ax, b, by]

    def with_core(self, own, *deps):
        own = [after(p, *deps) for p in own] if deps else own
        return own + [self.core(p) for p in own]

    def gather(self, blocks):
        first, second, third = (block[None] for block in blocks)
        a1, b1, z_done1 = self.along_z(first)
        a2, b2, z_done2 = self.along_z(after(second, *z_done1))
        a1, b1 = self.one_axis(a1, b1)
        a1, b1 = jnp.concatenate(a1, 0), jnp.concatenate(b1, 0)
        own1 = self.rest(a1, b1)
        w1 = self.with_core(own1)
        self.a2, self.b2 = after(a2, *own1), after(b2, *own1)
        self.third = after(third, *z_done2, *own1)
        return w1

    def stage0(self):
        self.pair2 = self.one_axis(self.a2, self.b2)
        self.z3 = self.z[0](self.third)
        return self.a2, self.b2, self.third

    def stage1(self, *deps):
        (a, ay), (b, bx) = self.pair2
        deps = (*deps, self.z3, ay, bx)
        a = jnp.concatenate([after(a, *deps), ay], 0)
        b = jnp.concatenate([after(b, *deps), bx], 0)
        a3 = jnp.concatenate([after(self.third, *deps), self.z3], 0)
        self.a3, self.b3 = a3, self.z[1](a3)
        self.own2 = self.rest(a, b)
        self.core2 = [self.core(a), None, self.core(b), None]
        return a, b, a3

    def stage3(self, *deps):
        deps = (*deps, *self.own2, self.b3, self.core2[0], self.core2[2])
        block = jnp.concatenate([after(self.a3, *deps), after(self.b3, *deps)], 0)
        self.own3 = [block, self.y(block), self.x_move(block), self.xy(block)]
        for i in (1, 3):
            self.core2[i] = self.core(after(self.own2[i], *deps, block))
        self.own2 += self.core2
        return (block,)

    def scatter(self, grads, direct=False):
        return Direct.Sum(self, grads, direct)

    class Sum:
        def __init__(self, moves, grads, direct):
            self.moves = moves
            self.keep, self.send = grads
            over_z = [self.over_z] if direct else [self.over_z2, self.over_z1]
            self.steps = [self.over_core, self.over_two, self.over_other, *over_z, self.over_x]
            self.start = self.steps[0]
            self.got = ()

        def step(self, *deps):
            if deps:
                self.keep = after(self.keep, *deps)
                if self.steps[0] == self.start:
                    self.send = after(self.send, *deps)
            return self.steps.pop(0)()

        def finish(self):
            while self.steps:
                self.step()
            return self.result

        @staticmethod
        def add(*terms):
            total = terms[0].astype(f32)
            for term in terms[1:]:
                total = total + term.astype(f32)
            return total.astype(bf16)

        def over_core(self):
            self.core = self.moves.core(self.send)
            self.got = (self.core,)
            return (self.send,)

        def over_two(self):
            keep, core = self.keep, self.core
            to_x, to_y = self.add(keep[4:8], core[4:8]), self.add(keep[12:16], core[12:16])
            self.ax, self.by = self.got = self.moves.x_move(to_x), self.moves.y(to_y)
            return to_x, to_y

        def over_other(self):
            keep, core, ax, by = self.keep, self.core, self.ax, self.by
            to_y = self.add(keep[2:4], core[2:4], ax[2:4])
            to_x = self.add(keep[10:12], core[10:12], by[2:4])
            self.ay, self.bx = self.got = self.moves.y(to_y), self.moves.x_move(to_x)
            return to_y, to_x

        def over_z(self):
            keep, core, ax, by, ay, bx = self.keep, self.core, self.ax, self.by, self.ay, self.bx
            sends = (
                self.add(keep[1], core[1], ax[1], ay[1]),
                self.add(keep[8], core[8], by[0], bx[0]),
                self.add(keep[9], core[9], by[1], bx[1]),
            )
            self.got = self.zs = tuple(move(send) for move, send in zip(self.moves.z, sends))
            return sends

        def over_z2(self):
            keep, core = self.keep, self.core
            send = self.add(keep[8:10], core[8:10], self.by[0:2], self.bx[0:2])
            self.z2 = self.moves.z[1](send)
            self.got = (self.z2,)
            return (send,)

        def over_z1(self):
            send = self.add(self.keep[1], self.core[1], self.ax[1], self.ay[1], self.z2[1])
            z1 = self.moves.z[0](send)
            self.zs = (self.z2[0], z1)
            self.got = (z1,)
            return (send,)

        def over_x(self):
            own = self.add(self.keep[0], self.core[0], self.ax[0], self.ay[0], *self.zs)
            other = self.moves.x_move(own)
            first = self.moves.x == 0
            self.result = [jnp.where(first, own, other), jnp.where(first, other, own)]
            self.got = (other,)
            return (own,)


class Wide:
    halves = 1
    kept = 8

    def __init__(self, moves, place):
        self.moves, self.place = moves, place

    def scatter(self, grads, direct=False):
        return Wide.Sum(self.moves, grads, direct)

    class Sum(Direct.Sum):
        def __init__(self, moves, grads, direct):
            super().__init__(moves, grads, direct)
            self.steps = [s for s in self.steps if s != self.over_other]

        def over_two(self):
            send = self.add(self.keep[4:8], self.core[4:8])
            self.by = self.moves.y(send)
            self.got = (self.by,)
            return (send,)

        def over_z(self):
            sends = tuple(self.add(self.keep[i], self.core[i], self.by[i]) for i in (1, 2, 3))
            self.got = self.zs = tuple(move(send) for move, send in zip(self.moves.z, sends))
            return sends

        def over_z2(self):
            send = self.add(self.keep[2:4], self.core[2:4], self.by[2:4])
            self.z2 = self.moves.z[1](send)
            self.got = (self.z2,)
            return (send,)

        def over_z1(self):
            send = self.add(self.keep[1], self.core[1], self.by[1], self.z2[1])
            z1 = self.moves.z[0](send)
            self.zs = (self.z2[0], z1)
            self.got = (z1,)
            return (send,)

        def over_x(self):
            own = self.add(self.keep[0], self.core[0], self.by[0], *self.zs)
            other = self.moves.x_move(own)
            self.result = [own.astype(f32) + other.astype(f32)]
            self.got = (other,)
            return (own,)


class Plain:
    halves = 1
    kept = 1

    def __init__(self):
        self.place = jnp.zeros((1,), jnp.int32)
        self.tab = self.tab3 = jnp.zeros((2, 1), jnp.int32)
        self.wide = self

    def pack(self, arrays, gain):
        return pack(jnp.int32(0), arrays, gain, 1)

    def gather(self, blocks):
        first, *others = (
            [lax.all_gather(block, "shard", axis=0, tiled=True)[None]] for block in blocks
        )
        self.own2, self.own3 = others
        return first

    def with_core(self, own, *deps):
        return own

    def stage0(self):
        return ()

    def stage1(self, *deps):
        return ()

    stage3 = stage1

    def scatter(self, grads, direct=False):
        return Plain.Sum(grads)

    class Sum:
        got = ()

        def __init__(self, grads):
            self.grads = grads

        def step(self, *deps):
            return ()

        def finish(self):
            total = self.grads[0][0].astype(f32)
            part = lax.psum_scatter(total, "shard", scatter_dimension=0, tiled=True)
            return [lax.psum(part.astype(bf16), "rep")]


def columns(halves, start, width):
    step = width // len(halves)
    first = start // len(halves)
    return jnp.concatenate([h[:, first : first + step] for h in halves], 1).astype(f32)


def one_sequence(moves, x, docs, w1, cot, inner):
    cosine, sine = rope_tables(x.shape[0])
    q_marks, k_marks = marks(docs.reshape(-1, 1))
    halves, tab = moves.halves, moves.tab
    sends = moves.stage0()
    normed1, q, k, v = project(tab, w1, after(x, *sends), cosine, sine, halves)
    sends = moves.stage1(normed1)
    mixed, inv, exps = attend(q, k, v, after(q_marks, *sends), k_marks)
    sends = moves.stage3(mixed)
    w2 = moves.own2
    middle, normed2, hidden, slope_g, slope_u = ffn(
        tab, w2, after(x, *sends), mixed, inner, halves
    )
    w3 = moves.with_core(moves.own3, hidden)
    g3 = weight_grad(moves.wide, [([after(hidden, *moves.own3)], [cot])], "grad_down", row_steps=4)
    sum3 = moves.wide.scatter(g3)
    sum3.step(*g3, *w3)
    output, gg, gu = hidden_back(
        moves.tab3, w3, middle, after(hidden, *g3), slope_g, slope_u, cot, halves
    )
    sends = sum3.step(gg, *sum3.got)
    g2 = weight_grad(moves, [([after(normed2, *sends)], [gg, gu])], "grad_gate_up", chunks=2)
    sum2 = moves.scatter(g2)
    sum2.step(*g2)
    grad_middle, attn_grad, grad_mixed = middle_back(
        tab, w2, after(middle, *g2), gg, gu, cot, halves
    )
    due = (attn_grad, *sum3.got, *sum2.got)
    sends = sum3.step(*due)
    sends = (*sends, *sum2.step(*due))

    def back(call, sends):
        return attend_back(q, k, v, mixed, inv, exps, after(grad_mixed, *sends), cosine, sine, call)

    turned0 = back(0, sends)
    due = (*turned0[:1], *sum2.got, *sum3.got)
    sends = sum2.step(*due)
    sends = (*sends, *sum3.step(*due))
    g1 = weight_grad(
        moves,
        [([after(normed1, *sends)], turned0), ([mixed], [attn_grad])],
        "grad_qk_out",
        row_steps=2,
    )
    sum1 = moves.scatter(g1)
    due = (*g1, *sum2.got, *sum3.got)
    sum1.step(*due)
    sends = (*sum2.step(*due), *sum3.step(*due))
    sends = (*sends, *sum1.step(*sends, *sum1.got))
    turned1 = back(1, (*g1, *sends))
    due = (*turned1[:1], *sum1.got, *sum2.got)
    sends = sum1.step(*due)
    sends = (*sends, *sum2.step(*due))
    g0 = weight_grad(moves.wide, [([after(normed1, *sends)], turned1)], "grad_qkv_rest", row_steps=2)
    sum0 = moves.wide.scatter(g0, True)
    due = (*g0, *sum1.got, *sum2.got)
    sum0.step(*due)
    sends = (*sum1.step(*due), *sum2.step(*due))
    sends = (*sends, *sum0.step(*sends, *sum0.got))
    parts = [t[part] for part in range(3) for t in (turned0, turned1)]
    grad_input = input_grad(tab, w1, after(x, *g0, *sends), grad_middle, parts, halves)
    sums = (sum0, sum1, sum2, sum3)
    due = (grad_input, *sum2.got, *sum1.got, *sum0.got)
    for one in (sum0, sum1):
        one.step(*due)
    return output, grad_input, [s.finish() for s in sums]


def per_device(
    inputs,
    doc_ids,
    attn_gain,
    w_query,
    w_key,
    w_value,
    w_out,
    ffn_gain,
    w_gate,
    w_up,
    w_down,
    cotangent,
):
    batch_size, length, width = inputs.shape
    inner = w_gate.shape[1]
    replicas, members = lax.axis_size("rep"), lax.axis_size("shard")
    moves = Direct() if (replicas, members, batch_size) == (2, 16, 1) else Plain()
    gain1 = attn_gain.astype(f32)[:, None]
    gain2 = ffn_gain.astype(f32)[:, None]

    w1 = moves.gather(
        [
            moves.pack([(w, True) for w in (w_query, w_key, w_value)], gain1),
            moves.pack([(w_out, False), (w_gate, True), (w_up, True)], gain2),
            moves.pack([(w_down, False)], jnp.ones((w_down.shape[0], 1), f32)),
        ]
    )
    outputs, grad_inputs, sums = [], [], None
    for b in range(batch_size):
        output, grad_input, own = one_sequence(
            moves, inputs[b], doc_ids[b], w1, cotangent[b], inner
        )
        outputs.append(output)
        grad_inputs.append(grad_input)
        sums = own if sums is None else jax.tree.map(jnp.add, sums, own)
    s0, s1, s2, s3 = sums
    scale = 1.0 / (batch_size * replicas * members)
    down = columns(s3, 0, width)
    gate, up = columns(s2, 0, inner), columns(s2, inner, inner)
    shares = [width * count // sum(SPLIT) for count in SPLIT]
    out = columns(s1, 3 * shares[0], width)

    def head_columns(part):
        sources = [columns(s, part * share, share) for s, share in zip((s1, s0), shares)]
        return jnp.concatenate(
            [c[:, j * c.shape[1] // 2 : (j + 1) * c.shape[1] // 2] for j in range(2) for c in sources], 1
        )

    query, key, value = (head_columns(part) for part in range(3))

    def gain_grad(pairs):
        total = sum(jnp.sum(w.astype(f32) * g, 1) for w, g in pairs)
        return total * scale

    return (
        jnp.stack(outputs),
        jnp.stack(grad_inputs),
        gain_grad([(w_query, query), (w_key, key), (w_value, value)]),
        query * gain1 * scale,
        key * gain1 * scale,
        value * gain1 * scale,
        out * scale,
        gain_grad([(w_gate, gate), (w_up, up)]),
        gate * gain2 * scale,
        up * gain2 * scale,
        down * scale,
    )


def solution(mesh):
    row = P("shard", None)
    tokens = P(("rep", "shard"), None, None)
    return jax.shard_map(
        per_device,
        mesh=mesh,
        in_specs=(
            tokens, P(("rep", "shard"), None), P("shard"), row, row, row, row, P("shard"), row, row, row, tokens,
        ),
        out_specs=(tokens, tokens, P("shard"), row, row, row, row, P("shard"), row, row, row),
        check_vma=False,
    )
```

```python
import functools

import jax
import jax.numpy as jnp
import numpy as np
from jax import lax
from jax.experimental import pallas as pl
from jax.experimental.pallas import tpu as pltpu
from jax.sharding import PartitionSpec as P

H = 12
HD = 64
BLOCK = 256
MAX_DOC = 512

epsilon = 1e-06
rope_base = 10000.0
far = 1e30

bf16 = jnp.bfloat16
f32 = jnp.float32
MIB = 1 << 20
NN = (((1,), (0,)), ((), ()))
NT = (((1,), (1,)), ((), ()))
TN = (((0,), (0,)), ((), ()))


def dot(left, right, dims=NN):
    return lax.dot_general(left, right, dims, preferred_element_type=f32)


def params(mib=60):
    return pltpu.CompilerParams(vmem_limit_bytes=mib * MIB)


HINT = 1.0


def cost(flops, nbytes, trans=0):
    return pl.CostEstimate(
        flops=int(HINT * flops), bytes_accessed=int(HINT * nbytes), transcendentals=int(HINT * trans)
    )


ANY = pl.BlockSpec(memory_space=pl.ANY)


class WeightCopies:
    def __init__(self, pieces, tab_ref, dest, sem, start, width):
        self.pieces, self.tab, self.dest, self.sem = pieces, tab_ref, dest, sem
        self.start_col, self.width = start, width

    def each(self, act):
        for number, piece in enumerate(self.pieces):
            count, rows = piece.shape[0], piece.shape[1]

            def step(b, carry):
                index = number * count + b
                row = pl.multiple_of(self.tab[0, index] * rows, 16)
                col = pl.multiple_of(self.tab[1, index] * self.width, 128)
                act(
                    pltpu.make_async_copy(
                        piece.at[b, :, pl.ds(self.start_col, self.width)],
                        self.dest.at[pl.ds(row, rows), pl.ds(col, self.width)],
                        self.sem.at[index],
                    )
                )
                return carry

            lax.fori_loop(0, count, step, 0)

    def start(self):
        self.each(lambda copy: copy.start())

    def wait(self):
        self.each(lambda copy: copy.wait())


def load_weight(pieces, tab_ref, dest, sem):
    copies = WeightCopies(pieces, tab_ref, dest, sem, 0, pieces[0].shape[2])
    copies.start()
    copies.wait()


SPLIT = (2, 1)


def in_order(refs, half=0, halves=1):
    return jnp.concatenate(
        [
            ref[:, j * (ref.shape[1] // 2) : (j + 1) * (ref.shape[1] // 2)]
            for j in range(2)
            if j * halves // 2 == half
            for ref in refs
        ],
        1,
    )


def pair_of(call):
    first, count = sum(SPLIT[:call]), SPLIT[call]
    return lambda i: (0, first + i % count + sum(SPLIT) * (i // count))


def pack_kernel(half_ref, *refs, folded):
    *sources, gain_ref, out_ref = refs
    offset = 0
    for source, scaled in zip(sources, folded):
        width = source.shape[1]
        value = source[...]
        if scaled:
            value = (value.astype(f32) * gain_ref[...]).astype(bf16)
        out_ref[:, offset : offset + width] = value
        offset += width


def pack(half, arrays, gain, halves):
    folded = [scaled for _, scaled in arrays]
    arrays = [array for array, _ in arrays]
    rows = arrays[0].shape[0]
    columns = sum(array.shape[1] for array in arrays) // halves
    return pl.pallas_call(
        functools.partial(pack_kernel, folded=folded),
        grid_spec=pltpu.PrefetchScalarGridSpec(
            num_scalar_prefetch=1,
            grid=(1,),
            in_specs=[
                pl.BlockSpec((rows, array.shape[1] // halves), lambda i, h: (0, h[0])) for array in arrays
            ]
            + [pl.BlockSpec((rows, 1), lambda i, h: (0, 0))],
            out_specs=pl.BlockSpec((rows, columns), lambda i, h: (0, 0)),
        ),
        out_shape=jax.ShapeDtypeStruct((rows, columns), bf16),
        compiler_params=params(),
        cost_estimate=cost(rows * columns, 4 * rows * columns),
        name="pack",
    )(half.reshape(1), *arrays, gain)


def rope_tables(length):
    frequency = rope_base ** -(np.arange(HD // 2) * (2.0 / HD))
    coarse = np.arange(length // 32)[:, None] * 32.0 * frequency[None, :]
    fine = np.arange(32)[:, None] * frequency[None, :]
    coarse, fine = np.tile(coarse, (1, 4))[:, None, :], np.tile(fine, (1, 4))[None, :, :]
    sign = np.tile(np.repeat([-1.0, 1.0], HD // 2), 2)
    cos_a, sin_a = jnp.asarray(np.cos(coarse), f32), jnp.asarray(np.sin(coarse), f32)
    cos_b, sin_b = jnp.asarray(np.cos(fine), f32), jnp.asarray(np.sin(fine), f32)
    cosine = cos_a * cos_b - sin_a * sin_b
    sine = (sin_a * cos_b + cos_a * sin_b) * jnp.asarray(sign, f32)
    return cosine.reshape(length, 128), sine.reshape(length, 128)


def swap_halves(tensor):
    lane = lax.broadcasted_iota(jnp.int32, tensor.shape, 1)
    return jnp.where(
        (lane & (HD // 2)) == 0, pltpu.roll(tensor, 128 - HD // 2, 1), pltpu.roll(tensor, HD // 2, 1)
    )


def project_kernel(tab_ref, *refs, n_pieces, halves):
    pieces, (x_ref, cos_ref, sin_ref) = refs[:n_pieces], refs[n_pieces : n_pieces + 3]
    n_ref, q_ref, k_ref, v_ref, weight, sem = refs[n_pieces + 3 :]

    @pl.when(pl.program_id(0) == 0)
    def _():
        load_weight(pieces, tab_ref, weight, sem)

    x = x_ref[...].astype(f32)
    normed = (x * lax.rsqrt(jnp.mean(x * x, -1, keepdims=True) + epsilon)).astype(bf16)
    n_ref[...] = normed
    width = x_ref.shape[1] // halves
    cosine, sine = cos_ref[...], sin_ref[...]
    everything = dot(normed, weight[...])
    for half in range(halves):
        result = everything[:, 3 * half * width : 3 * (half + 1) * width]
        for part, out, scale in ((0, q_ref, HD**-0.5), (1, k_ref, 1.0)):
            for c in range(0, width, 128):
                piece = result[:, part * width + c : part * width + c + 128]
                turned = piece * cosine + swap_halves(piece) * sine
                out[:, half * width + c : half * width + c + 128] = (
                    turned.astype(bf16) * jnp.asarray(scale, bf16)
                )
        v_ref[:, half * width : (half + 1) * width] = result[:, 2 * width :].astype(bf16)


def project(tab, pieces, x, cosine, sine, halves):
    length, width = x.shape
    rows = BLOCK
    n = len(pieces)
    blocks = sum(p.shape[0] for p in pieces)
    block = pl.BlockSpec((rows, width), lambda i, t: (i, 0))
    table = pl.BlockSpec((rows, 128), lambda i, t: (i, 0))
    shape = jax.ShapeDtypeStruct((length, width), bf16)
    return pl.pallas_call(
        functools.partial(project_kernel, n_pieces=n, halves=halves),
        grid_spec=pltpu.PrefetchScalarGridSpec(
            num_scalar_prefetch=1,
            grid=(length // rows,),
            in_specs=[ANY] * n + [block, table, table],
            out_specs=[block] * 4,
            scratch_shapes=[
                pltpu.VMEM((width, 3 * width), bf16),
                pltpu.SemaphoreType.DMA((blocks,)),
            ],
        ),
        out_shape=[shape] * 4,
        compiler_params=params(),
        cost_estimate=cost(6 * length * width * width, 16 * length * width),
        name="project",
    )(tab, *pieces, x, cosine, sine)


def key_range(block):
    low = max(0, (block * BLOCK - (MAX_DOC - 1)) // BLOCK) if block * BLOCK > MAX_DOC - 1 else 0
    return low * BLOCK, (block + 1) * BLOCK


def marks(docs):
    lane = jnp.arange(128, dtype=jnp.int32)[None, :] % HD
    used = lane < 4
    same = docs == lane
    return (
        jnp.where(used & ~same, -far, 0.0).astype(bf16),
        jnp.where(used & same, 1.0, 0.0).astype(bf16),
    )


def pipeline(items, first, second, third, ahead=2):
    made = [first(item) for item in items[:ahead]]
    pending = None
    for i, item in enumerate(items):
        if i + ahead < len(items):
            made.append(first(items[i + ahead]))
        middle = second(item, made[i])
        made[i] = None
        if pending is not None:
            third(*pending)
        pending = (item, middle)
    third(*pending)


def attend_kernel(q_ref, k_ref, v_ref, qm_ref, km_ref, mixed_ref, inv_ref, e_ref):
    length = q_ref.shape[0]
    lane = lax.broadcasted_iota(jnp.int32, (length, 128), 1)
    front = lax.broadcasted_iota(jnp.int32, (BLOCK, 128), 1) < HD
    q, k, v = q_ref[...], k_ref[...], v_ref[...]
    ones = jnp.ones((length, 128), bf16)
    operands = []
    for head in range(2):
        own = (lane < HD) if head == 0 else (lane >= HD)
        operands.append(
            (jnp.where(own, q, qm_ref[...]), jnp.where(own, k, km_ref[...]), jnp.where(own, v, ones))
        )
    outs = {}

    def scores(item):
        block, head = item
        low, high = key_range(block)
        qa, ka, _ = operands[head]
        return dot(ka[low:high], qa[block * BLOCK : (block + 1) * BLOCK], NT)

    def softmax(item, values):
        block, head = item
        low, high = key_range(block)
        exps = jnp.exp(values - jnp.max(values, 0, keepdims=True)).astype(bf16)
        for kb in range(low // BLOCK, high // BLOCK):
            e_ref[head, kb, :, (block - kb) * BLOCK : (block - kb + 1) * BLOCK] = exps[
                kb * BLOCK - low : (kb + 1) * BLOCK - low
            ]
        return exps

    def mix(item, exps):
        block, head = item
        low, high = key_range(block)
        outs[head] = dot(exps, operands[head][2][low:high], TN)
        if head == 1:
            rows = slice(block * BLOCK, (block + 1) * BLOCK)
            value = jnp.where(front, outs[0], outs[1])
            total = jnp.where(front, outs[1], outs[0])
            inverse = pltpu.roll(1.0 / total, HD, 1)
            mixed_ref[rows, :] = (value * inverse).astype(bf16)
            inv_ref[rows, :] = inverse

    items = [(block, head) for block in range(length // BLOCK) for head in range(2)]
    pipeline(items, scores, softmax, mix)


def span(length):
    return min(length, MAX_DOC + BLOCK)


def attend(q, k, v, q_marks, k_marks):
    length, width = q.shape
    blocks = length // BLOCK
    pairs = width // 128
    column = pl.BlockSpec((length, 128), lambda i: (0, i))
    fixed = pl.BlockSpec((length, 128), lambda i: (0, 0))
    return pl.pallas_call(
        attend_kernel,
        grid=(pairs,),
        in_specs=[column, column, column, fixed, fixed],
        out_specs=[column, column, pl.BlockSpec((2, blocks, BLOCK, span(length)), lambda i: (i, 0, 0, 0))],
        out_shape=[
            jax.ShapeDtypeStruct((length, 128 * pairs), bf16),
            jax.ShapeDtypeStruct((length, 128 * pairs), f32),
            jax.ShapeDtypeStruct((2 * pairs, blocks, BLOCK, span(length)), bf16),
        ],
        compiler_params=params(),
        cost_estimate=cost(1280 * pairs * length * length, 3840 * pairs * length, 2 * pairs * length * length),
        name="attend",
    )(q, k, v, q_marks, k_marks)


def attend_back_kernel(
    q_ref, k_ref, v_ref, mixed_ref, inv_ref, e_ref, grad_ref, cos_ref, sin_ref,
    dq_ref, dk_ref, dv_ref, ds_ref,
):
    length = q_ref.shape[0]
    count = length // BLOCK
    lane = lax.broadcasted_iota(jnp.int32, (length, 128), 1)
    q, k, v = q_ref[...], k_ref[...], v_ref[...]
    zero = jnp.zeros((length, 128), bf16)
    scaled = grad_ref[...].astype(f32) * inv_ref[...]
    inner = scaled * mixed_ref[...].astype(f32)
    operands = []
    for head in range(2):
        own = (lane < HD) if head == 0 else (lane >= HD)
        first = HD if head == 0 else 0
        spare = (lane == first) | (lane == first + 1)
        minus = jnp.where(spare, -1.0, 0.0).astype(bf16)
        delta = jnp.sum(jnp.where(own, inner, 0.0), 1, keepdims=True)
        upper = delta.astype(bf16).astype(f32)
        masked = jnp.where(own, scaled, 0.0)
        joined = jnp.where(lane == first, upper, masked)
        joined = jnp.where(lane == first + 1, delta - upper, joined).astype(bf16)
        operands.append(
            (
                jnp.where(own, q, zero),
                jnp.where(own, k, zero),
                jnp.where(own, v, minus),
                masked.astype(bf16),
                joined,
            )
        )
    sums = {}

    def turn_back(value, rows):
        return (value * cos_ref[rows, :] - swap_halves(value) * sin_ref[rows, :]).astype(bf16)

    def slopes(item):
        block, head = item
        low, high = key_range(block)
        return dot(
            operands[head][2][low:high], operands[head][4][block * BLOCK : (block + 1) * BLOCK], NT
        )

    def products(item, slope):
        block, head = item
        low, high = key_range(block)
        parts = []
        for kb in range(low // BLOCK, high // BLOCK):
            cols = slice((block - kb) * BLOCK, (block - kb + 1) * BLOCK)
            part = e_ref[head, kb, :, cols].astype(f32) * slope[kb * BLOCK - low : (kb + 1) * BLOCK - low]
            part = part.astype(bf16)
            ds_ref[head, kb, :, cols] = part
            parts.append(part)
        return jnp.concatenate(parts, 0)

    def finish(item, ds):
        block, head = item
        low, high = key_range(block)
        rows = slice(block * BLOCK, (block + 1) * BLOCK)
        part = dot(ds, operands[head][1][low:high], TN)
        if head == 0:
            sums["q"] = part
        else:
            dq_ref[rows, :] = turn_back((sums["q"] + part) * (HD**-0.5), rows)
        for kb in range(count):
            if max(b for b in range(count) if key_range(b)[0] <= kb * BLOCK) != block:
                continue
            width = (block - kb + 1) * BLOCK
            seen = slice(kb * BLOCK, kb * BLOCK + width)
            keys = slice(kb * BLOCK, (kb + 1) * BLOCK)
            dv = dot(e_ref[head, kb, :, 0:width], operands[head][3][seen])
            dk = dot(ds_ref[head, kb, :, 0:width], operands[head][0][seen])
            if head == 0:
                sums[kb] = (dv, dk)
            else:
                dv_ref[keys, :] = (sums[kb][0] + dv).astype(bf16)
                dk_ref[keys, :] = turn_back(sums[kb][1] + dk, keys)

    items = [(block, head) for block in range(count) for head in range(2)]
    pipeline(items, slopes, products, finish)


def attend_back(q, k, v, mixed, inv, exps, grad, cosine, sine, call):
    length = q.shape[0]
    pairs = 2 * SPLIT[call]
    column = pl.BlockSpec((length, 128), pair_of(call))
    part = pl.BlockSpec((length, 128), lambda i: (0, i))
    fixed = pl.BlockSpec((length, 128), lambda i: (0, 0))
    shape = jax.ShapeDtypeStruct((length, 128 * pairs), bf16)
    return pl.pallas_call(
        attend_back_kernel,
        grid=(pairs,),
        in_specs=[column] * 5
        + [
            pl.BlockSpec((2,) + exps.shape[1:], lambda i: (pair_of(call)(i)[1], 0, 0, 0)),
            column,
            fixed,
            fixed,
        ],
        out_specs=[part] * 3,
        out_shape=[shape] * 3,
        scratch_shapes=[pltpu.VMEM((2,) + exps.shape[1:], bf16)],
        compiler_params=params(54),
        cost_estimate=cost(2560 * pairs * length * length, 4608 * pairs * length),
        name="attend_back",
    )(q, k, v, mixed, inv, exps, grad, cosine, sine)


def ffn_kernel(tab_ref, *refs, n_pieces, halves):
    pieces, (x_ref, mixed_ref), refs = refs[:n_pieces], refs[n_pieces : n_pieces + 2], refs[n_pieces + 2 :]
    middle_ref, normed_ref, hidden_ref, slope_g_ref, slope_u_ref, w_out, w_in, sem = refs
    width = x_ref.shape[1] // halves
    inner = hidden_ref.shape[1] // halves
    early = WeightCopies(pieces, tab_ref, w_out, sem.at[0], 0, width)
    late = WeightCopies(pieces, tab_ref, w_in, sem.at[1], width, 2 * inner)

    @pl.when(pl.program_id(0) == 0)
    def _():
        early.start()
        late.start()
        early.wait()

    middle = x_ref[...].astype(f32) + dot(mixed_ref[...], w_out[...])
    middle_ref[...] = middle
    normed = (middle * lax.rsqrt(jnp.mean(middle * middle, -1, keepdims=True) + epsilon)).astype(bf16)
    normed_ref[...] = normed

    @pl.when(pl.program_id(0) == 0)
    def _():
        late.wait()

    step = min(256, inner)

    def dots(first):
        return (
            dot(normed, w_in[:, first : first + step]),
            dot(normed, w_in[:, first + inner : first + inner + step]),
        )

    def activate(first, values):
        gate, up = values
        half_tanh = 0.5 * jnp.tanh(0.5 * gate)
        sigmoid = half_tanh + 0.5
        silu = gate * sigmoid
        cols = slice(first - first // (2 * inner) * inner, first - first // (2 * inner) * inner + step)
        hidden_ref[:, cols] = (silu * up).astype(bf16)
        slope_u_ref[:, cols] = silu.astype(bf16)
        slope_g_ref[:, cols] = (up * (sigmoid + silu * (0.5 - half_tanh))).astype(bf16)

    items = [2 * h * inner + c for h in range(halves) for c in range(0, inner, step)]
    pipeline(items, dots, activate, lambda *_: None)


def ffn(tab, pieces, x, mixed, inner, halves):
    length, width = x.shape
    rows = BLOCK
    n = len(pieces)
    blocks = sum(p.shape[0] for p in pieces)
    narrow = pl.BlockSpec((rows, width), lambda i, t: (i, 0))
    wide = pl.BlockSpec((rows, inner), lambda i, t: (i, 0))
    wide_shape = jax.ShapeDtypeStruct((length, inner), bf16)
    return pl.pallas_call(
        functools.partial(ffn_kernel, n_pieces=n, halves=halves),
        grid_spec=pltpu.PrefetchScalarGridSpec(
            num_scalar_prefetch=1,
            grid=(length // rows,),
            in_specs=[ANY] * n + [narrow, narrow],
            out_specs=[narrow, narrow, wide, wide, wide],
            scratch_shapes=[
                pltpu.VMEM((width, width), bf16),
                pltpu.VMEM((width, 2 * inner), bf16),
                pltpu.SemaphoreType.DMA((2, blocks)),
            ],
        ),
        out_shape=[
            jax.ShapeDtypeStruct((length, width), f32),
            jax.ShapeDtypeStruct((length, width), bf16),
            wide_shape,
            wide_shape,
            wide_shape,
        ],
        compiler_params=params(),
        cost_estimate=cost(2 * length * width * (width + 2 * inner), 8 * width * inner + 8 * length * inner),
        name="ffn",
    )(tab, *pieces, x, mixed)


def hidden_back_kernel(tab_ref, *refs, n_pieces, halves):
    pieces = refs[:n_pieces]
    middle_ref, hidden_ref, slope_g_ref, slope_u_ref, cot_ref = refs[n_pieces : n_pieces + 5]
    output_ref, gg_ref, gu_ref, weight, sem = refs[n_pieces + 5 :]

    @pl.when(pl.program_id(0) == 0)
    def _():
        load_weight(pieces, tab_ref, weight, sem)

    inner = hidden_ref.shape[1]
    step = min(512, inner)
    cot = cot_ref[...]
    for c in range(0, inner, step):
        cols = slice(c, c + step)
        grad_hidden = dot(cot, weight[cols, :], NT)
        gg_ref[:, cols] = (grad_hidden * slope_g_ref[:, cols].astype(f32)).astype(bf16)
        gu_ref[:, cols] = (grad_hidden * slope_u_ref[:, cols].astype(f32)).astype(bf16)
    output_ref[...] = (middle_ref[...] + dot(hidden_ref[...], weight[...])).astype(bf16)


def hidden_back(tab, pieces, middle, hidden, slope_g, slope_u, cot, halves):
    length, width = middle.shape
    inner = hidden.shape[1]
    rows = BLOCK
    n = len(pieces)
    narrow = pl.BlockSpec((rows, width), lambda i, t: (i, 0))
    wide = pl.BlockSpec((rows, inner), lambda i, t: (i, 0))
    wide_low = jax.ShapeDtypeStruct((length, inner), bf16)
    return pl.pallas_call(
        functools.partial(hidden_back_kernel, n_pieces=n, halves=halves),
        grid_spec=pltpu.PrefetchScalarGridSpec(
            num_scalar_prefetch=1,
            grid=(length // rows,),
            in_specs=[ANY] * n + [narrow, wide, wide, wide, narrow],
            out_specs=[narrow, wide, wide],
            scratch_shapes=[
                pltpu.VMEM((inner, width), bf16),
                pltpu.SemaphoreType.DMA((sum(p.shape[0] for p in pieces),)),
            ],
        ),
        out_shape=[jax.ShapeDtypeStruct((length, width), bf16), wide_low, wide_low],
        compiler_params=params(),
        cost_estimate=cost(4 * length * width * inner, 2 * width * inner + 12 * length * inner),
        name="hidden_back",
    )(tab, *pieces, middle, hidden, slope_g, slope_u, cot)


def middle_back_kernel(tab_ref, *refs, n_pieces, halves):
    pieces = refs[:n_pieces]
    middle_ref, gg_ref, gu_ref, cot_ref = refs[n_pieces : n_pieces + 4]
    grad_middle_ref, attn_grad_ref, grad_mixed_ref, w_out, w_in, sem = refs[n_pieces + 4 :]
    width = cot_ref.shape[1] // halves
    inner = gg_ref.shape[1] // halves
    early = WeightCopies(pieces, tab_ref, w_in, sem.at[0], width, 2 * inner)
    late = WeightCopies(pieces, tab_ref, w_out, sem.at[1], 0, width)

    @pl.when(pl.program_id(0) == 0)
    def _():
        early.start()
        late.start()
        early.wait()
        late.wait()

    def gradient(rows):
        both = [
            ref[rows, h * inner : (h + 1) * inner] for h in range(halves) for ref in (gg_ref, gu_ref)
        ]
        return dot(jnp.concatenate(both, 1), w_in[...], NT)

    def norm_back(rows, grad):
        middle = middle_ref[rows, :]
        inverse = lax.rsqrt(jnp.mean(middle * middle, -1, keepdims=True) + epsilon)
        normed = middle * inverse
        grad_middle = cot_ref[rows, :].astype(f32) + inverse * (
            grad - normed * jnp.mean(grad * normed, -1, keepdims=True)
        )
        grad_middle_ref[rows, :] = grad_middle
        low = grad_middle.astype(bf16)
        attn_grad_ref[rows, :] = low
        return low

    def mixed_grad(rows, low):
        grad_mixed_ref[rows, :] = dot(low, w_out[...], NT).astype(bf16)

    total = middle_ref.shape[0]
    items = [slice(r, r + SUB) for r in range(0, total, SUB)]
    pipeline(items, gradient, norm_back, mixed_grad, 1)


SUB = 256
MB_ROWS = 256


def middle_back(tab, pieces, middle, gg, gu, cot, halves):
    length, width = middle.shape
    inner = gg.shape[1]
    rows = MB_ROWS
    n = len(pieces)
    narrow = pl.BlockSpec((rows, width), lambda i, t: (i, 0))
    wide = pl.BlockSpec((rows, inner), lambda i, t: (i, 0))
    low = jax.ShapeDtypeStruct((length, width), bf16)
    return pl.pallas_call(
        functools.partial(middle_back_kernel, n_pieces=n, halves=halves),
        grid_spec=pltpu.PrefetchScalarGridSpec(
            num_scalar_prefetch=1,
            grid=(length // rows,),
            in_specs=[ANY] * n + [narrow, wide, wide, narrow],
            out_specs=[narrow] * 3,
            scratch_shapes=[
                pltpu.VMEM((width, width), bf16),
                pltpu.VMEM((width, 2 * inner), bf16),
                pltpu.SemaphoreType.DMA((2, sum(p.shape[0] for p in pieces))),
            ],
        ),
        out_shape=[jax.ShapeDtypeStruct((length, width), f32), low, low],
        compiler_params=params(),
        cost_estimate=cost(
            2 * length * width * (width + 2 * inner), 4 * width * inner + 4 * length * inner
        ),
        name="middle_back",
    )(tab, *pieces, middle, gg, gu, cot)


def input_kernel(tab_ref, *refs, n_pieces, halves):
    pieces = refs[:n_pieces]
    x_ref, grad_middle_ref = refs[n_pieces : n_pieces + 2]
    calls = len(SPLIT)
    parts = refs[n_pieces + 2 : n_pieces + 2 + 3 * calls]
    out_ref, weight, sem = refs[n_pieces + 2 + 3 * calls :]

    @pl.when(pl.program_id(0) == 0)
    def _():
        load_weight(pieces, tab_ref, weight, sem)

    left = [
        in_order(parts[part * calls : (part + 1) * calls], h, halves)
        for h in range(halves)
        for part in range(3)
    ]
    grad = dot(jnp.concatenate(left, 1), weight[...], NT)
    x = x_ref[...].astype(f32)
    inverse = lax.rsqrt(jnp.mean(x * x, -1, keepdims=True) + epsilon)
    normed = x * inverse
    out_ref[...] = grad_middle_ref[...] + inverse * (
        grad - normed * jnp.mean(grad * normed, -1, keepdims=True)
    )


def input_grad(tab, pieces, x, grad_middle, parts, halves):
    length, width = x.shape
    rows = BLOCK
    n = len(pieces)
    blocks = sum(p.shape[0] for p in pieces)
    block = pl.BlockSpec((rows, width), lambda i, t: (i, 0))
    shares = [pl.BlockSpec((rows, p.shape[1]), lambda i, t: (i, 0)) for p in parts]
    return pl.pallas_call(
        functools.partial(input_kernel, n_pieces=n, halves=halves),
        grid_spec=pltpu.PrefetchScalarGridSpec(
            num_scalar_prefetch=1,
            grid=(length // rows,),
            in_specs=[ANY] * n + [block] * 2 + shares,
            out_specs=block,
            scratch_shapes=[
                pltpu.VMEM((width, 3 * width), bf16),
                pltpu.SemaphoreType.DMA((blocks,)),
            ],
        ),
        out_shape=jax.ShapeDtypeStruct((length, width), f32),
        compiler_params=params(),
        cost_estimate=cost(6 * length * width * width, 20 * length * width),
        name="input_grad",
    )(tab, *pieces, x, grad_middle, *parts)


def weight_kernel(tab_ref, *refs, counts, block_rows, chunks, halves):
    n_left, n_right = sum(n for n, _ in counts), sum(n for _, n in counts)
    lefts, rights = list(refs[:n_left]), list(refs[n_left : n_left + n_right])
    keep_ref, send_ref, held, sem = refs[n_left + n_right :]
    step, steps = pl.program_id(0), pl.num_programs(0)
    slot = lax.rem(step, 2)
    here = halves if chunks == 0 else 1
    parts = max(1, chunks)
    rows = held.shape[2]
    kept = keep_ref.shape[0]
    widths = [r.shape[1] // here for r in rights]
    sizes = [sum(widths)] if parts == 1 else widths

    def pieces():
        for b in range(rows // block_rows):
            for h in range(here):
                offset = 0
                for i, width in enumerate(sizes):
                    yield b, h, (b * here + h) * len(sizes) + i, offset, width
                    offset += width

    def wait(which):
        for _, h, number, offset, width in pieces():
            pltpu.make_async_copy(
                held.at[which, h, pl.ds(0, block_rows), pl.ds(offset, width)],
                keep_ref.at[0, :, pl.ds(offset, width)],
                sem.at[which, number],
            ).wait()

    @pl.when(step >= 2)
    def _():
        wait(slot)

    offset = 0
    for _, n_right in counts:
        left = lefts.pop(0)[...]
        group = [rights.pop(0)[...] for _ in range(n_right)]
        result = dot(left, jnp.concatenate(group, 1), TN).astype(bf16)
        column = 0
        for right in group:
            width = right.shape[1] // here
            for h in range(here):
                held[slot, h, :, offset : offset + width] = result[:, column : column + width]
                column += width
            offset += width
    if chunks == 0:
        first, half, chunk = step * (rows // block_rows), 0, 0
    else:
        first, half, chunk = 0, step // chunks, lax.rem(step, chunks)
    def send_out(parity):
        for b, h, number, offset, width in pieces():
            place = tab_ref[(first + b) * halves + half + h]
            if b % 2 == parity:
                target = keep_ref.at[place]
            else:
                target = send_ref.at[place - kept]
            pltpu.make_async_copy(
                held.at[slot, h, pl.ds(b * block_rows, block_rows), pl.ds(offset, width)],
                target.at[:, pl.ds(pl.multiple_of(offset * parts + chunk * width, 128), width)],
                sem.at[slot, number],
            ).start()

    for parity in range(2):
        pl.when((tab_ref[0] < kept) == (parity == 0))(functools.partial(send_out, parity))

    @pl.when(step == steps - 1)
    def _():
        wait(slot)

        @pl.when(steps > 1)
        def _():
            wait(1 - slot)


def weight_grad(moves, products, name, chunks=0, row_steps=1):
    lefts = [left for group, _ in products for left in group]
    rights = [right for _, group in products for right in group]
    counts = [(len(left), len(right)) for left, right in products]
    length = lefts[0].shape[0]
    rows = sum(left.shape[1] for left in products[0][0])
    halves, blocks = moves.halves, moves.place.shape[0]
    block_rows = rows * halves // blocks
    columns = sum(r.shape[1] for r in rights) // halves
    kept = moves.kept
    sent = max(1, blocks - kept)
    if blocks == 1 and chunks == 0:
        row_steps = 1
    steps = halves * chunks if chunks else row_steps
    here = 1 if chunks else halves
    step_rows = rows if chunks else rows // row_steps
    n_pieces = step_rows // block_rows * here * (len(rights) if chunks > 1 else 1)
    if chunks:
        left_specs = [pl.BlockSpec(left.shape, lambda i, t: (0, 0)) for left in lefts]
        right_specs = [pl.BlockSpec((length, r.shape[1] // steps), lambda i, t: (0, i)) for r in rights]
    else:
        left_specs = [
            pl.BlockSpec((length, left.shape[1] // row_steps), lambda i, t: (0, i)) for left in lefts
        ]
        right_specs = [pl.BlockSpec(r.shape, lambda i, t: (0, 0)) for r in rights]
    return pl.pallas_call(
        functools.partial(
            weight_kernel, counts=counts, block_rows=block_rows, chunks=chunks, halves=halves
        ),
        grid_spec=pltpu.PrefetchScalarGridSpec(
            num_scalar_prefetch=1,
            grid=(steps,),
            in_specs=left_specs + right_specs,
            out_specs=[ANY, ANY],
            scratch_shapes=[
                pltpu.VMEM((2, here, step_rows, columns // max(1, chunks)), bf16),
                pltpu.SemaphoreType.DMA((2, n_pieces)),
            ],
        ),
        out_shape=[
            jax.ShapeDtypeStruct((kept, block_rows, columns), bf16),
            jax.ShapeDtypeStruct((sent, block_rows, columns), bf16),
        ],
        compiler_params=params(54),
        cost_estimate=cost(
            2 * length * rows * columns * halves,
            2 * (length * rows + length * columns * halves + rows * columns * halves),
        ),
        name=name,
    )(moves.place, *lefts, *rights)


def after(value, *others):
    return lax.optimization_barrier((value, others))[0]


def place_of(xr, yr, zr, cr):
    low = xr * 4 + yr * 2 + zr
    high = 8 + yr * 4 + xr * 2 + (zr - 2)
    return cr * 16 + jnp.where(zr < 2, low, high)


def swapped(bits, axis="shard"):
    count = lax.axis_size(axis)
    pairs = [(i, i ^ bits) for i in range(count)]
    return lambda array: lax.ppermute(array, axis, pairs)


class Direct:
    halves = 2
    kept = 16

    def __init__(self):
        self.me = lax.axis_index("shard")
        self.x = lax.axis_index("rep")
        self.core, self.y, self.x_move = swapped(1), swapped(2), swapped(1, "rep")
        self.z = [swapped(4), swapped(8), swapped(12)]
        shard = jnp.arange(16, dtype=jnp.int32)[:, None]
        half = jnp.arange(2, dtype=jnp.int32)[None, :]
        rel = shard ^ self.me
        place = place_of(half ^ self.x, (rel >> 1) & 1, rel >> 2, rel & 1)
        self.place = place.reshape(32)
        order = []
        for cr in range(2):
            for zs in ((0, 1), (2, 3)):
                for outer in range(2):
                    for inner in range(2):
                        for zr in zs:
                            xr, yr = (outer, inner) if zs[0] == 0 else (inner, outer)
                            order.append((zr * 4 + yr * 2 + cr, xr))
        rel_shard = jnp.array([o[0] for o in order], jnp.int32)
        rel_half = jnp.array([o[1] for o in order], jnp.int32)
        self.tab = jnp.stack([rel_shard ^ self.me, rel_half ^ self.x])
        order = [(zr * 4 + yr * 2 + cr, xr) for cr in range(2) for xr in range(2) for yr in range(2) for zr in range(4)]
        rel_shard = jnp.array([o[0] for o in order], jnp.int32)
        rel_half = jnp.array([o[1] for o in order], jnp.int32)
        self.tab3 = jnp.stack([rel_shard ^ self.me, rel_half ^ self.x])
        rel = rel[:, 0]
        self.wide = Wide(self, (rel & 1) * 8 + ((rel >> 1) & 1) * 4 + (rel >> 2))

    def xy(self, array):
        pairs = [(i, i ^ 18) for i in range(32)]
        return lax.ppermute(array, ("rep", "shard"), pairs)

    def pack(self, arrays, gain):
        return pack(self.x, arrays, gain, 2)

    def along_z(self, own):
        z1, z2, z3 = (move(own) for move in self.z)
        return jnp.concatenate([own, z1], 0), jnp.concatenate([z2, z3], 0), (z1, z2, z3)

    def one_axis(self, a, b):
        ay, bx = self.y(a), self.x_move(b)
        return (a, ay), (b, bx)

    def rest(self, a, b):
        ax, by = self.x_move(a), self.y(b)
        return [a, ax, b, by]

    def with_core(self, own, *deps):
        own = [after(p, *deps) for p in own] if deps else own
        return own + [self.core(p) for p in own]

    def gather(self, blocks):
        first, second, third = (block[None] for block in blocks)
        a1, b1, z_done1 = self.along_z(first)
        a2, b2, z_done2 = self.along_z(after(second, *z_done1))
        a1, b1 = self.one_axis(a1, b1)
        a1, b1 = jnp.concatenate(a1, 0), jnp.concatenate(b1, 0)
        own1 = self.rest(a1, b1)
        w1 = self.with_core(own1)
        self.a2, self.b2 = after(a2, *own1), after(b2, *own1)
        self.third = after(third, *z_done2, *own1)
        return w1

    def stage0(self):
        self.pair2 = self.one_axis(self.a2, self.b2)
        self.z3 = self.z[0](self.third)
        return self.a2, self.b2, self.third

    def stage1(self, *deps):
        (a, ay), (b, bx) = self.pair2
        deps = (*deps, self.z3, ay, bx)
        a = jnp.concatenate([after(a, *deps), ay], 0)
        b = jnp.concatenate([after(b, *deps), bx], 0)
        a3 = jnp.concatenate([after(self.third, *deps), self.z3], 0)
        self.a3, self.b3 = a3, self.z[1](a3)
        self.own2 = self.rest(a, b)
        self.core2 = [self.core(a), None, self.core(b), None]
        return a, b, a3

    def stage3(self, *deps):
        deps = (*deps, *self.own2, self.b3, self.core2[0], self.core2[2])
        block = jnp.concatenate([after(self.a3, *deps), after(self.b3, *deps)], 0)
        self.own3 = [block, self.y(block), self.x_move(block), self.xy(block)]
        for i in (1, 3):
            self.core2[i] = self.core(after(self.own2[i], *deps, block))
        self.own2 += self.core2
        return (block,)

    def scatter(self, grads, direct=False):
        return Direct.Sum(self, grads, direct)

    class Sum:
        def __init__(self, moves, grads, direct):
            self.moves = moves
            self.keep, self.send = grads
            over_z = [self.over_z] if direct else [self.over_z2, self.over_z1]
            self.steps = [self.over_core, self.over_two, self.over_other, *over_z, self.over_x]
            self.start = self.steps[0]
            self.got = ()

        def step(self, *deps):
            if deps:
                self.keep = after(self.keep, *deps)
                if self.steps[0] == self.start:
                    self.send = after(self.send, *deps)
            return self.steps.pop(0)()

        def finish(self):
            while self.steps:
                self.step()
            return self.result

        @staticmethod
        def add(*terms):
            total = terms[0].astype(f32)
            for term in terms[1:]:
                total = total + term.astype(f32)
            return total.astype(bf16)

        def over_core(self):
            self.core = self.moves.core(self.send)
            self.got = (self.core,)
            return (self.send,)

        def over_two(self):
            keep, core = self.keep, self.core
            to_x, to_y = self.add(keep[4:8], core[4:8]), self.add(keep[12:16], core[12:16])
            self.ax, self.by = self.got = self.moves.x_move(to_x), self.moves.y(to_y)
            return to_x, to_y

        def over_other(self):
            keep, core, ax, by = self.keep, self.core, self.ax, self.by
            to_y = self.add(keep[2:4], core[2:4], ax[2:4])
            to_x = self.add(keep[10:12], core[10:12], by[2:4])
            self.ay, self.bx = self.got = self.moves.y(to_y), self.moves.x_move(to_x)
            return to_y, to_x

        def over_z(self):
            keep, core, ax, by, ay, bx = self.keep, self.core, self.ax, self.by, self.ay, self.bx
            sends = (
                self.add(keep[1], core[1], ax[1], ay[1]),
                self.add(keep[8], core[8], by[0], bx[0]),
                self.add(keep[9], core[9], by[1], bx[1]),
            )
            self.got = self.zs = tuple(move(send) for move, send in zip(self.moves.z, sends))
            return sends

        def over_z2(self):
            keep, core = self.keep, self.core
            send = self.add(keep[8:10], core[8:10], self.by[0:2], self.bx[0:2])
            self.z2 = self.moves.z[1](send)
            self.got = (self.z2,)
            return (send,)

        def over_z1(self):
            send = self.add(self.keep[1], self.core[1], self.ax[1], self.ay[1], self.z2[1])
            z1 = self.moves.z[0](send)
            self.zs = (self.z2[0], z1)
            self.got = (z1,)
            return (send,)

        def over_x(self):
            own = self.add(self.keep[0], self.core[0], self.ax[0], self.ay[0], *self.zs)
            other = self.moves.x_move(own)
            first = self.moves.x == 0
            self.result = [jnp.where(first, own, other), jnp.where(first, other, own)]
            self.got = (other,)
            return (own,)


class Wide:
    halves = 1
    kept = 8

    def __init__(self, moves, place):
        self.moves, self.place = moves, place

    def scatter(self, grads, direct=False):
        return Wide.Sum(self.moves, grads, direct)

    class Sum(Direct.Sum):
        def __init__(self, moves, grads, direct):
            super().__init__(moves, grads, direct)
            self.steps = [s for s in self.steps if s != self.over_other]

        def over_two(self):
            send = self.add(self.keep[4:8], self.core[4:8])
            self.by = self.moves.y(send)
            self.got = (self.by,)
            return (send,)

        def over_z(self):
            sends = tuple(self.add(self.keep[i], self.core[i], self.by[i]) for i in (1, 2, 3))
            self.got = self.zs = tuple(move(send) for move, send in zip(self.moves.z, sends))
            return sends

        def over_z2(self):
            send = self.add(self.keep[2:4], self.core[2:4], self.by[2:4])
            self.z2 = self.moves.z[1](send)
            self.got = (self.z2,)
            return (send,)

        def over_z1(self):
            send = self.add(self.keep[1], self.core[1], self.by[1], self.z2[1])
            z1 = self.moves.z[0](send)
            self.zs = (self.z2[0], z1)
            self.got = (z1,)
            return (send,)

        def over_x(self):
            own = self.add(self.keep[0], self.core[0], self.by[0], *self.zs)
            other = self.moves.x_move(own)
            self.result = [own.astype(f32) + other.astype(f32)]
            self.got = (other,)
            return (own,)


class Plain:
    halves = 1
    kept = 1

    def __init__(self):
        self.place = jnp.zeros((1,), jnp.int32)
        self.tab = self.tab3 = jnp.zeros((2, 1), jnp.int32)
        self.wide = self

    def pack(self, arrays, gain):
        return pack(jnp.int32(0), arrays, gain, 1)

    def gather(self, blocks):
        first, *others = (
            [lax.all_gather(block, "shard", axis=0, tiled=True)[None]] for block in blocks
        )
        self.own2, self.own3 = others
        return first

    def with_core(self, own, *deps):
        return own

    def stage0(self):
        return ()

    def stage1(self, *deps):
        return ()

    stage3 = stage1

    def scatter(self, grads, direct=False):
        return Plain.Sum(grads)

    class Sum:
        got = ()

        def __init__(self, grads):
            self.grads = grads

        def step(self, *deps):
            return ()

        def finish(self):
            total = self.grads[0][0].astype(f32)
            part = lax.psum_scatter(total, "shard", scatter_dimension=0, tiled=True)
            return [lax.psum(part.astype(bf16), "rep")]


def columns(halves, start, width):
    step = width // len(halves)
    first = start // len(halves)
    return jnp.concatenate([h[:, first : first + step] for h in halves], 1).astype(f32)


def one_sequence(moves, x, docs, w1, cot, inner):
    cosine, sine = rope_tables(x.shape[0])
    q_marks, k_marks = marks(docs.reshape(-1, 1))
    halves, tab = moves.halves, moves.tab
    sends = moves.stage0()
    normed1, q, k, v = project(tab, w1, after(x, *sends), cosine, sine, halves)
    sends = moves.stage1(normed1)
    mixed, inv, exps = attend(q, k, v, after(q_marks, *sends), k_marks)
    sends = moves.stage3(mixed)
    w2 = moves.own2
    middle, normed2, hidden, slope_g, slope_u = ffn(
        tab, w2, after(x, *sends), mixed, inner, halves
    )
    w3 = moves.with_core(moves.own3, hidden)
    g3 = weight_grad(moves.wide, [([after(hidden, *moves.own3)], [cot])], "grad_down", row_steps=4)
    sum3 = moves.wide.scatter(g3)
    sum3.step(*g3, *w3)
    output, gg, gu = hidden_back(
        moves.tab3, w3, middle, after(hidden, *g3), slope_g, slope_u, cot, halves
    )
    sends = sum3.step(gg, *sum3.got)
    g2 = weight_grad(moves, [([after(normed2, *sends)], [gg, gu])], "grad_gate_up", chunks=2)
    sum2 = moves.scatter(g2)
    sum2.step(*g2)
    grad_middle, attn_grad, grad_mixed = middle_back(
        tab, w2, after(middle, *g2), gg, gu, cot, halves
    )
    due = (attn_grad, *sum3.got, *sum2.got)
    sends = sum3.step(*due)
    sends = (*sends, *sum2.step(*due))

    def back(call, sends):
        return attend_back(q, k, v, mixed, inv, exps, after(grad_mixed, *sends), cosine, sine, call)

    turned0 = back(0, sends)
    due = (*turned0[:1], *sum2.got, *sum3.got)
    sends = sum2.step(*due)
    sends = (*sends, *sum3.step(*due))
    g1 = weight_grad(
        moves,
        [([after(normed1, *sends)], turned0), ([mixed], [attn_grad])],
        "grad_qk_out",
        row_steps=2,
    )
    sum1 = moves.scatter(g1)
    due = (*g1, *sum2.got, *sum3.got)
    sum1.step(*due)
    sends = (*sum2.step(*due), *sum3.step(*due))
    sends = (*sends, *sum1.step(*sends, *sum1.got))
    turned1 = back(1, (*g1, *sends))
    due = (*turned1[:1], *sum1.got, *sum2.got)
    sends = sum1.step(*due)
    sends = (*sends, *sum2.step(*due))
    g0 = weight_grad(moves.wide, [([after(normed1, *sends)], turned1)], "grad_qkv_rest", row_steps=2)
    sum0 = moves.wide.scatter(g0, True)
    due = (*g0, *sum1.got, *sum2.got)
    sum0.step(*due)
    sends = (*sum1.step(*due), *sum2.step(*due))
    sends = (*sends, *sum0.step(*sends, *sum0.got))
    parts = [t[part] for part in range(3) for t in (turned0, turned1)]
    grad_input = input_grad(tab, w1, after(x, *g0, *sends), grad_middle, parts, halves)
    sums = (sum0, sum1, sum2, sum3)
    due = (grad_input, *sum2.got, *sum1.got, *sum0.got)
    for one in (sum0, sum1):
        one.step(*due)
    return output, grad_input, [s.finish() for s in sums]


def per_device(
    inputs,
    doc_ids,
    attn_gain,
    w_query,
    w_key,
    w_value,
    w_out,
    ffn_gain,
    w_gate,
    w_up,
    w_down,
    cotangent,
):
    batch_size, length, width = inputs.shape
    inner = w_gate.shape[1]
    replicas, members = lax.axis_size("rep"), lax.axis_size("shard")
    moves = Direct() if (replicas, members, batch_size) == (2, 16, 1) else Plain()
    gain1 = attn_gain.astype(f32)[:, None]
    gain2 = ffn_gain.astype(f32)[:, None]

    w1 = moves.gather(
        [
            moves.pack([(w, True) for w in (w_query, w_key, w_value)], gain1),
            moves.pack([(w_out, False), (w_gate, True), (w_up, True)], gain2),
            moves.pack([(w_down, False)], jnp.ones((w_down.shape[0], 1), f32)),
        ]
    )
    outputs, grad_inputs, sums = [], [], None
    for b in range(batch_size):
        output, grad_input, own = one_sequence(
            moves, inputs[b], doc_ids[b], w1, cotangent[b], inner
        )
        outputs.append(output)
        grad_inputs.append(grad_input)
        sums = own if sums is None else jax.tree.map(jnp.add, sums, own)
    s0, s1, s2, s3 = sums
    scale = 1.0 / (batch_size * replicas * members)
    down = columns(s3, 0, width)
    gate, up = columns(s2, 0, inner), columns(s2, inner, inner)
    shares = [width * count // sum(SPLIT) for count in SPLIT]
    out = columns(s1, 3 * shares[0], width)

    def head_columns(part):
        sources = [columns(s, part * share, share) for s, share in zip((s1, s0), shares)]
        return jnp.concatenate(
            [c[:, j * c.shape[1] // 2 : (j + 1) * c.shape[1] // 2] for j in range(2) for c in sources], 1
        )

    query, key, value = (head_columns(part) for part in range(3))

    def gain_grad(pairs):
        total = sum(jnp.sum(w.astype(f32) * g, 1) for w, g in pairs)
        return total * scale

    return (
        jnp.stack(outputs),
        jnp.stack(grad_inputs),
        gain_grad([(w_query, query), (w_key, key), (w_value, value)]),
        query * gain1 * scale,
        key * gain1 * scale,
        value * gain1 * scale,
        out * scale,
        gain_grad([(w_gate, gate), (w_up, up)]),
        gate * gain2 * scale,
        up * gain2 * scale,
        down * scale,
    )


def solution(mesh):
    row = P("shard", None)
    tokens = P(("rep", "shard"), None, None)
    return jax.shard_map(
        per_device,
        mesh=mesh,
        in_specs=(
            tokens, P(("rep", "shard"), None), P("shard"), row, row, row, row, P("shard"), row, row, row, tokens,
        ),
        out_specs=(tokens, tokens, P("shard"), row, row, row, row, P("shard"), row, row, row),
        check_vma=False,
    )
```

```python
import functools

import jax
import jax.numpy as jnp
import numpy as np
from jax import lax
from jax.experimental import pallas as pl
from jax.experimental.pallas import tpu as pltpu
from jax.sharding import PartitionSpec as P

H = 12
HD = 64
BLOCK = 256
MAX_DOC = 512

epsilon = 1e-06
rope_base = 10000.0
far = 1e30

bf16 = jnp.bfloat16
f32 = jnp.float32
MIB = 1 << 20
NN = (((1,), (0,)), ((), ()))
NT = (((1,), (1,)), ((), ()))
TN = (((0,), (0,)), ((), ()))


def dot(left, right, dims=NN):
    return lax.dot_general(left, right, dims, preferred_element_type=f32)


def params(mib=60):
    return pltpu.CompilerParams(vmem_limit_bytes=mib * MIB)


HINT = 1.0


def cost(flops, nbytes, trans=0):
    return pl.CostEstimate(
        flops=int(HINT * flops), bytes_accessed=int(HINT * nbytes), transcendentals=int(HINT * trans)
    )


ANY = pl.BlockSpec(memory_space=pl.ANY)


class WeightCopies:
    def __init__(self, pieces, tab_ref, dest, sem, start, width):
        self.pieces, self.tab, self.dest, self.sem = pieces, tab_ref, dest, sem
        self.start_col, self.width = start, width

    def each(self, act):
        for number, piece in enumerate(self.pieces):
            count, rows = piece.shape[0], piece.shape[1]

            def step(b, carry):
                index = number * count + b
                row = pl.multiple_of(self.tab[0, index] * rows, 16)
                col = pl.multiple_of(self.tab[1, index] * self.width, 128)
                act(
                    pltpu.make_async_copy(
                        piece.at[b, :, pl.ds(self.start_col, self.width)],
                        self.dest.at[pl.ds(row, rows), pl.ds(col, self.width)],
                        self.sem.at[index],
                    )
                )
                return carry

            lax.fori_loop(0, count, step, 0)

    def start(self):
        self.each(lambda copy: copy.start())

    def wait(self):
        self.each(lambda copy: copy.wait())


def load_weight(pieces, tab_ref, dest, sem):
    copies = WeightCopies(pieces, tab_ref, dest, sem, 0, pieces[0].shape[2])
    copies.start()
    copies.wait()


SPLIT = (2, 1)


def in_order(refs, half=0, halves=1):
    return jnp.concatenate(
        [
            ref[:, j * (ref.shape[1] // 2) : (j + 1) * (ref.shape[1] // 2)]
            for j in range(2)
            if j * halves // 2 == half
            for ref in refs
        ],
        1,
    )


def pair_of(call):
    first, count = sum(SPLIT[:call]), SPLIT[call]
    return lambda i: (0, first + i % count + sum(SPLIT) * (i // count))


def pack_kernel(half_ref, *refs, folded):
    *sources, gain_ref, out_ref = refs
    offset = 0
    for source, scaled in zip(sources, folded):
        width = source.shape[1]
        value = source[...]
        if scaled:
            value = (value.astype(f32) * gain_ref[...]).astype(bf16)
        out_ref[:, offset : offset + width] = value
        offset += width


def pack(half, arrays, gain, halves):
    folded = [scaled for _, scaled in arrays]
    arrays = [array for array, _ in arrays]
    rows = arrays[0].shape[0]
    columns = sum(array.shape[1] for array in arrays) // halves
    return pl.pallas_call(
        functools.partial(pack_kernel, folded=folded),
        grid_spec=pltpu.PrefetchScalarGridSpec(
            num_scalar_prefetch=1,
            grid=(1,),
            in_specs=[
                pl.BlockSpec((rows, array.shape[1] // halves), lambda i, h: (0, h[0])) for array in arrays
            ]
            + [pl.BlockSpec((rows, 1), lambda i, h: (0, 0))],
            out_specs=pl.BlockSpec((rows, columns), lambda i, h: (0, 0)),
        ),
        out_shape=jax.ShapeDtypeStruct((rows, columns), bf16),
        compiler_params=params(),
        cost_estimate=cost(rows * columns, 4 * rows * columns),
        name="pack",
    )(half.reshape(1), *arrays, gain)


def rope_tables(length):
    frequency = rope_base ** -(np.arange(HD // 2) * (2.0 / HD))
    coarse = np.arange(length // 32)[:, None] * 32.0 * frequency[None, :]
    fine = np.arange(32)[:, None] * frequency[None, :]
    coarse, fine = np.tile(coarse, (1, 4))[:, None, :], np.tile(fine, (1, 4))[None, :, :]
    sign = np.tile(np.repeat([-1.0, 1.0], HD // 2), 2)
    cos_a, sin_a = jnp.asarray(np.cos(coarse), f32), jnp.asarray(np.sin(coarse), f32)
    cos_b, sin_b = jnp.asarray(np.cos(fine), f32), jnp.asarray(np.sin(fine), f32)
    cosine = cos_a * cos_b - sin_a * sin_b
    sine = (sin_a * cos_b + cos_a * sin_b) * jnp.asarray(sign, f32)
    return cosine.reshape(length, 128), sine.reshape(length, 128)


def swap_halves(tensor):
    lane = lax.broadcasted_iota(jnp.int32, tensor.shape, 1)
    return jnp.where(
        (lane & (HD // 2)) == 0, pltpu.roll(tensor, 128 - HD // 2, 1), pltpu.roll(tensor, HD // 2, 1)
    )


def project_kernel(tab_ref, *refs, n_pieces, halves):
    pieces, (x_ref, cos_ref, sin_ref) = refs[:n_pieces], refs[n_pieces : n_pieces + 3]
    n_ref, q_ref, k_ref, v_ref, weight, sem = refs[n_pieces + 3 :]

    @pl.when(pl.program_id(0) == 0)
    def _():
        load_weight(pieces, tab_ref, weight, sem)

    x = x_ref[...].astype(f32)
    normed = (x * lax.rsqrt(jnp.mean(x * x, -1, keepdims=True) + epsilon)).astype(bf16)
    n_ref[...] = normed
    width = x_ref.shape[1] // halves
    cosine, sine = cos_ref[...], sin_ref[...]
    everything = dot(normed, weight[...])
    for half in range(halves):
        result = everything[:, 3 * half * width : 3 * (half + 1) * width]
        for part, out, scale in ((0, q_ref, HD**-0.5), (1, k_ref, 1.0)):
            for c in range(0, width, 128):
                piece = result[:, part * width + c : part * width + c + 128]
                turned = piece * cosine + swap_halves(piece) * sine
                out[:, half * width + c : half * width + c + 128] = (
                    turned.astype(bf16) * jnp.asarray(scale, bf16)
                )
        v_ref[:, half * width : (half + 1) * width] = result[:, 2 * width :].astype(bf16)


def project(tab, pieces, x, cosine, sine, halves):
    length, width = x.shape
    rows = BLOCK
    n = len(pieces)
    blocks = sum(p.shape[0] for p in pieces)
    block = pl.BlockSpec((rows, width), lambda i, t: (i, 0))
    table = pl.BlockSpec((rows, 128), lambda i, t: (i, 0))
    shape = jax.ShapeDtypeStruct((length, width), bf16)
    return pl.pallas_call(
        functools.partial(project_kernel, n_pieces=n, halves=halves),
        grid_spec=pltpu.PrefetchScalarGridSpec(
            num_scalar_prefetch=1,
            grid=(length // rows,),
            in_specs=[ANY] * n + [block, table, table],
            out_specs=[block] * 4,
            scratch_shapes=[
                pltpu.VMEM((width, 3 * width), bf16),
                pltpu.SemaphoreType.DMA((blocks,)),
            ],
        ),
        out_shape=[shape] * 4,
        compiler_params=params(),
        cost_estimate=cost(6 * length * width * width, 16 * length * width),
        name="project",
    )(tab, *pieces, x, cosine, sine)


def key_range(block):
    low = max(0, (block * BLOCK - (MAX_DOC - 1)) // BLOCK) if block * BLOCK > MAX_DOC - 1 else 0
    return low * BLOCK, (block + 1) * BLOCK


def marks(docs):
    lane = jnp.arange(128, dtype=jnp.int32)[None, :] % HD
    used = lane < 4
    same = docs == lane
    return (
        jnp.where(used & ~same, -far, 0.0).astype(bf16),
        jnp.where(used & same, 1.0, 0.0).astype(bf16),
    )


def pipeline(items, first, second, third, ahead=2):
    made = [first(item) for item in items[:ahead]]
    pending = None
    for i, item in enumerate(items):
        if i + ahead < len(items):
            made.append(first(items[i + ahead]))
        middle = second(item, made[i])
        made[i] = None
        if pending is not None:
            third(*pending)
        pending = (item, middle)
    third(*pending)


def attend_kernel(q_ref, k_ref, v_ref, qm_ref, km_ref, mixed_ref, inv_ref, e_ref):
    length = q_ref.shape[0]
    lane = lax.broadcasted_iota(jnp.int32, (length, 128), 1)
    front = lax.broadcasted_iota(jnp.int32, (BLOCK, 128), 1) < HD
    q, k, v = q_ref[...], k_ref[...], v_ref[...]
    ones = jnp.ones((length, 128), bf16)
    operands = []
    for head in range(2):
        own = (lane < HD) if head == 0 else (lane >= HD)
        operands.append(
            (jnp.where(own, q, qm_ref[...]), jnp.where(own, k, km_ref[...]), jnp.where(own, v, ones))
        )
    outs = {}

    def scores(item):
        block, head = item
        low, high = key_range(block)
        qa, ka, _ = operands[head]
        return dot(ka[low:high], qa[block * BLOCK : (block + 1) * BLOCK], NT)

    def softmax(item, values):
        block, head = item
        low, high = key_range(block)
        exps = jnp.exp(values - jnp.max(values, 0, keepdims=True)).astype(bf16)
        for kb in range(low // BLOCK, high // BLOCK):
            e_ref[head, kb, :, (block - kb) * BLOCK : (block - kb + 1) * BLOCK] = exps[
                kb * BLOCK - low : (kb + 1) * BLOCK - low
            ]
        return exps

    def mix(item, exps):
        block, head = item
        low, high = key_range(block)
        outs[head] = dot(exps, operands[head][2][low:high], TN)
        if head == 1:
            rows = slice(block * BLOCK, (block + 1) * BLOCK)
            value = jnp.where(front, outs[0], outs[1])
            total = jnp.where(front, outs[1], outs[0])
            inverse = pltpu.roll(1.0 / total, HD, 1)
            mixed_ref[rows, :] = (value * inverse).astype(bf16)
            inv_ref[rows, :] = inverse

    items = [(block, head) for block in range(length // BLOCK) for head in range(2)]
    pipeline(items, scores, softmax, mix)


def span(length):
    return min(length, MAX_DOC + BLOCK)


def attend(q, k, v, q_marks, k_marks):
    length, width = q.shape
    blocks = length // BLOCK
    pairs = width // 128
    column = pl.BlockSpec((length, 128), lambda i: (0, i))
    fixed = pl.BlockSpec((length, 128), lambda i: (0, 0))
    return pl.pallas_call(
        attend_kernel,
        grid=(pairs,),
        in_specs=[column, column, column, fixed, fixed],
        out_specs=[column, column, pl.BlockSpec((2, blocks, BLOCK, span(length)), lambda i: (i, 0, 0, 0))],
        out_shape=[
            jax.ShapeDtypeStruct((length, 128 * pairs), bf16),
            jax.ShapeDtypeStruct((length, 128 * pairs), f32),
            jax.ShapeDtypeStruct((2 * pairs, blocks, BLOCK, span(length)), bf16),
        ],
        compiler_params=params(),
        cost_estimate=cost(1280 * pairs * length * length, 3840 * pairs * length, 2 * pairs * length * length),
        name="attend",
    )(q, k, v, q_marks, k_marks)


def attend_back_kernel(
    q_ref, k_ref, v_ref, mixed_ref, inv_ref, e_ref, grad_ref, cos_ref, sin_ref,
    dq_ref, dk_ref, dv_ref, ds_ref,
):
    length = q_ref.shape[0]
    count = length // BLOCK
    lane = lax.broadcasted_iota(jnp.int32, (length, 128), 1)
    q, k, v = q_ref[...], k_ref[...], v_ref[...]
    zero = jnp.zeros((length, 128), bf16)
    scaled = grad_ref[...].astype(f32) * inv_ref[...]
    inner = scaled * mixed_ref[...].astype(f32)
    operands = []
    for head in range(2):
        own = (lane < HD) if head == 0 else (lane >= HD)
        first = HD if head == 0 else 0
        spare = (lane == first) | (lane == first + 1)
        minus = jnp.where(spare, -1.0, 0.0).astype(bf16)
        delta = jnp.sum(jnp.where(own, inner, 0.0), 1, keepdims=True)
        upper = delta.astype(bf16).astype(f32)
        masked = jnp.where(own, scaled, 0.0)
        joined = jnp.where(lane == first, upper, masked)
        joined = jnp.where(lane == first + 1, delta - upper, joined).astype(bf16)
        operands.append(
            (
                jnp.where(own, q, zero),
                jnp.where(own, k, zero),
                jnp.where(own, v, minus),
                masked.astype(bf16),
                joined,
            )
        )
    sums = {}

    def turn_back(value, rows):
        return (value * cos_ref[rows, :] - swap_halves(value) * sin_ref[rows, :]).astype(bf16)

    def slopes(item):
        block, head = item
        low, high = key_range(block)
        return dot(
            operands[head][2][low:high], operands[head][4][block * BLOCK : (block + 1) * BLOCK], NT
        )

    def products(item, slope):
        block, head = item
        low, high = key_range(block)
        parts = []
        for kb in range(low // BLOCK, high // BLOCK):
            cols = slice((block - kb) * BLOCK, (block - kb + 1) * BLOCK)
            part = e_ref[head, kb, :, cols].astype(f32) * slope[kb * BLOCK - low : (kb + 1) * BLOCK - low]
            part = part.astype(bf16)
            ds_ref[head, kb, :, cols] = part
            parts.append(part)
        return jnp.concatenate(parts, 0)

    def finish(item, ds):
        block, head = item
        low, high = key_range(block)
        rows = slice(block * BLOCK, (block + 1) * BLOCK)
        part = dot(ds, operands[head][1][low:high], TN)
        if head == 0:
            sums["q"] = part
        else:
            dq_ref[rows, :] = turn_back((sums["q"] + part) * (HD**-0.5), rows)
        for kb in range(count):
            if max(b for b in range(count) if key_range(b)[0] <= kb * BLOCK) != block:
                continue
            width = (block - kb + 1) * BLOCK
            seen = slice(kb * BLOCK, kb * BLOCK + width)
            keys = slice(kb * BLOCK, (kb + 1) * BLOCK)
            dv = dot(e_ref[head, kb, :, 0:width], operands[head][3][seen])
            dk = dot(ds_ref[head, kb, :, 0:width], operands[head][0][seen])
            if head == 0:
                sums[kb] = (dv, dk)
            else:
                dv_ref[keys, :] = (sums[kb][0] + dv).astype(bf16)
                dk_ref[keys, :] = turn_back(sums[kb][1] + dk, keys)

    items = [(block, head) for block in range(count) for head in range(2)]
    pipeline(items, slopes, products, finish)


def attend_back(q, k, v, mixed, inv, exps, grad, cosine, sine, call):
    length = q.shape[0]
    pairs = 2 * SPLIT[call]
    column = pl.BlockSpec((length, 128), pair_of(call))
    part = pl.BlockSpec((length, 128), lambda i: (0, i))
    fixed = pl.BlockSpec((length, 128), lambda i: (0, 0))
    shape = jax.ShapeDtypeStruct((length, 128 * pairs), bf16)
    return pl.pallas_call(
        attend_back_kernel,
        grid=(pairs,),
        in_specs=[column] * 5
        + [
            pl.BlockSpec((2,) + exps.shape[1:], lambda i: (pair_of(call)(i)[1], 0, 0, 0)),
            column,
            fixed,
            fixed,
        ],
        out_specs=[part] * 3,
        out_shape=[shape] * 3,
        scratch_shapes=[pltpu.VMEM((2,) + exps.shape[1:], bf16)],
        compiler_params=params(54),
        cost_estimate=cost(2560 * pairs * length * length, 4608 * pairs * length),
        name="attend_back",
    )(q, k, v, mixed, inv, exps, grad, cosine, sine)


def ffn_kernel(tab_ref, *refs, n_pieces, halves):
    pieces, (x_ref, mixed_ref), refs = refs[:n_pieces], refs[n_pieces : n_pieces + 2], refs[n_pieces + 2 :]
    middle_ref, normed_ref, hidden_ref, slope_g_ref, slope_u_ref, w_out, w_in, sem = refs
    width = x_ref.shape[1] // halves
    inner = hidden_ref.shape[1] // halves
    early = WeightCopies(pieces, tab_ref, w_out, sem.at[0], 0, width)
    late = WeightCopies(pieces, tab_ref, w_in, sem.at[1], width, 2 * inner)

    @pl.when(pl.program_id(0) == 0)
    def _():
        early.start()
        late.start()
        early.wait()

    middle = x_ref[...].astype(f32) + dot(mixed_ref[...], w_out[...])
    middle_ref[...] = middle
    normed = (middle * lax.rsqrt(jnp.mean(middle * middle, -1, keepdims=True) + epsilon)).astype(bf16)
    normed_ref[...] = normed

    @pl.when(pl.program_id(0) == 0)
    def _():
        late.wait()

    step = min(256, inner)

    def dots(first):
        return (
            dot(normed, w_in[:, first : first + step]),
            dot(normed, w_in[:, first + inner : first + inner + step]),
        )

    def activate(first, values):
        gate, up = values
        half_tanh = 0.5 * jnp.tanh(0.5 * gate)
        sigmoid = half_tanh + 0.5
        silu = gate * sigmoid
        cols = slice(first - first // (2 * inner) * inner, first - first // (2 * inner) * inner + step)
        hidden_ref[:, cols] = (silu * up).astype(bf16)
        slope_u_ref[:, cols] = silu.astype(bf16)
        slope_g_ref[:, cols] = (up * (sigmoid + silu * (0.5 - half_tanh))).astype(bf16)

    items = [2 * h * inner + c for h in range(halves) for c in range(0, inner, step)]
    pipeline(items, dots, activate, lambda *_: None)


def ffn(tab, pieces, x, mixed, inner, halves):
    length, width = x.shape
    rows = BLOCK
    n = len(pieces)
    blocks = sum(p.shape[0] for p in pieces)
    narrow = pl.BlockSpec((rows, width), lambda i, t: (i, 0))
    wide = pl.BlockSpec((rows, inner), lambda i, t: (i, 0))
    wide_shape = jax.ShapeDtypeStruct((length, inner), bf16)
    return pl.pallas_call(
        functools.partial(ffn_kernel, n_pieces=n, halves=halves),
        grid_spec=pltpu.PrefetchScalarGridSpec(
            num_scalar_prefetch=1,
            grid=(length // rows,),
            in_specs=[ANY] * n + [narrow, narrow],
            out_specs=[narrow, narrow, wide, wide, wide],
            scratch_shapes=[
                pltpu.VMEM((width, width), bf16),
                pltpu.VMEM((width, 2 * inner), bf16),
                pltpu.SemaphoreType.DMA((2, blocks)),
            ],
        ),
        out_shape=[
            jax.ShapeDtypeStruct((length, width), f32),
            jax.ShapeDtypeStruct((length, width), bf16),
            wide_shape,
            wide_shape,
            wide_shape,
        ],
        compiler_params=params(),
        cost_estimate=cost(2 * length * width * (width + 2 * inner), 8 * width * inner + 8 * length * inner),
        name="ffn",
    )(tab, *pieces, x, mixed)


def hidden_back_kernel(tab_ref, *refs, n_pieces, halves):
    pieces = refs[:n_pieces]
    middle_ref, hidden_ref, slope_g_ref, slope_u_ref, cot_ref = refs[n_pieces : n_pieces + 5]
    output_ref, gg_ref, gu_ref, weight, sem = refs[n_pieces + 5 :]

    @pl.when(pl.program_id(0) == 0)
    def _():
        load_weight(pieces, tab_ref, weight, sem)

    inner = hidden_ref.shape[1]
    step = min(512, inner)
    cot = cot_ref[...]
    for c in range(0, inner, step):
        cols = slice(c, c + step)
        grad_hidden = dot(cot, weight[cols, :], NT)
        gg_ref[:, cols] = (grad_hidden * slope_g_ref[:, cols].astype(f32)).astype(bf16)
        gu_ref[:, cols] = (grad_hidden * slope_u_ref[:, cols].astype(f32)).astype(bf16)
    output_ref[...] = (middle_ref[...] + dot(hidden_ref[...], weight[...])).astype(bf16)


def hidden_back(tab, pieces, middle, hidden, slope_g, slope_u, cot, halves):
    length, width = middle.shape
    inner = hidden.shape[1]
    rows = BLOCK
    n = len(pieces)
    narrow = pl.BlockSpec((rows, width), lambda i, t: (i, 0))
    wide = pl.BlockSpec((rows, inner), lambda i, t: (i, 0))
    wide_low = jax.ShapeDtypeStruct((length, inner), bf16)
    return pl.pallas_call(
        functools.partial(hidden_back_kernel, n_pieces=n, halves=halves),
        grid_spec=pltpu.PrefetchScalarGridSpec(
            num_scalar_prefetch=1,
            grid=(length // rows,),
            in_specs=[ANY] * n + [narrow, wide, wide, wide, narrow],
            out_specs=[narrow, wide, wide],
            scratch_shapes=[
                pltpu.VMEM((inner, width), bf16),
                pltpu.SemaphoreType.DMA((sum(p.shape[0] for p in pieces),)),
            ],
        ),
        out_shape=[jax.ShapeDtypeStruct((length, width), bf16), wide_low, wide_low],
        compiler_params=params(),
        cost_estimate=cost(4 * length * width * inner, 2 * width * inner + 12 * length * inner),
        name="hidden_back",
    )(tab, *pieces, middle, hidden, slope_g, slope_u, cot)


def middle_back_kernel(tab_ref, *refs, n_pieces, halves):
    pieces = refs[:n_pieces]
    middle_ref, gg_ref, gu_ref, cot_ref = refs[n_pieces : n_pieces + 4]
    grad_middle_ref, attn_grad_ref, grad_mixed_ref, w_out, w_in, sem = refs[n_pieces + 4 :]
    width = cot_ref.shape[1] // halves
    inner = gg_ref.shape[1] // halves
    early = WeightCopies(pieces, tab_ref, w_in, sem.at[0], width, 2 * inner)
    late = WeightCopies(pieces, tab_ref, w_out, sem.at[1], 0, width)

    @pl.when(pl.program_id(0) == 0)
    def _():
        early.start()
        late.start()
        early.wait()
        late.wait()

    def gradient(rows):
        both = [
            ref[rows, h * inner : (h + 1) * inner] for h in range(halves) for ref in (gg_ref, gu_ref)
        ]
        return dot(jnp.concatenate(both, 1), w_in[...], NT)

    def norm_back(rows, grad):
        middle = middle_ref[rows, :]
        inverse = lax.rsqrt(jnp.mean(middle * middle, -1, keepdims=True) + epsilon)
        normed = middle * inverse
        grad_middle = cot_ref[rows, :].astype(f32) + inverse * (
            grad - normed * jnp.mean(grad * normed, -1, keepdims=True)
        )
        grad_middle_ref[rows, :] = grad_middle
        low = grad_middle.astype(bf16)
        attn_grad_ref[rows, :] = low
        return low

    def mixed_grad(rows, low):
        grad_mixed_ref[rows, :] = dot(low, w_out[...], NT).astype(bf16)

    total = middle_ref.shape[0]
    items = [slice(r, r + SUB) for r in range(0, total, SUB)]
    pipeline(items, gradient, norm_back, mixed_grad, 1)


SUB = 256
MB_ROWS = 256


def middle_back(tab, pieces, middle, gg, gu, cot, halves):
    length, width = middle.shape
    inner = gg.shape[1]
    rows = MB_ROWS
    n = len(pieces)
    narrow = pl.BlockSpec((rows, width), lambda i, t: (i, 0))
    wide = pl.BlockSpec((rows, inner), lambda i, t: (i, 0))
    low = jax.ShapeDtypeStruct((length, width), bf16)
    return pl.pallas_call(
        functools.partial(middle_back_kernel, n_pieces=n, halves=halves),
        grid_spec=pltpu.PrefetchScalarGridSpec(
            num_scalar_prefetch=1,
            grid=(length // rows,),
            in_specs=[ANY] * n + [narrow, wide, wide, narrow],
            out_specs=[narrow] * 3,
            scratch_shapes=[
                pltpu.VMEM((width, width), bf16),
                pltpu.VMEM((width, 2 * inner), bf16),
                pltpu.SemaphoreType.DMA((2, sum(p.shape[0] for p in pieces))),
            ],
        ),
        out_shape=[jax.ShapeDtypeStruct((length, width), f32), low, low],
        compiler_params=params(54),
        cost_estimate=cost(
            2 * length * width * (width + 2 * inner), 4 * width * inner + 4 * length * inner
        ),
        name="middle_back",
    )(tab, *pieces, middle, gg, gu, cot)


def input_kernel(tab_ref, *refs, n_pieces, halves):
    pieces = refs[:n_pieces]
    x_ref, grad_middle_ref = refs[n_pieces : n_pieces + 2]
    calls = len(SPLIT)
    parts = refs[n_pieces + 2 : n_pieces + 2 + 3 * calls]
    out_ref, weight, sem = refs[n_pieces + 2 + 3 * calls :]

    @pl.when(pl.program_id(0) == 0)
    def _():
        load_weight(pieces, tab_ref, weight, sem)

    left = [
        in_order(parts[part * calls : (part + 1) * calls], h, halves)
        for h in range(halves)
        for part in range(3)
    ]
    grad = dot(jnp.concatenate(left, 1), weight[...], NT)
    x = x_ref[...].astype(f32)
    inverse = lax.rsqrt(jnp.mean(x * x, -1, keepdims=True) + epsilon)
    normed = x * inverse
    out_ref[...] = grad_middle_ref[...] + inverse * (
        grad - normed * jnp.mean(grad * normed, -1, keepdims=True)
    )


def input_grad(tab, pieces, x, grad_middle, parts, halves):
    length, width = x.shape
    rows = BLOCK
    n = len(pieces)
    blocks = sum(p.shape[0] for p in pieces)
    block = pl.BlockSpec((rows, width), lambda i, t: (i, 0))
    shares = [pl.BlockSpec((rows, p.shape[1]), lambda i, t: (i, 0)) for p in parts]
    return pl.pallas_call(
        functools.partial(input_kernel, n_pieces=n, halves=halves),
        grid_spec=pltpu.PrefetchScalarGridSpec(
            num_scalar_prefetch=1,
            grid=(length // rows,),
            in_specs=[ANY] * n + [block] * 2 + shares,
            out_specs=block,
            scratch_shapes=[
                pltpu.VMEM((width, 3 * width), bf16),
                pltpu.SemaphoreType.DMA((blocks,)),
            ],
        ),
        out_shape=jax.ShapeDtypeStruct((length, width), f32),
        compiler_params=params(),
        cost_estimate=cost(6 * length * width * width, 20 * length * width),
        name="input_grad",
    )(tab, *pieces, x, grad_middle, *parts)


def weight_kernel(tab_ref, *refs, counts, block_rows, chunks, halves):
    n_left, n_right = sum(n for n, _ in counts), sum(n for _, n in counts)
    lefts, rights = list(refs[:n_left]), list(refs[n_left : n_left + n_right])
    keep_ref, send_ref, held, sem = refs[n_left + n_right :]
    step, steps = pl.program_id(0), pl.num_programs(0)
    slot = lax.rem(step, 2)
    here = halves if chunks == 0 else 1
    parts = max(1, chunks)
    rows = held.shape[2]
    kept = keep_ref.shape[0]
    widths = [r.shape[1] // here for r in rights]
    sizes = [sum(widths)] if parts == 1 else widths

    def pieces():
        for b in range(rows // block_rows):
            for h in range(here):
                offset = 0
                for i, width in enumerate(sizes):
                    yield b, h, (b * here + h) * len(sizes) + i, offset, width
                    offset += width

    def wait(which):
        for _, h, number, offset, width in pieces():
            pltpu.make_async_copy(
                held.at[which, h, pl.ds(0, block_rows), pl.ds(offset, width)],
                keep_ref.at[0, :, pl.ds(offset, width)],
                sem.at[which, number],
            ).wait()

    @pl.when(step >= 2)
    def _():
        wait(slot)

    offset = 0
    for _, n_right in counts:
        left = lefts.pop(0)[...]
        group = [rights.pop(0)[...] for _ in range(n_right)]
        result = dot(left, jnp.concatenate(group, 1), TN).astype(bf16)
        column = 0
        for right in group:
            width = right.shape[1] // here
            for h in range(here):
                held[slot, h, :, offset : offset + width] = result[:, column : column + width]
                column += width
            offset += width
    if chunks == 0:
        first, half, chunk = step * (rows // block_rows), 0, 0
    else:
        first, half, chunk = 0, step // chunks, lax.rem(step, chunks)
    def send_out(parity):
        for b, h, number, offset, width in pieces():
            place = tab_ref[(first + b) * halves + half + h]
            if b % 2 == parity:
                target = keep_ref.at[place]
            else:
                target = send_ref.at[place - kept]
            pltpu.make_async_copy(
                held.at[slot, h, pl.ds(b * block_rows, block_rows), pl.ds(offset, width)],
                target.at[:, pl.ds(pl.multiple_of(offset * parts + chunk * width, 128), width)],
                sem.at[slot, number],
            ).start()

    for parity in range(2):
        pl.when((tab_ref[0] < kept) == (parity == 0))(functools.partial(send_out, parity))

    @pl.when(step == steps - 1)
    def _():
        wait(slot)

        @pl.when(steps > 1)
        def _():
            wait(1 - slot)


def weight_grad(moves, products, name, chunks=0, row_steps=1):
    lefts = [left for group, _ in products for left in group]
    rights = [right for _, group in products for right in group]
    counts = [(len(left), len(right)) for left, right in products]
    length = lefts[0].shape[0]
    rows = sum(left.shape[1] for left in products[0][0])
    halves, blocks = moves.halves, moves.place.shape[0]
    block_rows = rows * halves // blocks
    columns = sum(r.shape[1] for r in rights) // halves
    kept = moves.kept
    sent = max(1, blocks - kept)
    if blocks == 1 and chunks == 0:
        row_steps = 1
    steps = halves * chunks if chunks else row_steps
    here = 1 if chunks else halves
    step_rows = rows if chunks else rows // row_steps
    n_pieces = step_rows // block_rows * here * (len(rights) if chunks > 1 else 1)
    if chunks:
        left_specs = [pl.BlockSpec(left.shape, lambda i, t: (0, 0)) for left in lefts]
        right_specs = [pl.BlockSpec((length, r.shape[1] // steps), lambda i, t: (0, i)) for r in rights]
    else:
        left_specs = [
            pl.BlockSpec((length, left.shape[1] // row_steps), lambda i, t: (0, i)) for left in lefts
        ]
        right_specs = [pl.BlockSpec(r.shape, lambda i, t: (0, 0)) for r in rights]
    return pl.pallas_call(
        functools.partial(
            weight_kernel, counts=counts, block_rows=block_rows, chunks=chunks, halves=halves
        ),
        grid_spec=pltpu.PrefetchScalarGridSpec(
            num_scalar_prefetch=1,
            grid=(steps,),
            in_specs=left_specs + right_specs,
            out_specs=[ANY, ANY],
            scratch_shapes=[
                pltpu.VMEM((2, here, step_rows, columns // max(1, chunks)), bf16),
                pltpu.SemaphoreType.DMA((2, n_pieces)),
            ],
        ),
        out_shape=[
            jax.ShapeDtypeStruct((kept, block_rows, columns), bf16),
            jax.ShapeDtypeStruct((sent, block_rows, columns), bf16),
        ],
        compiler_params=params(54),
        cost_estimate=cost(
            2 * length * rows * columns * halves,
            2 * (length * rows + length * columns * halves + rows * columns * halves),
        ),
        name=name,
    )(moves.place, *lefts, *rights)


def after(value, *others):
    return lax.optimization_barrier((value, others))[0]


def place_of(xr, yr, zr, cr):
    low = xr * 4 + yr * 2 + zr
    high = 8 + yr * 4 + xr * 2 + (zr - 2)
    return cr * 16 + jnp.where(zr < 2, low, high)


def swapped(bits, axis="shard"):
    count = lax.axis_size(axis)
    pairs = [(i, i ^ bits) for i in range(count)]
    return lambda array: lax.ppermute(array, axis, pairs)


class Direct:
    halves = 2
    kept = 16

    def __init__(self):
        self.me = lax.axis_index("shard")
        self.x = lax.axis_index("rep")
        self.core, self.y, self.x_move = swapped(1), swapped(2), swapped(1, "rep")
        self.z = [swapped(4), swapped(8), swapped(12)]
        shard = jnp.arange(16, dtype=jnp.int32)[:, None]
        half = jnp.arange(2, dtype=jnp.int32)[None, :]
        rel = shard ^ self.me
        place = place_of(half ^ self.x, (rel >> 1) & 1, rel >> 2, rel & 1)
        self.place = place.reshape(32)
        order = []
        for cr in range(2):
            for zs in ((0, 1), (2, 3)):
                for outer in range(2):
                    for inner in range(2):
                        for zr in zs:
                            xr, yr = (outer, inner) if zs[0] == 0 else (inner, outer)
                            order.append((zr * 4 + yr * 2 + cr, xr))
        rel_shard = jnp.array([o[0] for o in order], jnp.int32)
        rel_half = jnp.array([o[1] for o in order], jnp.int32)
        self.tab = jnp.stack([rel_shard ^ self.me, rel_half ^ self.x])
        order = [(zr * 4 + yr * 2 + cr, xr) for cr in range(2) for xr in range(2) for yr in range(2) for zr in range(4)]
        rel_shard = jnp.array([o[0] for o in order], jnp.int32)
        rel_half = jnp.array([o[1] for o in order], jnp.int32)
        self.tab3 = jnp.stack([rel_shard ^ self.me, rel_half ^ self.x])
        rel = rel[:, 0]
        self.wide = Wide(self, (rel & 1) * 8 + ((rel >> 1) & 1) * 4 + (rel >> 2))

    def xy(self, array):
        pairs = [(i, i ^ 18) for i in range(32)]
        return lax.ppermute(array, ("rep", "shard"), pairs)

    def pack(self, arrays, gain):
        return pack(self.x, arrays, gain, 2)

    def along_z(self, own):
        z1, z2, z3 = (move(own) for move in self.z)
        return jnp.concatenate([own, z1], 0), jnp.concatenate([z2, z3], 0), (z1, z2, z3)

    def one_axis(self, a, b):
        ay, bx = self.y(a), self.x_move(b)
        return (a, ay), (b, bx)

    def rest(self, a, b):
        ax, by = self.x_move(a), self.y(b)
        return [a, ax, b, by]

    def with_core(self, own, *deps):
        own = [after(p, *deps) for p in own] if deps else own
        return own + [self.core(p) for p in own]

    def gather(self, blocks):
        first, second, third = (block[None] for block in blocks)
        a1, b1, z_done1 = self.along_z(first)
        a2, b2, z_done2 = self.along_z(after(second, *z_done1))
        a1, b1 = self.one_axis(a1, b1)
        a1, b1 = jnp.concatenate(a1, 0), jnp.concatenate(b1, 0)
        own1 = self.rest(a1, b1)
        w1 = self.with_core(own1)
        self.a2, self.b2 = after(a2, *own1), after(b2, *own1)
        self.third = after(third, *z_done2, *own1)
        return w1

    def stage0(self):
        self.pair2 = self.one_axis(self.a2, self.b2)
        self.z3 = self.z[0](self.third)
        return self.a2, self.b2, self.third

    def stage1(self, *deps):
        (a, ay), (b, bx) = self.pair2
        deps = (*deps, self.z3, ay, bx)
        a = jnp.concatenate([after(a, *deps), ay], 0)
        b = jnp.concatenate([after(b, *deps), bx], 0)
        a3 = jnp.concatenate([after(self.third, *deps), self.z3], 0)
        self.a3, self.b3 = a3, self.z[1](a3)
        self.own2 = self.rest(a, b)
        self.core2 = [self.core(a), None, self.core(b), None]
        return a, b, a3

    def stage3(self, *deps):
        deps = (*deps, *self.own2, self.b3, self.core2[0], self.core2[2])
        block = jnp.concatenate([after(self.a3, *deps), after(self.b3, *deps)], 0)
        self.own3 = [block, self.y(block), self.x_move(block), self.xy(block)]
        for i in (1, 3):
            self.core2[i] = self.core(after(self.own2[i], *deps, block))
        self.own2 += self.core2
        return (block,)

    def scatter(self, grads, direct=False):
        return Direct.Sum(self, grads, direct)

    class Sum:
        def __init__(self, moves, grads, direct):
            self.moves = moves
            self.keep, self.send = grads
            over_z = [self.over_z] if direct else [self.over_z2, self.over_z1]
            self.steps = [self.over_core, self.over_two, self.over_other, *over_z, self.over_x]
            self.start = self.steps[0]
            self.got = ()

        def step(self, *deps):
            if deps:
                self.keep = after(self.keep, *deps)
                if self.steps[0] == self.start:
                    self.send = after(self.send, *deps)
            return self.steps.pop(0)()

        def finish(self):
            while self.steps:
                self.step()
            return self.result

        @staticmethod
        def add(*terms):
            total = terms[0].astype(f32)
            for term in terms[1:]:
                total = total + term.astype(f32)
            return total.astype(bf16)

        def over_core(self):
            self.core = self.moves.core(self.send)
            self.got = (self.core,)
            return (self.send,)

        def over_two(self):
            keep, core = self.keep, self.core
            to_x, to_y = self.add(keep[4:8], core[4:8]), self.add(keep[12:16], core[12:16])
            self.ax, self.by = self.got = self.moves.x_move(to_x), self.moves.y(to_y)
            return to_x, to_y

        def over_other(self):
            keep, core, ax, by = self.keep, self.core, self.ax, self.by
            to_y = self.add(keep[2:4], core[2:4], ax[2:4])
            to_x = self.add(keep[10:12], core[10:12], by[2:4])
            self.ay, self.bx = self.got = self.moves.y(to_y), self.moves.x_move(to_x)
            return to_y, to_x

        def over_z(self):
            keep, core, ax, by, ay, bx = self.keep, self.core, self.ax, self.by, self.ay, self.bx
            sends = (
                self.add(keep[1], core[1], ax[1], ay[1]),
                self.add(keep[8], core[8], by[0], bx[0]),
                self.add(keep[9], core[9], by[1], bx[1]),
            )
            self.got = self.zs = tuple(move(send) for move, send in zip(self.moves.z, sends))
            return sends

        def over_z2(self):
            keep, core = self.keep, self.core
            send = self.add(keep[8:10], core[8:10], self.by[0:2], self.bx[0:2])
            self.z2 = self.moves.z[1](send)
            self.got = (self.z2,)
            return (send,)

        def over_z1(self):
            send = self.add(self.keep[1], self.core[1], self.ax[1], self.ay[1], self.z2[1])
            z1 = self.moves.z[0](send)
            self.zs = (self.z2[0], z1)
            self.got = (z1,)
            return (send,)

        def over_x(self):
            own = self.add(self.keep[0], self.core[0], self.ax[0], self.ay[0], *self.zs)
            other = self.moves.x_move(own)
            first = self.moves.x == 0
            self.result = [jnp.where(first, own, other), jnp.where(first, other, own)]
            self.got = (other,)
            return (own,)


class Wide:
    halves = 1
    kept = 8

    def __init__(self, moves, place):
        self.moves, self.place = moves, place

    def scatter(self, grads, direct=False):
        return Wide.Sum(self.moves, grads, direct)

    class Sum(Direct.Sum):
        def __init__(self, moves, grads, direct):
            super().__init__(moves, grads, direct)
            self.steps = [s for s in self.steps if s != self.over_other]

        def over_two(self):
            send = self.add(self.keep[4:8], self.core[4:8])
            self.by = self.moves.y(send)
            self.got = (self.by,)
            return (send,)

        def over_z(self):
            sends = tuple(self.add(self.keep[i], self.core[i], self.by[i]) for i in (1, 2, 3))
            self.got = self.zs = tuple(move(send) for move, send in zip(self.moves.z, sends))
            return sends

        def over_z2(self):
            send = self.add(self.keep[2:4], self.core[2:4], self.by[2:4])
            self.z2 = self.moves.z[1](send)
            self.got = (self.z2,)
            return (send,)

        def over_z1(self):
            send = self.add(self.keep[1], self.core[1], self.by[1], self.z2[1])
            z1 = self.moves.z[0](send)
            self.zs = (self.z2[0], z1)
            self.got = (z1,)
            return (send,)

        def over_x(self):
            own = self.add(self.keep[0], self.core[0], self.by[0], *self.zs)
            other = self.moves.x_move(own)
            self.result = [own.astype(f32) + other.astype(f32)]
            self.got = (other,)
            return (own,)


class Plain:
    halves = 1
    kept = 1

    def __init__(self):
        self.place = jnp.zeros((1,), jnp.int32)
        self.tab = self.tab3 = jnp.zeros((2, 1), jnp.int32)
        self.wide = self

    def pack(self, arrays, gain):
        return pack(jnp.int32(0), arrays, gain, 1)

    def gather(self, blocks):
        first, *others = (
            [lax.all_gather(block, "shard", axis=0, tiled=True)[None]] for block in blocks
        )
        self.own2, self.own3 = others
        return first

    def with_core(self, own, *deps):
        return own

    def stage0(self):
        return ()

    def stage1(self, *deps):
        return ()

    stage3 = stage1

    def scatter(self, grads, direct=False):
        return Plain.Sum(grads)

    class Sum:
        got = ()

        def __init__(self, grads):
            self.grads = grads

        def step(self, *deps):
            return ()

        def finish(self):
            total = self.grads[0][0].astype(f32)
            part = lax.psum_scatter(total, "shard", scatter_dimension=0, tiled=True)
            return [lax.psum(part.astype(bf16), "rep")]


def columns(halves, start, width):
    step = width // len(halves)
    first = start // len(halves)
    return jnp.concatenate([h[:, first : first + step] for h in halves], 1).astype(f32)


def one_sequence(moves, x, docs, w1, cot, inner):
    cosine, sine = rope_tables(x.shape[0])
    q_marks, k_marks = marks(docs.reshape(-1, 1))
    halves, tab = moves.halves, moves.tab
    sends = moves.stage0()
    normed1, q, k, v = project(tab, w1, after(x, *sends), cosine, sine, halves)
    sends = moves.stage1(normed1)
    mixed, inv, exps = attend(q, k, v, after(q_marks, *sends), k_marks)
    sends = moves.stage3(mixed)
    w2 = moves.own2
    middle, normed2, hidden, slope_g, slope_u = ffn(
        tab, w2, after(x, *sends), mixed, inner, halves
    )
    w3 = moves.with_core(moves.own3, hidden)
    g3 = weight_grad(moves.wide, [([after(hidden, *moves.own3)], [cot])], "grad_down", row_steps=4)
    sum3 = moves.wide.scatter(g3)
    sum3.step(*g3, *w3)
    output, gg, gu = hidden_back(
        moves.tab3, w3, middle, after(hidden, *g3), slope_g, slope_u, cot, halves
    )
    sends = sum3.step(gg, *sum3.got)
    g2 = weight_grad(moves, [([after(normed2, *sends)], [gg, gu])], "grad_gate_up", chunks=2)
    sum2 = moves.scatter(g2)
    sum2.step(*g2)
    grad_middle, attn_grad, grad_mixed = middle_back(
        tab, w2, after(middle, *g2), gg, gu, cot, halves
    )
    due = (attn_grad, *sum3.got, *sum2.got)
    sends = sum3.step(*due)
    sends = (*sends, *sum2.step(*due))

    def back(call, sends):
        return attend_back(q, k, v, mixed, inv, exps, after(grad_mixed, *sends), cosine, sine, call)

    turned0 = back(0, sends)
    due = (*turned0[:1], *sum2.got, *sum3.got)
    sends = sum2.step(*due)
    sends = (*sends, *sum3.step(*due))
    g1 = weight_grad(
        moves,
        [([after(normed1, *sends)], turned0), ([mixed], [attn_grad])],
        "grad_qk_out",
        row_steps=2,
    )
    sum1 = moves.scatter(g1)
    due = (*g1, *sum2.got, *sum3.got)
    sum1.step(*due)
    sends = (*sum2.step(*due), *sum3.step(*due))
    sends = (*sends, *sum1.step(*sends, *sum1.got))
    turned1 = back(1, (*g1, *sends))
    due = (*turned1[:1], *sum1.got, *sum2.got)
    sends = sum1.step(*due)
    sends = (*sends, *sum2.step(*due))
    g0 = weight_grad(moves.wide, [([after(normed1, *sends)], turned1)], "grad_qkv_rest", row_steps=2)
    sum0 = moves.wide.scatter(g0, True)
    due = (*g0, *sum1.got, *sum2.got)
    sum0.step(*due)
    sends = (*sum1.step(*due), *sum2.step(*due))
    sends = (*sends, *sum0.step(*sends, *sum0.got))
    parts = [t[part] for part in range(3) for t in (turned0, turned1)]
    grad_input = input_grad(tab, w1, after(x, *g0, *sends), grad_middle, parts, halves)
    sums = (sum0, sum1, sum2, sum3)
    due = (grad_input, *sum2.got, *sum1.got, *sum0.got)
    for one in (sum0, sum1):
        one.step(*due)
    return output, grad_input, [s.finish() for s in sums]


def per_device(
    inputs,
    doc_ids,
    attn_gain,
    w_query,
    w_key,
    w_value,
    w_out,
    ffn_gain,
    w_gate,
    w_up,
    w_down,
    cotangent,
):
    batch_size, length, width = inputs.shape
    inner = w_gate.shape[1]
    replicas, members = lax.axis_size("rep"), lax.axis_size("shard")
    moves = Direct() if (replicas, members, batch_size) == (2, 16, 1) else Plain()
    gain1 = attn_gain.astype(f32)[:, None]
    gain2 = ffn_gain.astype(f32)[:, None]

    w1 = moves.gather(
        [
            moves.pack([(w, True) for w in (w_query, w_key, w_value)], gain1),
            moves.pack([(w_out, False), (w_gate, True), (w_up, True)], gain2),
            moves.pack([(w_down, False)], jnp.ones((w_down.shape[0], 1), f32)),
        ]
    )
    outputs, grad_inputs, sums = [], [], None
    for b in range(batch_size):
        output, grad_input, own = one_sequence(
            moves, inputs[b], doc_ids[b], w1, cotangent[b], inner
        )
        outputs.append(output)
        grad_inputs.append(grad_input)
        sums = own if sums is None else jax.tree.map(jnp.add, sums, own)
    s0, s1, s2, s3 = sums
    scale = 1.0 / (batch_size * replicas * members)
    down = columns(s3, 0, width)
    gate, up = columns(s2, 0, inner), columns(s2, inner, inner)
    shares = [width * count // sum(SPLIT) for count in SPLIT]
    out = columns(s1, 3 * shares[0], width)

    def head_columns(part):
        sources = [columns(s, part * share, share) for s, share in zip((s1, s0), shares)]
        return jnp.concatenate(
            [c[:, j * c.shape[1] // 2 : (j + 1) * c.shape[1] // 2] for j in range(2) for c in sources], 1
        )

    query, key, value = (head_columns(part) for part in range(3))

    def gain_grad(pairs):
        total = sum(jnp.sum(w.astype(f32) * g, 1) for w, g in pairs)
        return total * scale

    return (
        jnp.stack(outputs),
        jnp.stack(grad_inputs),
        gain_grad([(w_query, query), (w_key, key), (w_value, value)]),
        query * gain1 * scale,
        key * gain1 * scale,
        value * gain1 * scale,
        out * scale,
        gain_grad([(w_gate, gate), (w_up, up)]),
        gate * gain2 * scale,
        up * gain2 * scale,
        down * scale,
    )


def solution(mesh):
    row = P("shard", None)
    tokens = P(("rep", "shard"), None, None)
    return jax.shard_map(
        per_device,
        mesh=mesh,
        in_specs=(
            tokens, P(("rep", "shard"), None), P("shard"), row, row, row, row, P("shard"), row, row, row, tokens,
        ),
        out_specs=(tokens, tokens, P("shard"), row, row, row, row, P("shard"), row, row, row),
        check_vma=False,
    )
```
